256 devices in a mesh: elem: 64 (over y, z, core), dir: 4 (over x).
Axes of the slice: x: 4, y: 4, z: 8, core: 2. Of those that a mesh axis runs over, the one named last changes fastest.
Arguments:
- history: bfloat16 [8, 32, 24576], P(None, 'dir', 'elem'), may hold values from -6 to 6
- incident: bfloat16 [2, 32, 24576], P(None, 'dir', 'elem'), may hold values from -6 to 6
- ztiles: bfloat16 [192, 32, 128, 128], P('elem'), may hold values from -0.09375 to 0.09375
- zinv: bfloat16 [192, 128, 128], P('elem'), may hold values from -0.5 to 0.5
- columns: int32 [192, 32], P('elem'), may hold values from 0 to 191, as said below
- lags: int32 [192, 32], P('elem'), may hold values from 1 to 8
- counts: int32 [192], P('elem'), may hold values from 8 to 32
- basis: bfloat16 [24576, 256], P('elem'), may hold values from -0.109375 to 0.109375
Outputs:
- densities: bfloat16 [2, 32, 24576], P(None, 'dir', 'elem')
- far_field: float32 [2, 32, 256], P(None, 'dir', 'elem')
The draws below stay inside these ranges and needn't reach their ends.
Inputs may be any that keep to these rules, and one draw needn't show every extreme that they name: A block row's slots at or beyond counts are unused; a source block may repeat within a row. `columns`: all slots, used or not, of the block rows of one index of elem name blocks whose panels lie on any one index of elem at most 4 times, and exactly 4 times for some index.
All inputs are finite; a program needn't handle non-finite values.
Results may differ from the reference program's by a relative error of at most 0.005.
Values may be sent and summed in bfloat16 or wider, within the bound.
No kernel may reach another device: no remote copies, remote signals or barrier semaphores. Data moves between devices by JAX's collectives and lax.ppermute only.
A program may use at most 64 MiB of HBM per device.

```python
import jax
import jax.numpy as jnp

PAN_DEV = 384
BLK = 128
K_MAX = 32
L = 8
DIRS = 32
SH = 256
STEPS = 2
PANELS = 24576
NBLK = 192
CAP = 4


def draw_columns(key, part):
    rows_dev = PAN_DEV // BLK
    devices_elem = NBLK // rows_dev
    slots_dev = rows_dev * K_MAX

    def one_device(dev_key):
        key_slots = jax.random.fold_in(dev_key, 11)
        key_owner = jax.random.fold_in(dev_key, 12)
        key_local = jax.random.fold_in(dev_key, 13)
        slot_order = jax.random.permutation(key_slots, slots_dev)
        owner_order = jax.random.permutation(key_owner, devices_elem)
        owner = owner_order[slot_order // CAP]
        local = jax.random.randint(key_local, (slots_dev,), 0, rows_dev)
        return (owner * rows_dev + local).astype(jnp.int32)
    dev_keys = jax.vmap(lambda index: jax.random.fold_in(key, index))(jnp.arange(devices_elem))
    blocks = jax.vmap(one_device)(dev_keys)
    return blocks.reshape(NBLK, K_MAX).astype(jnp.int32)


def set_ends(array, own_key, smallest, largest):
    spot = [jax.random.randint(jax.random.fold_in(own_key, axis), (), 0, length) for axis, length in enumerate(array.shape)]
    longest = array.shape.index(max(array.shape))
    beside = spot[:longest] + [(spot[longest] + 1) % array.shape[longest]] + spot[longest + 1:]
    return array.at[tuple(spot)].set(smallest).at[tuple(beside)].set(largest)


def strengthened(values, key, source, target, shards_of, factor):
    def block_of(axis_at):
        return (jnp.arange(values.shape[axis_at]) // (values.shape[axis_at] // shards_of)).reshape((-1,) + (1,) * (values.ndim - 1 - axis_at))

    first = jax.random.permutation(key, shards_of)[block_of(target)]
    second = (block_of(target) + shards_of // 2) % shards_of
    return jnp.where((block_of(source) == first) | (block_of(source) == second), factor * values, values)


def block_levels(own_key, shape, pieces, smallest, largest):
    def one(dim, parts):
        heights = jax.random.uniform(jax.random.fold_in(jax.random.fold_in(own_key, 6), dim), (parts,), jnp.float32, smallest / len(pieces), largest / len(pieces))
        return jnp.repeat(jnp.exp(heights), shape[dim] // parts).reshape((-1,) + (1,) * (len(shape) - dim - 1))

    loudness = one(*pieces[0])
    for cut in pieces[1:]:
        loudness = loudness * one(*cut)
    return loudness


def bell_draw(stream_key, shape, spread, most, pieces=(), held_as=jnp.bfloat16):
    drawn = jax.random.normal(stream_key, shape, jnp.float32) * spread
    if len(pieces) > 0:
        drawn = block_levels(stream_key, shape, pieces, -0.22, 0.18) * drawn
    return jnp.clip(drawn, min=-most, max=most).astype(held_as)


def bell_draw_with(rng, extent, scale, most, split, heavy, kind=jnp.bfloat16):
    result = scale * jax.random.normal(rng, extent, jnp.float32)
    if split:
        result = result * block_levels(rng, extent, split, -0.22, 0.18)
    return jnp.clip(strengthened(result, jax.random.fold_in(rng, 3), *heavy), -most, most).astype(kind)


def setup_inputs(seed: int = 0) -> dict:
    key_of = jax.random.split(jax.random.key(seed), 9)
    return {
        "history": bell_draw(key_of[0], (L, DIRS, PANELS), 1.0, 6.0, ((1, 4), (2, 64))),
        "incident": bell_draw(key_of[1], (STEPS, DIRS, PANELS), 1.0, 6.0, ((1, 4), (2, 64))),
        "ztiles": bell_draw(key_of[2], (NBLK, K_MAX, BLK, BLK), (BLK * K_MAX) ** -0.5, 0.09375, ((0, 64),)),
        "zinv": bell_draw(key_of[3], (NBLK, BLK, BLK), BLK ** -0.5, 0.5, ((0, 64),)),
        "columns": draw_columns(jax.random.fold_in(key_of[8], 71), 0),
        "lags": set_ends(jax.random.randint(key_of[5], (NBLK, K_MAX), 1, L + 1), jax.random.fold_in(key_of[5], 1), 1, L).astype(jnp.int32),
        "counts": set_ends(jax.random.randint(key_of[6], (NBLK,), max(1, K_MAX // 4), K_MAX + 1), jax.random.fold_in(key_of[6], 1), max(1, K_MAX // 4), K_MAX).astype(jnp.int32),
        "basis": bell_draw_with(key_of[7], (PANELS, SH), PANELS ** -0.5, 0.109375, ((0, 64),), (0, 1, 64, 4.0)),
    }


def reference(history, incident, ztiles, zinv, columns, lags, counts, basis):
    window = history
    slot_index = jnp.arange(K_MAX, dtype=jnp.int32)
    active = slot_index[None, :] < counts[:, None]
    dens_list = []
    far_list = []
    for step_index in range(STEPS):
        grid = window.reshape(L, DIRS, NBLK, BLK)
        picked = grid[lags - 1, :, columns, :]
        picked = jnp.where(active[:, :, None, None], picked, jnp.zeros((), picked.dtype))
        history_sum = jnp.einsum('rkdj,rkji->dri', picked.astype(jnp.float32), ztiles.astype(jnp.float32))
        own = incident[step_index].astype(jnp.float32).reshape(DIRS, NBLK, BLK)
        source = (own - history_sum).astype(jnp.bfloat16)
        density = jnp.einsum('drj,rji->dri', source.astype(jnp.float32), zinv.astype(jnp.float32))
        density = density.reshape(DIRS, PANELS).astype(jnp.bfloat16)
        far_part = jnp.dot(density, basis, preferred_element_type=jnp.float32)
        dens_list.append(density)
        far_list.append(far_part)
        window = jnp.concatenate([density[None], window[:-1]], axis=0)
    return jnp.stack(dens_list), jnp.stack(far_list)
```

```python
import jax
import jax.numpy as jnp
from jax import lax
from jax.experimental import pallas as pl
from jax.experimental.pallas import tpu as pltpu
from jax.sharding import Mesh, PartitionSpec as P

STEPS = 2
Y, Z, C = 4, 8, 2
GROUPS = Y * C
E = ("y", "z", "c")
BLOCK_CAP = 4


def vmem():
    return pl.BlockSpec(memory_space=pltpu.VMEM)


def smem():
    return pl.BlockSpec(memory_space=pltpu.SMEM)


def spread(value, axis, length):
    whole = jnp.broadcast_to(value[None], (length, *value.shape))
    return lax.all_to_all(whole, axis, 0, 0, tiled=True)


def pick_kernel(asked, held, first, second):
    back = held.shape[0] // (Z * 8)

    @pl.loop(0, first.shape[0], step=16)
    def _(base):
        for k in range(16):
            spot = asked[base + k]
            first[base + k] = held[spot]
            second[base + k] = held[jnp.maximum(spot - back, 0)]


def pick(asked, held):
    out = jax.ShapeDtypeStruct((asked.shape[0], *held.shape[1:]), held.dtype)
    return pl.pallas_call(
        pick_kernel,
        out_shape=(out, out),
        in_specs=[smem(), vmem()],
        out_specs=(vmem(), vmem()),
        name="pick",
    )(asked, held)


def row_density(load, counts, ztiles, zinv, own, row):
    slots, tile = ztiles.shape[1], ztiles.shape[2]
    live = counts[row]
    parts = []
    for k in range(slots):
        tile_k = load(row * slots + k)
        parts.append(jnp.where(k < live, tile_k, jnp.zeros_like(tile_k)))
    picked = jnp.concatenate(parts, axis=1)
    flat = ztiles[row].reshape(slots * tile, tile)
    total = jnp.dot(picked, flat, preferred_element_type=jnp.float32)
    source = (own.astype(jnp.float32) - total).astype(jnp.bfloat16)
    density = jnp.dot(source, zinv[row], preferred_element_type=jnp.float32)
    return density.astype(jnp.bfloat16)


def first_kernel(spots, counts, held, ztiles, zinv, incident, out):
    tile = ztiles.shape[2]
    for row in range(ztiles.shape[0]):
        own = incident[0, :, row * tile : (row + 1) * tile]
        out[row] = row_density(lambda s: held[spots[s]], counts, ztiles, zinv, own, row)


def first_step(spots, counts, held, ztiles, zinv, incident):
    rows, tile, dirs = ztiles.shape[0], ztiles.shape[2], held.shape[1]
    return pl.pallas_call(
        first_kernel,
        out_shape=jax.ShapeDtypeStruct((rows, dirs, tile), jnp.bfloat16),
        in_specs=[smem(), smem(), vmem(), vmem(), vmem(), vmem()],
        out_specs=vmem(),
        name="first_step",
    )(spots, counts, held, ztiles, zinv, incident)


def second_kernel(spots, counts, before, old, here, there, ztiles, zinv, incident, basis, dens, far, pool, flipped, sems):
    rows, tile = ztiles.shape[0], ztiles.shape[2]
    near = here.shape[0]
    copies = [
        pltpu.make_async_copy(old, pool.at[pl.ds(0, old.shape[0])], sems.at[0]),
        pltpu.make_async_copy(here, pool.at[pl.ds(old.shape[0], near)], sems.at[1]),
        pltpu.make_async_copy(there, pool.at[pl.ds(old.shape[0] + near, near)], sems.at[2]),
    ]
    for copy in copies:
        copy.start()
    for copy in copies:
        copy.wait()
    earlier, later = [], []
    for row in range(rows):
        own = incident[1, :, row * tile : (row + 1) * tile]
        later.append(row_density(lambda s: pool[spots[s]], counts, ztiles, zinv, own, row))
        earlier.append(before[row])
    steps = [jnp.concatenate(earlier, axis=1), jnp.concatenate(later, axis=1)]
    sums = []
    for step, value in enumerate(steps):
        dens[step] = value
        sums.append(jnp.dot(value, basis[...], preferred_element_type=jnp.float32))
    total = jnp.concatenate(sums, axis=0)
    lanes = total.shape[0]
    flipped[:, :lanes] = total.T
    each = basis.shape[1] // far.shape[0]
    cols = [flipped[pl.ds(c, far.shape[0], stride=each), :] for c in range(each)]
    far[...] = jnp.concatenate(
        [c[:, :lanes] for c in cols] + [jnp.zeros((far.shape[0], 128 - each * lanes), jnp.float32)], axis=1
    )


def second_step(spots, counts, before, old, here, there, ztiles, zinv, incident, basis, owners):
    dirs = before.shape[1]
    panels, harmonics = basis.shape
    anywhere = pl.BlockSpec(memory_space=pl.ANY)
    return pl.pallas_call(
        second_kernel,
        out_shape=(
            jax.ShapeDtypeStruct((STEPS, dirs, panels), jnp.bfloat16),
            jax.ShapeDtypeStruct((owners, 128), jnp.float32),
        ),
        in_specs=[smem(), smem(), vmem(), anywhere, anywhere, anywhere, vmem(), vmem(), vmem(), vmem()],
        out_specs=(vmem(), vmem()),
        scratch_shapes=[
            pltpu.VMEM((old.shape[0] + 2 * here.shape[0], *old.shape[1:]), jnp.bfloat16),
            pltpu.VMEM((harmonics, 128), jnp.float32),
            pltpu.SemaphoreType.DMA((3,)),
        ],
        name="second_step",
    )(spots, counts, before, old, here, there, ztiles, zinv, incident, basis)


def sum_kernel(parts, out):
    total = jnp.sum(parts[...], axis=0, keepdims=True)
    steps, each, dirs = out.shape
    for step in range(steps):
        for c in range(each):
            at = (c * steps + step) * dirs
            out[step, c : c + 1, :] = total[:, at : at + dirs]


def sum_parts(parts, steps, each, dirs):
    return pl.pallas_call(
        sum_kernel,
        out_shape=jax.ShapeDtypeStruct((steps, each, dirs), jnp.float32),
        in_specs=[vmem()],
        out_specs=vmem(),
        name="sum_parts",
    )(parts)


def on_device(history, incident, ztiles, zinv, columns, lags, counts, basis):
    rows, slots, tile = ztiles.shape[0], ztiles.shape[1], ztiles.shape[2]
    levels, dirs, panels = history.shape
    slots_dev = rows * slots
    owners = Y * Z * C
    cap = BLOCK_CAP * Z
    mine = history.reshape(levels, dirs, rows, tile).transpose(0, 2, 1, 3)
    held = spread(mine.reshape(levels * rows, dirs, tile), "z", Z)
    held = held.reshape(Z * levels * rows, dirs, tile)
    flat_cols = columns.reshape(slots_dev)
    flat_lags = lags.reshape(slots_dev) - 1
    owner = flat_cols // rows
    local = flat_cols - owner * rows
    own_c = owner % C
    own_z = (owner // C) % Z
    own_y = owner // (C * Z)
    group = own_y * C + own_c
    spot = (own_z * levels + flat_lags) * rows + local
    ids = jnp.arange(slots_dev, dtype=jnp.int32)
    earlier = (group[:, None] == group[None, :]) & (ids[None, :] < ids[:, None])
    position = jnp.sum(earlier.astype(jnp.int32), axis=1)
    at = group * cap + position
    asks = jnp.arange(GROUPS * cap, dtype=jnp.int32)
    wanted = jnp.sum(jnp.where(at[None, :] == asks[:, None], spot[None, :], 0), axis=1)
    asked = lax.all_to_all(wanted.reshape(GROUPS, cap), ("y", "c"), 0, 0, tiled=True)
    first, second = pick(asked.reshape(GROUPS * cap), held)
    shape = (GROUPS, cap, dirs, tile)
    got = lax.all_to_all(first.reshape(shape), ("y", "c"), 0, 0, tiled=True)
    density = first_step(at, counts, got.reshape(GROUPS * cap, dirs, tile), ztiles, zinv, incident)
    old = lax.all_to_all(second.reshape(shape), ("y", "c"), 0, 0, tiled=True)
    here = spread(density, ("y", "z"), Y * Z).reshape(Y * Z * rows, dirs, tile)
    there = lax.ppermute(here, "c", [(0, 1), (1, 0)])
    far_side = (own_c != lax.axis_index("c")).astype(jnp.int32)
    fresh = GROUPS * cap + (far_side * (Y * Z) + own_y * Z + own_z) * rows + local
    spots = jnp.where(flat_lags == 0, fresh, at)
    dens, far = second_step(
        spots, counts, density, old.reshape(GROUPS * cap, dirs, tile), here, there, ztiles, zinv, incident, basis, owners
    )
    each = basis.shape[1] // owners
    parts = lax.all_to_all(far.reshape(owners, 1, 128), E, 0, 0, tiled=True).reshape(owners, 128)
    total = sum_parts(parts, STEPS, each, dirs)
    return dens, total.transpose(0, 2, 1)


def solution(mesh):
    fine = Mesh(mesh.devices.reshape(Y, Z, C, mesh.shape["dir"]), ("y", "z", "c", "dir"))
    in_specs = (
        P(None, "dir", E),
        P(None, "dir", E),
        P(E, None, None, None),
        P(E, None, None),
        P(E, None),
        P(E, None),
        P(E),
        P(E, None),
    )
    out_specs = (P(None, "dir", E), P(None, "dir", E))
    return jax.shard_map(on_device, mesh=fine, in_specs=in_specs, out_specs=out_specs, check_vma=False)
```

```python
import jax
import jax.numpy as jnp
from jax import lax
from jax.experimental import pallas as pl
from jax.experimental.pallas import tpu as pltpu
from jax.sharding import Mesh, PartitionSpec as P


STEPS = 2
Y, Z, C = 4, 8, 2
GROUPS = Y * C
E = ("y", "z", "c")
BLOCK_CAP = 4
LEVELS = 8


def grant(mib):
    return pltpu.CompilerParams(vmem_limit_bytes=mib << 20)


def vmem():
    return pl.BlockSpec(memory_space=pltpu.VMEM)


def smem():
    return pl.BlockSpec(memory_space=pltpu.SMEM)


def spread(value, axis, length):
    whole = jnp.broadcast_to(value[None], (length, *value.shape))
    return lax.all_to_all(whole, axis, 0, 0, tiled=True)


def pick_kernel(place, *refs):
    lists, held, first, later = refs[:Y], refs[Y], refs[Y + 1], refs[Y + 2 :]
    y, c = place[0], place[1]
    cap = first.shape[0] // GROUPS
    back = held.shape[0] // (Z * LEVELS)
    mine = (y * C + c) * cap
    for shift in range(Y):
        for other in range(C):
            whose = (lax.rem(y - shift + Y, Y) * C + (c if other == 0 else 1 - c)) * cap

            @pl.loop(0, cap, step=16)
            def _(base):
                for k in range(16):
                    spot = lists[shift][other * GROUPS * cap + mine + base + k]
                    first[whose + base + k] = held[spot]
                    later[shift][other * cap + base + k] = held[jnp.maximum(spot - back, 0)]


def pick(place, lists, held, cap):
    def out(entries):
        return jax.ShapeDtypeStruct((entries, *held.shape[1:]), held.dtype)

    return pl.pallas_call(
        pick_kernel,
        out_shape=(out(GROUPS * cap), *[out(C * cap)] * Y),
        in_specs=[smem()] * (1 + Y) + [vmem()],
        out_specs=[vmem()] * (1 + Y),
        compiler_params=grant(8),
        name="pick",
    )(place, *lists, held)


def row_density(load, counts, ztiles, zinv, own, row):
    slots, tile = ztiles.shape[1], ztiles.shape[2]
    live = counts[row]
    parts = []
    for k in range(slots):
        tile_k = load(row * slots + k)
        parts.append(jnp.where(k < live, tile_k, jnp.zeros_like(tile_k)))
    picked = jnp.concatenate(parts, axis=1)
    flat = ztiles[row].reshape(slots * tile, tile)
    total = jnp.dot(picked, flat, preferred_element_type=jnp.float32)
    source = (own.astype(jnp.float32) - total).astype(jnp.bfloat16)
    density = jnp.dot(source, zinv[row], preferred_element_type=jnp.float32)
    return density.astype(jnp.bfloat16)


def first_kernel(spots, counts, held, ztiles, zinv, incident, out):
    tile = ztiles.shape[2]
    for row in range(ztiles.shape[0]):
        own = incident[0, :, row * tile : (row + 1) * tile]
        out[row] = row_density(lambda s: held[spots[s]], counts, ztiles, zinv, own, row)


def first_step(spots, counts, held, ztiles, zinv, incident):
    rows, tile, dirs = ztiles.shape[0], ztiles.shape[2], held.shape[1]
    return pl.pallas_call(
        first_kernel,
        out_shape=jax.ShapeDtypeStruct((rows, dirs, tile), jnp.bfloat16),
        in_specs=[smem(), smem(), vmem(), vmem(), vmem(), vmem()],
        out_specs=vmem(),
        compiler_params=grant(16),
        name="first_step",
    )(spots, counts, held, ztiles, zinv, incident)


def second_kernel(spots, counts, before, *refs):
    near, cross = refs[:Y], refs[Y : 2 * Y]
    here, there, ztiles, zinv, incident, basis, dens, far, pool, flipped, sems = refs[2 * Y :]
    rows, tile = ztiles.shape[0], ztiles.shape[2]
    cap = near[0].shape[0] // C
    pieces = []
    for shift in range(Y):
        pieces += [near[shift].at[pl.ds(0, cap)], cross[shift].at[pl.ds(cap, cap)]]
    copies, start = [], 0
    for piece in (*pieces, here, there):
        length = piece.shape[0]
        copies.append(pltpu.make_async_copy(piece, pool.at[pl.ds(start, length)], sems.at[len(copies)]))
        start += length
    for copy in copies:
        copy.start()
    for copy in copies:
        copy.wait()
    earlier, later = [], []
    for row in range(rows):
        own = incident[1, :, row * tile : (row + 1) * tile]
        later.append(row_density(lambda s: pool[spots[s]], counts, ztiles, zinv, own, row))
        earlier.append(before[row])
    steps = [jnp.concatenate(earlier, axis=1), jnp.concatenate(later, axis=1)]
    sums = []
    for step, value in enumerate(steps):
        dens[step] = value
        sums.append(jnp.dot(value, basis[...], preferred_element_type=jnp.float32))
    total = jnp.concatenate(sums, axis=0)
    lanes = total.shape[0]
    flipped[:, :lanes] = total.T
    each = basis.shape[1] // far.shape[0]
    cols = [flipped[pl.ds(c, far.shape[0], stride=each), :] for c in range(each)]
    far[...] = jnp.concatenate(
        [c[:, :lanes] for c in cols] + [jnp.zeros((far.shape[0], 128 - each * lanes), jnp.float32)], axis=1
    )


def second_step(spots, counts, before, near, cross, here, there, ztiles, zinv, incident, basis, owners):
    dirs = before.shape[1]
    panels, harmonics = basis.shape
    anywhere = pl.BlockSpec(memory_space=pl.ANY)
    return pl.pallas_call(
        second_kernel,
        out_shape=(
            jax.ShapeDtypeStruct((STEPS, dirs, panels), jnp.bfloat16),
            jax.ShapeDtypeStruct((owners, 128), jnp.float32),
        ),
        in_specs=[smem(), smem(), vmem()] + [anywhere] * (2 * Y + 2) + [vmem()] * 4,
        out_specs=(vmem(), vmem()),
        scratch_shapes=[
            pltpu.VMEM((Y * near[0].shape[0] + 2 * here.shape[0], *here.shape[1:]), jnp.bfloat16),
            pltpu.VMEM((harmonics, 128), jnp.float32),
            pltpu.SemaphoreType.DMA((2 * Y + 2,)),
        ],
        compiler_params=grant(16),
        name="second_step",
    )(spots, counts, before, *near, *cross, here, there, ztiles, zinv, incident, basis)


def sum_kernel(parts, out):
    total = jnp.sum(parts[...], axis=0, keepdims=True)
    steps, each, dirs = out.shape
    for step in range(steps):
        for c in range(each):
            at = (c * steps + step) * dirs
            out[step, c : c + 1, :] = total[:, at : at + dirs]


def sum_parts(parts, steps, each, dirs):
    return pl.pallas_call(
        sum_kernel,
        out_shape=jax.ShapeDtypeStruct((steps, each, dirs), jnp.float32),
        in_specs=[vmem()],
        out_specs=vmem(),
        compiler_params=grant(4),
        name="sum_parts",
    )(parts)


def march(history, incident, ztiles, zinv, columns, lags, counts, basis):
    rows, slots, tile = ztiles.shape[0], ztiles.shape[1], ztiles.shape[2]
    levels, dirs, _ = history.shape
    slots_dev = rows * slots
    owners = Y * Z * C
    cap = BLOCK_CAP * Z
    mine = history.reshape(levels, dirs, rows, tile).transpose(0, 2, 1, 3)
    held = spread(mine.reshape(levels * rows, dirs, tile), "z", Z)
    held = held.reshape(Z * levels * rows, dirs, tile)
    flat_cols = columns.reshape(slots_dev)
    flat_lags = lags.reshape(slots_dev) - 1
    owner = flat_cols // rows
    local = flat_cols - owner * rows
    own_c = owner % C
    own_z = (owner // C) % Z
    own_y = owner // (C * Z)
    group = own_y * C + own_c
    spot = (own_z * levels + flat_lags) * rows + local
    ids = jnp.arange(slots_dev, dtype=jnp.int32)
    earlier = (group[:, None] == group[None, :]) & (ids[None, :] < ids[:, None])
    position = jnp.sum(earlier.astype(jnp.int32), axis=1)
    at = group * cap + position
    asks = jnp.arange(GROUPS * cap, dtype=jnp.int32)
    wanted = jnp.sum(jnp.where(at[None, :] == asks[:, None], spot[None, :], 0), axis=1)
    swap = [(0, 1), (1, 0)]
    both = jnp.concatenate([wanted, lax.ppermute(wanted, "c", swap)])
    lists = [both] + [lax.ppermute(both, "y", [(i, (i + s) % Y) for i in range(Y)]) for s in range(1, Y)]
    y, c = lax.axis_index("y"), lax.axis_index("c")
    first, *later = pick(jnp.stack([y, c]), lists, held, cap)
    got = lax.all_to_all(first.reshape(GROUPS, cap, dirs, tile), ("y", "c"), 0, 0, tiled=True)
    density = first_step(at, counts, got.reshape(GROUPS * cap, dirs, tile), ztiles, zinv, incident)
    here = spread(density, ("y", "z"), Y * Z).reshape(Y * Z * rows, dirs, tile)
    near = later[:1] + [
        lax.ppermute(later[s], "y", [(i, (i - s) % Y) for i in range(Y)]) for s in range(1, Y)
    ]
    cross = [lax.ppermute(piece, "c", swap) for piece in near]
    there = lax.ppermute(here, "c", swap)
    other = (own_c != c).astype(jnp.int32)
    aged = (((own_y - y) % Y) * C + other) * cap + position
    fresh = GROUPS * cap + (other * (Y * Z) + own_y * Z + own_z) * rows + local
    spots = jnp.where(flat_lags == 0, fresh, aged)
    dens, far = second_step(
        spots, counts, density, near, cross, here, there, ztiles, zinv, incident, basis, owners
    )
    each = basis.shape[1] // owners
    parts = lax.all_to_all(far.reshape(owners, 1, 128), E, 0, 0, tiled=True).reshape(owners, 128)
    total = sum_parts(parts, STEPS, each, dirs)
    return dens, total.transpose(0, 2, 1)


def solution(mesh):
    fine = Mesh(mesh.devices.reshape(Y, Z, C, mesh.shape["dir"]), ("y", "z", "c", "dir"))
    in_specs = (
        P(None, "dir", E),
        P(None, "dir", E),
        P(E, None, None, None),
        P(E, None, None),
        P(E, None),
        P(E, None),
        P(E),
        P(E, None),
    )
    out_specs = (P(None, "dir", E), P(None, "dir", E))
    return jax.shard_map(march, mesh=fine, in_specs=in_specs, out_specs=out_specs, check_vma=False)
```

```python
import jax
import jax.numpy as jnp
from jax import lax
from jax.experimental import pallas as pl
from jax.experimental.pallas import tpu as pltpu
from jax.sharding import Mesh, PartitionSpec as P


STEPS = 2
LEVELS = 8
Y, Z, C = 4, 8, 2
GROUPS = Y * C
E = ("y", "z", "c")
BLOCK_CAP = 4
CHUNK = 8
WHOLE = 65_000_000
SMALL = 8 << 20
SWAP = [(0, 1), (1, 0)]


def vmem():
    return pl.BlockSpec(memory_space=pltpu.VMEM)


def smem():
    return pl.BlockSpec(memory_space=pltpu.SMEM)


def hbm():
    return pl.BlockSpec(memory_space=pltpu.HBM)


def anywhere():
    return pl.BlockSpec(memory_space=pl.ANY)


def kernel_call(body, grant, **options):
    return pl.pallas_call(body, compiler_params=pltpu.CompilerParams(vmem_limit_bytes=grant), **options)


def fan_kernel(history, out):
    levels, _, panels = history.shape
    tile = out.shape[3]
    rows = panels // tile
    for level in range(levels):
        for row in range(rows):
            value = history[level, :, row * tile : (row + 1) * tile]
            for z in range(Z):
                out[z, level * rows + row] = value


def fan(history, tile):
    levels, dirs, panels = history.shape
    return kernel_call(
        fan_kernel,
        SMALL,
        out_shape=jax.ShapeDtypeStruct((Z, levels * panels // tile, dirs, tile), history.dtype),
        in_specs=[vmem()],
        out_specs=vmem(),
    )(history)


def whose(place, shift, other):
    y, c = place[0], place[1]
    return lax.rem(y - shift + Y, Y) * C + (c if other == 0 else 1 - c)


def pick_kernel(place, *refs):
    lists, held, first = refs[:Y], refs[Y], refs[Y + 1]
    cap = first.shape[0] // GROUPS
    mine = (place[0] * C + place[1]) * cap
    for shift in range(Y):
        for other in range(C):
            to = whose(place, shift, other) * cap

            @pl.loop(0, cap, step=16)
            def _(base):
                for k in range(16):
                    first[to + base + k] = held[lists[shift][other * GROUPS * cap + mine + base + k]]


def pick_later_kernel(place, *refs):
    lists, held, later = refs[:Y], refs[Y], refs[Y + 1 :]
    cap = later[0].shape[0] // C
    back = held.shape[0] // (Z * LEVELS)
    mine = (place[0] * C + place[1]) * cap
    for shift in range(Y):
        for other in range(C):

            @pl.loop(0, cap, step=16)
            def _(base):
                for k in range(16):
                    spot = lists[shift][other * GROUPS * cap + mine + base + k]
                    later[shift][other * cap + base + k] = held[jnp.maximum(spot - back, 0)]


def picks(place, lists, held, cap):
    def out(entries):
        return jax.ShapeDtypeStruct((entries, *held.shape[1:]), held.dtype)

    specs = [smem()] * (1 + Y) + [vmem()]
    first = kernel_call(
        pick_kernel, SMALL, out_shape=out(GROUPS * cap), in_specs=specs, out_specs=vmem()
    )(place, *lists, held)
    later = kernel_call(
        pick_later_kernel, SMALL, out_shape=[out(C * cap)] * Y, in_specs=specs, out_specs=[vmem()] * Y
    )(place, *lists, held)
    return first, later


def row_sum(spots, pool, ztiles, row):
    slots, tile = ztiles.shape[1], ztiles.shape[2]
    parts = []
    for k in range(slots):
        spot = spots[row * slots + k]
        value = pool[jnp.maximum(spot, 0)]
        parts.append(jnp.where(spot >= 0, value, jnp.zeros_like(value)))
    picked = jnp.concatenate(parts, axis=1)
    return jnp.dot(picked, ztiles[row].reshape(slots * tile, tile), preferred_element_type=jnp.float32)


def density_of(own, total, zinv):
    source = (own.astype(jnp.float32) - total).astype(jnp.bfloat16)
    return jnp.dot(source, zinv, preferred_element_type=jnp.float32).astype(jnp.bfloat16)


def start_all(pairs, sems, base=0):
    copies = [pltpu.make_async_copy(src, dst, sems.at[base + i]) for i, (src, dst) in enumerate(pairs)]
    for copy in copies:
        copy.start()
    return copies


def first_kernel(spots, got, ztiles_hbm, zinv_hbm, incident_hbm, out, spread_out, ztiles, zinv, incident, sems):
    rows, tile = ztiles.shape[0], ztiles.shape[2]
    tiles = start_all([(ztiles_hbm.at[r], ztiles.at[r]) for r in range(rows)], sems)
    rest = start_all([(zinv_hbm, zinv), (incident_hbm.at[0], incident)], sems, rows)
    for row in range(rows):
        tiles[row].wait()
        total = row_sum(spots, got, ztiles, row)
        if row == 0:
            for copy in rest:
                copy.wait()
        density = density_of(incident[:, row * tile : (row + 1) * tile], total, zinv[row])
        out[row] = density
        for to in range(spread_out.shape[0]):
            spread_out[to, row] = density


def first_step(spots, got, ztiles, zinv, incident):
    rows, tile, dirs = ztiles.shape[0], ztiles.shape[2], got.shape[1]
    return kernel_call(
        first_kernel,
        WHOLE,
        out_shape=(
            jax.ShapeDtypeStruct((rows, dirs, tile), jnp.bfloat16),
            jax.ShapeDtypeStruct((Y * Z, rows, dirs, tile), jnp.bfloat16),
        ),
        in_specs=[smem(), vmem(), hbm(), hbm(), hbm()],
        out_specs=(vmem(), vmem()),
        scratch_shapes=[
            pltpu.VMEM(ztiles.shape, ztiles.dtype),
            pltpu.VMEM(zinv.shape, zinv.dtype),
            pltpu.VMEM(incident.shape[1:], incident.dtype),
            pltpu.SemaphoreType.DMA((rows + 2,)),
        ],
    )(spots, got, ztiles, zinv, incident)


def aged_kernel(spots, before, *refs):
    near, cross = refs[:Y], refs[Y : 2 * Y]
    ztiles_hbm, basis_hbm, sums, far, pool, ztiles, basis, sems = refs[2 * Y :]
    rows = ztiles.shape[0]
    cap = near[0].shape[0] // C
    pairs = []
    for shift in range(Y):
        for source, at in ((near[shift], 0), (cross[shift], cap)):
            pairs.append((source.at[pl.ds(at, cap)], pool.at[pl.ds(len(pairs) * cap, cap)]))
    pieces = start_all(pairs, sems)
    tiles = start_all([(ztiles_hbm.at[r], ztiles.at[r]) for r in range(rows)], sems, len(pairs))
    weights = start_all([(basis_hbm, basis)], sems, len(pairs) + rows)
    for copy in pieces:
        copy.wait()
    for row in range(rows):
        tiles[row].wait()
        sums[row] = row_sum(spots, pool, ztiles, row)
    weights[0].wait()
    value = jnp.concatenate([before[row] for row in range(rows)], axis=1)
    far[...] = jnp.dot(value, basis[...], preferred_element_type=jnp.float32)


def aged_step(spots, before, near, cross, ztiles, basis):
    rows, dirs, tile = before.shape
    cap = near[0].shape[0] // C
    return kernel_call(
        aged_kernel,
        WHOLE,
        out_shape=(
            jax.ShapeDtypeStruct((rows, dirs, tile), jnp.float32),
            jax.ShapeDtypeStruct((dirs, basis.shape[1]), jnp.float32),
        ),
        in_specs=[smem(), vmem()] + [anywhere()] * (2 * Y) + [hbm(), hbm()],
        out_specs=(vmem(), vmem()),
        scratch_shapes=[
            pltpu.VMEM((2 * Y * cap, dirs, tile), jnp.bfloat16),
            pltpu.VMEM(ztiles.shape, ztiles.dtype),
            pltpu.VMEM(basis.shape, basis.dtype),
            pltpu.SemaphoreType.DMA((2 * Y + rows + 1,)),
        ],
    )(spots, before, *near, *cross, ztiles, basis)


def second_kernel(table, before, sums, far_first, here, there, ztiles_hbm, zinv_hbm, incident_hbm, basis_hbm, *refs):
    dens, far, pool, ztiles, zinv, incident, basis, flipped, sems, tile_sems = refs
    rows, slots, tile = ztiles.shape[0], ztiles.shape[1], ztiles.shape[2]
    near = here.shape[0]
    chunks = [lax.div(table[2 * rows * slots + row] + (CHUNK - 1), CHUNK) for row in range(rows)]

    def fetch(row, i):
        slot = table[row * slots + i]
        return pltpu.make_async_copy(ztiles_hbm.at[row, slot], ztiles.at[row, i], tile_sems.at[row, i])

    for row in range(rows):

        @pl.loop(0, chunks[row] * CHUNK)
        def _(i):
            fetch(row, i).start()

    blocks = start_all([(here, pool.at[pl.ds(0, near)]), (there, pool.at[pl.ds(near, near)])], sems)
    rest = start_all([(zinv_hbm, zinv), (incident_hbm.at[1], incident), (basis_hbm, basis)], sems, 2)
    for copy in blocks:
        copy.wait()
    for row in range(rows):

        @pl.loop(0, chunks[row] * CHUNK)
        def _(i):
            fetch(row, i).wait()

    for copy in rest:
        copy.wait()
    later = []
    for row in range(rows):

        def add(chunk, total):
            parts = []
            for k in range(CHUNK):
                spot = table[rows * slots + row * slots + chunk * CHUNK + k]
                value = pool[jnp.maximum(spot, 0)]
                parts.append(jnp.where(spot >= 0, value, jnp.zeros_like(value)))
            weights = ztiles[row, pl.ds(chunk * CHUNK, CHUNK)].reshape(CHUNK * tile, tile)
            return total + jnp.dot(jnp.concatenate(parts, axis=1), weights, preferred_element_type=jnp.float32)

        total = lax.fori_loop(0, chunks[row], add, sums[row])
        later.append(density_of(incident[:, row * tile : (row + 1) * tile], total, zinv[row]))
    value = jnp.concatenate(later, axis=1)
    dens[0] = jnp.concatenate([before[row] for row in range(rows)], axis=1)
    dens[1] = value
    far_second = jnp.dot(value, basis[...], preferred_element_type=jnp.float32)
    both = jnp.concatenate([far_first[...], far_second], axis=0)
    lanes = both.shape[0]
    flipped[:, :lanes] = both.T
    owners = far.shape[0]
    each = basis.shape[1] // owners
    cols = [flipped[pl.ds(c, owners, stride=each), :][:, :lanes] for c in range(each)]
    far[...] = jnp.concatenate([*cols, jnp.zeros((owners, far.shape[1] - each * lanes), jnp.float32)], axis=1)


def second_step(table, before, sums, far_first, here, there, ztiles, zinv, incident, basis, owners):
    _, dirs, tile = before.shape
    panels, harmonics = basis.shape
    return kernel_call(
        second_kernel,
        WHOLE,
        out_shape=(
            jax.ShapeDtypeStruct((STEPS, dirs, panels), jnp.bfloat16),
            jax.ShapeDtypeStruct((owners, 128), jnp.float32),
        ),
        in_specs=[smem(), vmem(), vmem(), vmem(), anywhere(), anywhere(), hbm(), hbm(), hbm(), hbm()],
        out_specs=(vmem(), vmem()),
        scratch_shapes=[
            pltpu.VMEM((2 * here.shape[0], dirs, tile), jnp.bfloat16),
            pltpu.VMEM(ztiles.shape, ztiles.dtype),
            pltpu.VMEM(zinv.shape, zinv.dtype),
            pltpu.VMEM(incident.shape[1:], incident.dtype),
            pltpu.VMEM(basis.shape, basis.dtype),
            pltpu.VMEM((harmonics, 128), jnp.float32),
            pltpu.SemaphoreType.DMA((5,)),
            pltpu.SemaphoreType.DMA(ztiles.shape[:2]),
        ],
    )(table, before, sums, far_first, here, there, ztiles, zinv, incident, basis)


def sum_kernel(parts, out):
    total = jnp.sum(parts[...], axis=0, keepdims=True)
    steps, each, dirs = out.shape
    for step in range(steps):
        for c in range(each):
            at = (c * steps + step) * dirs
            out[step, c : c + 1, :] = total[:, at : at + dirs]


def sum_parts(parts, steps, each, dirs):
    return kernel_call(
        sum_kernel,
        SMALL,
        out_shape=jax.ShapeDtypeStruct((steps, each, dirs), jnp.float32),
        in_specs=[vmem()],
        out_specs=vmem(),
    )(parts)


def shifted(value, axis, length, shift):
    return lax.ppermute(value, axis, [(i, (i + shift) % length) for i in range(length)])


def march(history, incident, ztiles, zinv, columns, lags, counts, basis):
    rows, slots, tile = ztiles.shape[0], ztiles.shape[1], ztiles.shape[2]
    levels, dirs, _ = history.shape
    slots_dev = rows * slots
    owners = Y * Z * C
    cap = BLOCK_CAP * Z
    held = lax.all_to_all(fan(history, tile), "z", 0, 0, tiled=True)
    held = held.reshape(Z * levels * rows, dirs, tile)
    flat_cols = columns.reshape(slots_dev)
    flat_lags = lags.reshape(slots_dev) - 1
    owner = flat_cols // rows
    local = flat_cols - owner * rows
    own_c = owner % C
    own_z = (owner // C) % Z
    own_y = owner // (C * Z)
    group = own_y * C + own_c
    spot = (own_z * levels + flat_lags) * rows + local
    ids = jnp.arange(slots_dev, dtype=jnp.int32)
    ahead = (group[:, None] == group[None, :]) & (ids[None, :] < ids[:, None])
    position = jnp.sum(ahead.astype(jnp.int32), axis=1)
    at = group * cap + position
    asks = jnp.arange(GROUPS * cap, dtype=jnp.int32)
    wanted = jnp.sum(jnp.where(at[None, :] == asks[:, None], spot[None, :], 0), axis=1)
    both = jnp.concatenate([wanted, lax.ppermute(wanted, "c", SWAP)])
    lists = [both] + [shifted(both, "y", Y, s) for s in range(1, Y)]
    y, c = lax.axis_index("y"), lax.axis_index("c")
    other = (own_c != c).astype(jnp.int32)
    live = (jnp.arange(slots, dtype=jnp.int32)[None, :] < counts[:, None]).reshape(slots_dev)
    new = live & (flat_lags == 0)
    spots = jnp.where(live, at, -1)
    aged = jnp.where(live & ~new, (((own_y - y) % Y) * C + other) * cap + position, -1)
    fresh = (other * (Y * Z) + own_y * Z + own_z) * rows + local
    new_rows = new.reshape(rows, slots)
    slot_ids = jnp.arange(slots, dtype=jnp.int32)
    rank = jnp.sum((new_rows[:, None, :] & (slot_ids[None, None, :] < slot_ids[None, :, None])).astype(jnp.int32), axis=2)
    put = new_rows[:, None, :] & (rank[:, None, :] == slot_ids[None, :, None])
    order = jnp.sum(jnp.where(put, slot_ids[None, None, :], 0), axis=2)
    where = jnp.sum(jnp.where(put, fresh.reshape(rows, 1, slots) + 1, 0), axis=2) - 1
    table = jnp.concatenate(
        [order.reshape(slots_dev), where.reshape(slots_dev), jnp.sum(new_rows.astype(jnp.int32), axis=1)]
    )
    first, later = picks(jnp.stack([y, c]), lists, held, cap)
    got = lax.all_to_all(first.reshape(GROUPS, cap, dirs, tile), ("y", "c"), 0, 0, tiled=True)
    near = [later[0]] + [shifted(later[s], "y", Y, -s) for s in range(1, Y)]
    cross = [lax.ppermute(piece, "c", SWAP) for piece in near]
    density, fanned = first_step(spots, got.reshape(GROUPS * cap, dirs, tile), ztiles, zinv, incident)
    here = lax.all_to_all(fanned, ("y", "z"), 0, 0, tiled=True).reshape(Y * Z * rows, dirs, tile)
    sums, far_first = aged_step(aged, density, near, cross, ztiles, basis)
    there = lax.ppermute(here, "c", SWAP)
    dens, far = second_step(
        table, density, sums, far_first, here, there, ztiles, zinv, incident, basis, owners
    )
    each = basis.shape[1] // owners
    parts = lax.all_to_all(far.reshape(owners, 1, 128), E, 0, 0, tiled=True).reshape(owners, 128)
    total = sum_parts(parts, STEPS, each, dirs)
    return dens, total.transpose(0, 2, 1)


def solution(mesh):
    fine = Mesh(mesh.devices.reshape(Y, Z, C, mesh.shape["dir"]), ("y", "z", "c", "dir"))
    in_specs = (
        P(None, "dir", E),
        P(None, "dir", E),
        P(E, None, None, None),
        P(E, None, None),
        P(E, None),
        P(E, None),
        P(E),
        P(E, None),
    )
    out_specs = (P(None, "dir", E), P(None, "dir", E))
    return jax.shard_map(march, mesh=fine, in_specs=in_specs, out_specs=out_specs, check_vma=False)
```

```python
import jax
import jax.numpy as jnp
from jax import lax
from jax.experimental import pallas as pl
from jax.experimental.pallas import tpu as pltpu
from jax.sharding import Mesh, PartitionSpec as P


STEPS = 2
LEVELS = 8
Y, Z, C = 4, 8, 2
GROUPS = Y * C
E = ("y", "z", "c")
BLOCK_CAP = 4
CHUNK = 8
SMALL = 8 << 20
LARGE = 12 << 20
SWAP = [(0, 1), (1, 0)]


def vmem():
    return pl.BlockSpec(memory_space=pltpu.VMEM)


def smem():
    return pl.BlockSpec(memory_space=pltpu.SMEM)


def hbm():
    return pl.BlockSpec(memory_space=pltpu.HBM)


def anywhere():
    return pl.BlockSpec(memory_space=pl.ANY)


def kernel_call(body, grant, **options):
    return pl.pallas_call(body, compiler_params=pltpu.CompilerParams(vmem_limit_bytes=grant), **options)


def near_core(value):
    return pltpu.with_memory_space_constraint(value, pltpu.VMEM)


def off_core(value):
    return pltpu.with_memory_space_constraint(value, pltpu.HBM)


def fan_kernel(history, out):
    levels, _, panels = history.shape
    tile = out.shape[3]
    rows = panels // tile
    for level in range(levels):
        for row in range(rows):
            value = history[level, :, row * tile : (row + 1) * tile]
            for z in range(Z):
                out[z, level * rows + row] = value


def fan(history, tile):
    levels, dirs, panels = history.shape
    return kernel_call(
        fan_kernel,
        SMALL,
        out_shape=pltpu.VMEM((Z, levels * panels // tile, dirs, tile), history.dtype),
        in_specs=[vmem()],
        out_specs=vmem(),
    )(off_core(history))


def whose(place, shift, other):
    y, c = place[0], place[1]
    return lax.rem(y - shift + Y, Y) * C + (c if other == 0 else 1 - c)


def pick_kernel(place, *refs):
    lists, held, first = refs[:Y], refs[Y], refs[Y + 1]
    cap = first.shape[0] // GROUPS
    mine = (place[0] * C + place[1]) * cap
    for shift in range(Y):
        for other in range(C):
            to = whose(place, shift, other) * cap

            @pl.loop(0, cap, step=16)
            def _(base):
                for k in range(16):
                    first[to + base + k] = held[lists[shift][other * GROUPS * cap + mine + base + k]]


def pick_later_kernel(place, *refs):
    lists, held, later = refs[:Y], refs[Y], refs[Y + 1 :]
    cap = later[0].shape[0] // C
    back = held.shape[0] // (Z * LEVELS)
    mine = (place[0] * C + place[1]) * cap
    for shift in range(Y):
        for other in range(C):

            @pl.loop(0, cap, step=16)
            def _(base):
                for k in range(16):
                    spot = lists[shift][other * GROUPS * cap + mine + base + k]
                    later[shift][other * cap + base + k] = held[jnp.maximum(spot - back, 0)]


def picks(place, lists, held, cap):
    def out(entries):
        return pltpu.VMEM((entries, *held.shape[1:]), held.dtype)

    held = near_core(held)
    specs = [smem()] * (1 + Y) + [vmem()]
    first = kernel_call(
        pick_kernel, SMALL, out_shape=out(GROUPS * cap), in_specs=specs, out_specs=vmem()
    )(place, *lists, held)
    later = kernel_call(
        pick_later_kernel, SMALL, out_shape=[out(C * cap)] * Y, in_specs=specs, out_specs=[vmem()] * Y
    )(place, *lists, held)
    return first, later


def pieces_of(spots, base, load):
    parts = []
    for k in range(CHUNK):
        spot = spots[base + k]
        value = load(jnp.maximum(spot, 0))
        parts.append(jnp.where(spot >= 0, value, jnp.zeros_like(value)))
    return jnp.concatenate(parts, axis=1)


def row_sum(spots, base, load, ztiles, row, chunks, total):
    tile = ztiles.shape[-1]

    def add(chunk, total):
        weights = ztiles[row, pl.ds(chunk * CHUNK, CHUNK)].reshape(CHUNK * tile, tile)
        picked = pieces_of(spots, base + row * ztiles.shape[1] + chunk * CHUNK, load)
        return total + jnp.dot(picked, weights, preferred_element_type=jnp.float32)

    return lax.fori_loop(0, chunks, add, total)


def chunks_of(count):
    return lax.div(count + (CHUNK - 1), CHUNK)


def density_of(own, total, zinv):
    source = (own.astype(jnp.float32) - total).astype(jnp.bfloat16)
    return jnp.dot(source, zinv, preferred_element_type=jnp.float32).astype(jnp.bfloat16)


def start_all(pairs, sems, base=0):
    copies = [pltpu.make_async_copy(src, dst, sems.at[base + i]) for i, (src, dst) in enumerate(pairs)]
    for copy in copies:
        copy.start()
    return copies


def chunk_copy(ztiles_hbm, ztiles, sems, row, chunk):
    part = pl.ds(chunk * CHUNK, CHUNK)
    return pltpu.make_async_copy(ztiles_hbm.at[row, part], ztiles.at[row, part], sems.at[row, chunk])


def start_rows(ztiles_hbm, ztiles, sems, chunks):
    for row in range(ztiles.shape[0]):
        for chunk in range(ztiles.shape[1] // CHUNK):

            @pl.when(chunk < chunks[row])
            def _():
                chunk_copy(ztiles_hbm, ztiles, sems, row, chunk).start()


def wait_row(ztiles_hbm, ztiles, sems, chunks, row):
    for chunk in range(ztiles.shape[1] // CHUNK):

        @pl.when(chunk < chunks[row])
        def _():
            chunk_copy(ztiles_hbm, ztiles, sems, row, chunk).wait()


def first_kernel(spots, got, ztiles_hbm, zinv_hbm, incident_hbm, out, spread_out, ztiles, zinv, incident, sems, tile_sems):
    rows, slots, tile = ztiles.shape[0], ztiles.shape[1], ztiles.shape[2]
    chunks = [chunks_of(spots[rows * slots + row]) for row in range(rows)]
    start_rows(ztiles_hbm, ztiles, tile_sems, chunks)
    rest = start_all([(zinv_hbm, zinv), (incident_hbm.at[0], incident)], sems)
    for row in range(rows):
        wait_row(ztiles_hbm, ztiles, tile_sems, chunks, row)
        total = jnp.zeros(incident.shape[:1] + (tile,), jnp.float32)
        total = row_sum(spots, 0, lambda spot: got[spot], ztiles, row, chunks[row], total)
        if row == 0:
            for copy in rest:
                copy.wait()
        density = density_of(incident[:, row * tile : (row + 1) * tile], total, zinv[row])
        out[row] = density
        for to in range(spread_out.shape[0]):
            spread_out[to, row] = density


def first_step(spots, got, ztiles, zinv, incident):
    rows, slots, tile, dirs = ztiles.shape[0], ztiles.shape[1], ztiles.shape[2], got.shape[1]
    return kernel_call(
        first_kernel,
        LARGE,
        out_shape=(
            pltpu.VMEM((rows, dirs, tile), jnp.bfloat16),
            pltpu.VMEM((Y * Z, rows, dirs, tile), jnp.bfloat16),
        ),
        in_specs=[smem(), vmem(), hbm(), hbm(), hbm()],
        out_specs=(vmem(), vmem()),
        scratch_shapes=[
            pltpu.VMEM(ztiles.shape, ztiles.dtype),
            pltpu.VMEM(zinv.shape, zinv.dtype),
            pltpu.VMEM(incident.shape[1:], incident.dtype),
            pltpu.SemaphoreType.DMA((2,)),
            pltpu.SemaphoreType.DMA((rows, slots // CHUNK)),
        ],
    )(spots, near_core(got), off_core(ztiles), off_core(zinv), off_core(incident))


def aged_kernel(spots, table, before, *refs):
    near, cross = refs[:Y], refs[Y : 2 * Y]
    ztiles_hbm, zinv_hbm, incident_hbm, basis_hbm, packed, fresh, zinv, basis, pool, ztiles, incident, sems, tile_sems, fresh_sems = refs[2 * Y :]
    rows, slots, tile = ztiles.shape[0], ztiles.shape[1], ztiles.shape[2]
    cap = near[0].shape[0] // C
    panels = rows * tile
    pairs = []
    for shift in range(Y):
        for source, at in ((near[shift], 0), (cross[shift], cap)):
            pairs.append((source.at[pl.ds(at, cap)], pool.at[pl.ds(len(pairs) * cap, cap)]))
    pieces = start_all(pairs, sems)
    rest = start_all([(basis_hbm, basis), (incident_hbm.at[1], incident), (zinv_hbm, zinv)], sems, len(pairs))
    chunks = [chunks_of(spots[rows * slots + row]) for row in range(rows)]
    start_rows(ztiles_hbm, ztiles, tile_sems, chunks)
    lag_one = []
    for row in range(rows):
        for k in range(CHUNK):
            source = ztiles_hbm.at[row, table[row * slots + k]]
            lag_one.append(pltpu.make_async_copy(source, fresh.at[row, k], fresh_sems.at[row, k]))
    for copy in lag_one:
        copy.start()
    for copy in pieces:
        copy.wait()
    for copy in rest:
        copy.wait()
    for row in range(rows):
        wait_row(ztiles_hbm, ztiles, tile_sems, chunks, row)
        own = incident[:, row * tile : (row + 1) * tile].astype(jnp.float32)
        total = jnp.zeros(own.shape, jnp.float32)
        total = row_sum(spots, 0, lambda spot: pool[spot], ztiles, row, chunks[row], total)
        packed[0, :, row * tile : (row + 1) * tile] = own
        packed[1, :, row * tile : (row + 1) * tile] = total
    value = jnp.concatenate([before[row] for row in range(rows)], axis=1)
    packed[2, :, :] = value.astype(jnp.float32)
    packed[3, :, : basis.shape[1]] = jnp.dot(value, basis[...], preferred_element_type=jnp.float32)
    packed[3, :, basis.shape[1] :] = jnp.zeros((value.shape[0], panels - basis.shape[1]), jnp.float32)
    for copy in lag_one:
        copy.wait()


def aged_step(spots, table, before, near, cross, ztiles, zinv, incident, basis):
    rows, dirs, tile = before.shape
    slots = ztiles.shape[1]
    cap = near[0].shape[0] // C
    return kernel_call(
        aged_kernel,
        LARGE,
        out_shape=(
            pltpu.VMEM((4, dirs, rows * tile), jnp.float32),
            pltpu.VMEM((rows, CHUNK, tile, tile), ztiles.dtype),
            pltpu.VMEM(zinv.shape, zinv.dtype),
            pltpu.VMEM(basis.shape, basis.dtype),
        ),
        in_specs=[smem(), smem(), vmem()] + [anywhere()] * (2 * Y) + [hbm()] * 4,
        out_specs=[vmem()] * 4,
        scratch_shapes=[
            pltpu.VMEM((2 * Y * cap, dirs, tile), jnp.bfloat16),
            pltpu.VMEM(ztiles.shape, ztiles.dtype),
            pltpu.VMEM(incident.shape[1:], incident.dtype),
            pltpu.SemaphoreType.DMA((2 * Y + 3,)),
            pltpu.SemaphoreType.DMA((rows, slots // CHUNK)),
            pltpu.SemaphoreType.DMA((rows, CHUNK)),
        ],
    )(
        spots,
        table,
        near_core(before),
        *near,
        *cross,
        off_core(ztiles),
        off_core(zinv),
        off_core(incident),
        off_core(basis),
    )


def second_kernel(table, packed, fresh, zinv, basis, here, there, ztiles_hbm, dens, far, ztiles, flipped, tile_sems):
    rows, slots, tile = ztiles_hbm.shape[0], ztiles_hbm.shape[1], ztiles_hbm.shape[2]
    near = here.shape[0]

    def load(spot):
        ours = here[jnp.minimum(spot, near - 1)]
        theirs = there[jnp.maximum(spot - near, 0)]
        return jnp.where(spot < near, ours, theirs)

    later = []
    for row in range(rows):
        chunks = chunks_of(table[2 * rows * slots + row])
        at = pl.ds(row * tile, tile)
        first = pieces_of(table, rows * slots + row * slots, load)
        total = packed[1, :, at] + jnp.dot(
            first, fresh[row].reshape(CHUNK * tile, tile), preferred_element_type=jnp.float32
        )

        def more(chunk, total):
            copies = []
            for k in range(CHUNK):
                source = ztiles_hbm.at[row, table[row * slots + chunk * CHUNK + k]]
                copies.append(pltpu.make_async_copy(source, ztiles.at[k], tile_sems.at[k]))
            for copy in copies:
                copy.start()
            for copy in copies:
                copy.wait()
            picked = pieces_of(table, rows * slots + row * slots + chunk * CHUNK, load)
            return total + jnp.dot(
                picked, ztiles[...].reshape(CHUNK * tile, tile), preferred_element_type=jnp.float32
            )

        total = lax.fori_loop(1, chunks, more, total)
        later.append(density_of(packed[0, :, at], total, zinv[row]))
    value = jnp.concatenate(later, axis=1)
    dens[0] = packed[2].astype(dens.dtype)
    dens[1] = value
    far_second = jnp.dot(value, basis[...], preferred_element_type=jnp.float32)
    both = jnp.concatenate([packed[3, :, : basis.shape[1]], far_second], axis=0)
    lanes = both.shape[0]
    flipped[:, :lanes] = both.T
    owners = far.shape[0]
    each = basis.shape[1] // owners
    cols = [flipped[pl.ds(c, owners, stride=each), :][:, :lanes] for c in range(each)]
    far[...] = jnp.concatenate([*cols, jnp.zeros((owners, far.shape[1] - each * lanes), jnp.float32)], axis=1)


def second_step(table, packed, fresh, zinv, basis, here, there, ztiles, owners):
    tile, dirs = here.shape[2], here.shape[1]
    panels, harmonics = basis.shape
    return kernel_call(
        second_kernel,
        LARGE,
        out_shape=(
            jax.ShapeDtypeStruct((STEPS, dirs, panels), jnp.bfloat16),
            pltpu.VMEM((owners, 128), jnp.float32),
        ),
        in_specs=[smem()] + [vmem()] * 6 + [hbm()],
        out_specs=(vmem(), vmem()),
        scratch_shapes=[
            pltpu.VMEM((CHUNK, tile, tile), ztiles.dtype),
            pltpu.VMEM((harmonics, 128), jnp.float32),
            pltpu.SemaphoreType.DMA((CHUNK,)),
        ],
    )(
        table,
        near_core(packed),
        near_core(fresh),
        near_core(zinv),
        near_core(basis),
        near_core(here),
        near_core(there),
        off_core(ztiles),
    )


def sum_kernel(parts, out):
    total = jnp.sum(parts[...], axis=0, keepdims=True)
    steps, each, dirs = out.shape
    for step in range(steps):
        for c in range(each):
            at = (c * steps + step) * dirs
            out[step, c : c + 1, :] = total[:, at : at + dirs]


def sum_parts(parts, steps, each, dirs):
    return kernel_call(
        sum_kernel,
        SMALL,
        out_shape=jax.ShapeDtypeStruct((steps, each, dirs), jnp.float32),
        in_specs=[vmem()],
        out_specs=vmem(),
    )(near_core(parts))


def shifted(value, axis, length, shift):
    return lax.ppermute(value, axis, [(i, (i + shift) % length) for i in range(length)])


def march(history, incident, ztiles, zinv, columns, lags, counts, basis):
    rows, slots, tile = ztiles.shape[0], ztiles.shape[1], ztiles.shape[2]
    levels, dirs, _ = history.shape
    slots_dev = rows * slots
    owners = Y * Z * C
    cap = BLOCK_CAP * Z
    held = lax.all_to_all(fan(history, tile), "z", 0, 0, tiled=True)
    held = held.reshape(Z * levels * rows, dirs, tile)
    flat_cols = columns.reshape(slots_dev)
    flat_lags = lags.reshape(slots_dev) - 1
    owner = flat_cols // rows
    local = flat_cols - owner * rows
    own_c = owner % C
    own_z = (owner // C) % Z
    own_y = owner // (C * Z)
    group = own_y * C + own_c
    spot = (own_z * levels + flat_lags) * rows + local
    ids = jnp.arange(slots_dev, dtype=jnp.int32)
    ahead = (group[:, None] == group[None, :]) & (ids[None, :] < ids[:, None])
    position = jnp.sum(ahead.astype(jnp.int32), axis=1)
    at = group * cap + position
    asks = jnp.arange(GROUPS * cap, dtype=jnp.int32)
    wanted = jnp.sum(jnp.where(at[None, :] == asks[:, None], spot[None, :], 0), axis=1)
    both = jnp.concatenate([wanted, lax.ppermute(wanted, "c", SWAP)])
    lists = [both] + [shifted(both, "y", Y, s) for s in range(1, Y)]
    y, c = lax.axis_index("y"), lax.axis_index("c")
    other = (own_c != c).astype(jnp.int32)
    live = (jnp.arange(slots, dtype=jnp.int32)[None, :] < counts[:, None]).reshape(slots_dev)
    new = live & (flat_lags == 0)
    spots = jnp.concatenate([jnp.where(live, at, -1), counts])
    old = jnp.where(live & ~new, (((own_y - y) % Y) * C + other) * cap + position, -1)
    aged = jnp.concatenate([old, counts])
    fresh = (other * (Y * Z) + own_y * Z + own_z) * rows + local
    new_rows = new.reshape(rows, slots)
    slot_ids = jnp.arange(slots, dtype=jnp.int32)
    rank = jnp.sum((new_rows[:, None, :] & (slot_ids[None, None, :] < slot_ids[None, :, None])).astype(jnp.int32), axis=2)
    put = new_rows[:, None, :] & (rank[:, None, :] == slot_ids[None, :, None])
    order = jnp.sum(jnp.where(put, slot_ids[None, None, :], 0), axis=2)
    where = jnp.sum(jnp.where(put, fresh.reshape(rows, 1, slots) + 1, 0), axis=2) - 1
    table = jnp.concatenate(
        [order.reshape(slots_dev), where.reshape(slots_dev), jnp.sum(new_rows.astype(jnp.int32), axis=1)]
    )
    first, later = picks(jnp.stack([y, c]), lists, held, cap)
    got = lax.all_to_all(first.reshape(GROUPS, cap, dirs, tile), ("y", "c"), 0, 0, tiled=True)
    near = [later[0]] + [shifted(later[s], "y", Y, -s) for s in range(1, Y)]
    cross = [lax.ppermute(piece, "c", SWAP) for piece in near]
    density, fanned = first_step(spots, got.reshape(GROUPS * cap, dirs, tile), ztiles, zinv, incident)
    here = lax.all_to_all(fanned, ("y", "z"), 0, 0, tiled=True).reshape(Y * Z * rows, dirs, tile)
    packed, lag_one, inverse, weights = aged_step(aged, table, density, near, cross, ztiles, zinv, incident, basis)
    there = lax.ppermute(here, "c", SWAP)
    dens, far = second_step(table, packed, lag_one, inverse, weights, here, there, ztiles, owners)
    each = basis.shape[1] // owners
    parts = lax.all_to_all(far.reshape(owners, 1, 128), E, 0, 0, tiled=True).reshape(owners, 128)
    total = sum_parts(parts, STEPS, each, dirs)
    return dens, total.transpose(0, 2, 1)


def solution(mesh):
    fine = Mesh(mesh.devices.reshape(Y, Z, C, mesh.shape["dir"]), ("y", "z", "c", "dir"))
    in_specs = (
        P(None, "dir", E),
        P(None, "dir", E),
        P(E, None, None, None),
        P(E, None, None),
        P(E, None),
        P(E, None),
        P(E),
        P(E, None),
    )
    out_specs = (P(None, "dir", E), P(None, "dir", E))
    return jax.shard_map(march, mesh=fine, in_specs=in_specs, out_specs=out_specs, check_vma=False)
```

```python
import jax
import jax.numpy as jnp
from jax import lax
from jax.experimental import pallas as pl
from jax.experimental.pallas import tpu as pltpu
from jax.sharding import Mesh, PartitionSpec as P


STEPS = 2
LEVELS = 8
Y, Z, C = 4, 8, 2
GROUPS = Y * C
E = ("y", "z", "c")
BLOCK_CAP = 4
CHUNK = 8
SMALL = 8 << 20
SWAP = [(0, 1), (1, 0)]


def vmem():
    return pl.BlockSpec(memory_space=pltpu.VMEM)


def smem():
    return pl.BlockSpec(memory_space=pltpu.SMEM)


def hbm():
    return pl.BlockSpec(memory_space=pltpu.HBM)


def anywhere():
    return pl.BlockSpec(memory_space=pl.ANY)


def kernel_call(body, grant, **options):
    return pl.pallas_call(body, compiler_params=pltpu.CompilerParams(vmem_limit_bytes=grant), **options)


def near_core(value):
    return pltpu.with_memory_space_constraint(value, pltpu.VMEM)


def off_core(value):
    return pltpu.with_memory_space_constraint(value, pltpu.HBM)


def turned(row):
    return jnp.broadcast_to(row, (8, row.shape[1])).T[:, :1]


def open_kernel(place, counts, history, columns, lags, fanned, wanted, spots, aged, table, held, sems):
    levels, rows = held.shape[0], held.shape[1]
    tile = held.shape[3]
    slots = columns.shape[1]
    cap = BLOCK_CAP * Z
    into = [
        pltpu.make_async_copy(history.at[:, :, pl.ds(row * tile, tile)], held.at[:, row], sems.at[row])
        for row in range(rows)
    ]
    for copy in into:
        copy.start()
    y, c = place[0, 0], place[0, 1]
    col, lag = columns[...], lags[...] - 1
    owner = (col * ((1 << 17) // rows + 1)) >> 17
    local = col - owner * rows
    own_c = lax.rem(owner, C)
    own_z = lax.rem(owner // C, Z)
    own_y = owner // (C * Z)
    group = own_y * C + own_c
    spot = (own_z * levels + lag) * rows + local
    other = (own_c != c).astype(jnp.int32)
    across = (lax.rem(own_y - y + Y, Y) * C + other) * cap
    fresh = (other * (Y * Z) + own_y * Z + own_z) * rows + local
    for copy in into:
        copy.wait()
    out = [pltpu.make_async_copy(held, fanned.at[z], sems.at[rows + z]) for z in range(Z)]
    for copy in out:
        copy.start()
    here = lax.broadcasted_iota(jnp.int32, (slots, slots), 1)
    there = lax.broadcasted_iota(jnp.int32, (slots, slots), 0)
    groups = [group[row : row + 1] for row in range(rows)]
    down = [turned(value) for value in groups]
    asks = lax.broadcasted_iota(jnp.int32, (slots, GROUPS * cap), 1)
    total = jnp.zeros((1, GROUPS * cap), jnp.int32)
    lane = lax.broadcasted_iota(jnp.int32, (1, slots), 1)
    spot_parts, aged_parts, order_parts, where_parts, new_counts = [], [], [], [], []
    for row in range(rows):
        same = (down[row] == groups[row]) & (there < here)
        position = jnp.sum(same.astype(jnp.int32), axis=0, keepdims=True)
        for before in range(row):
            position += jnp.sum((down[before] == groups[row]).astype(jnp.int32), axis=0, keepdims=True)
        at = groups[row] * cap + position
        live = lane < counts[row]
        new = live & (lag[row : row + 1] == 0)
        total += jnp.sum(jnp.where(turned(at) == asks, turned(spot[row : row + 1]), 0), axis=0, keepdims=True)
        spot_parts.append(jnp.where(live, at, -1))
        aged_parts.append(jnp.where(live & ~new, across[row : row + 1] + position, -1))
        fresh_row = jnp.where(new, fresh[row : row + 1], -1)
        marked = turned(new.astype(jnp.int32)) == 1
        rank = jnp.sum((marked & (there < here)).astype(jnp.int32), axis=0, keepdims=True)
        put = marked & (turned(rank) == here)
        order_parts.append(jnp.sum(jnp.where(put, there, 0), axis=0, keepdims=True))
        where_parts.append(jnp.sum(jnp.where(put, turned(fresh_row) + 1, 0), axis=0, keepdims=True) - 1)
        new_counts.append(jnp.sum(new.astype(jnp.int32), axis=1, keepdims=True))
    wanted[...] = total
    rest = jnp.zeros((1, spots.shape[1] - rows * slots), jnp.int32)
    spots[...] = jnp.concatenate([*spot_parts, rest], axis=1)
    aged[...] = jnp.concatenate([*aged_parts, rest], axis=1)
    table[0:1, :] = jnp.concatenate([*order_parts, rest], axis=1)
    table[1:2, :] = jnp.concatenate([*where_parts, rest], axis=1)
    table[2:3, :] = jnp.concatenate(
        [jnp.broadcast_to(count, (1, slots)) for count in new_counts] + [rest], axis=1
    )
    for copy in out:
        copy.wait()


def open_up(place, counts, history, columns, lags, tile):
    levels, dirs, panels = history.shape
    rows = panels // tile
    shapes = ((1, GROUPS * BLOCK_CAP * Z), (1, 128), (1, 128), (3, 128))
    return kernel_call(
        open_kernel,
        SMALL,
        out_shape=(
            pltpu.HBM((Z, levels, rows, dirs, tile), history.dtype),
            pltpu.VMEM(shapes[0], jnp.int32),
            *[pltpu.HBM(shape, jnp.int32) for shape in shapes[1:]],
        ),
        in_specs=[smem(), smem(), hbm(), vmem(), vmem()],
        out_specs=(hbm(), *[vmem()] * 4),
        scratch_shapes=[
            pltpu.VMEM((levels, rows, dirs, tile), history.dtype),
            pltpu.SemaphoreType.DMA((rows + Z,)),
        ],
    )(place, off_core(counts), off_core(history), off_core(columns), off_core(lags))


def whose(place, shift, other):
    y, c = place[0, 0], place[0, 1]
    return lax.rem(y - shift + Y, Y) * C + (c if other == 0 else 1 - c)


def pick_kernel(place, *refs):
    lists, held, first = refs[:Y], refs[Y], refs[Y + 1]
    cap = first.shape[0] // GROUPS
    mine = (place[0, 0] * C + place[0, 1]) * cap
    for shift in range(Y):
        for other in range(C):
            to = whose(place, shift, other) * cap

            @pl.loop(0, cap, step=16)
            def _(base):
                for k in range(16):
                    first[to + base + k] = held[lists[shift][0, other * GROUPS * cap + mine + base + k]]


def pick_later_kernel(place, *refs):
    lists, held, later = refs[:Y], refs[Y], refs[Y + 1 :]
    cap = later[0].shape[0] // C
    back = held.shape[0] // (Z * LEVELS)
    mine = (place[0, 0] * C + place[0, 1]) * cap
    for shift in range(Y):
        for other in range(C):

            @pl.loop(0, cap, step=16)
            def _(base):
                for k in range(16):
                    spot = lists[shift][0, other * GROUPS * cap + mine + base + k]
                    later[shift][other * cap + base + k] = held[jnp.maximum(spot - back, 0)]


def picks(place, lists, held, cap):
    def out(entries):
        return pltpu.HBM((entries, *held.shape[1:]), held.dtype)

    held = near_core(held)
    specs = [smem()] * (1 + Y) + [vmem()]
    first = kernel_call(
        pick_kernel, SMALL, out_shape=out(GROUPS * cap), in_specs=specs, out_specs=vmem()
    )(place, *lists, held)
    later = kernel_call(
        pick_later_kernel, SMALL, out_shape=[out(C * cap)] * Y, in_specs=specs, out_specs=[vmem()] * Y
    )(place, *lists, held)
    return first, later


def pieces_of(spot_at, count, load):
    parts = []
    for k in range(count):
        spot = spot_at(k)
        value = load(jnp.maximum(spot, 0))
        parts.append(jnp.where(spot >= 0, value, jnp.zeros_like(value)))
    return jnp.concatenate(parts, axis=1)


def row_sum(spots, load, weights, row):
    slots, tile = weights.shape[0], weights.shape[1]
    picked = pieces_of(lambda k: spots[0, row * slots + k], slots, load)
    return jnp.dot(picked, weights[...].reshape(slots * tile, tile), preferred_element_type=jnp.float32)


def density_of(own, total, zinv):
    source = (own.astype(jnp.float32) - total).astype(jnp.bfloat16)
    return jnp.dot(source, zinv, preferred_element_type=jnp.float32).astype(jnp.bfloat16)


def start_all(pairs, sems, base=0):
    copies = [pltpu.make_async_copy(src, dst, sems.at[base + i]) for i, (src, dst) in enumerate(pairs)]
    for copy in copies:
        copy.start()
    return copies


def stage_kernel(ztiles_hbm, zinv_hbm, incident_hbm, top, zinv, incident, sems):
    kept = top.shape[0]
    pairs = [(ztiles_hbm.at[row], top.at[row]) for row in range(kept)]
    for copy in start_all([*pairs, (zinv_hbm, zinv), (incident_hbm.at[0], incident)], sems):
        copy.wait()


def stage(ztiles, zinv, incident):
    kept = ztiles.shape[0] - 1
    return kernel_call(
        stage_kernel,
        SMALL,
        out_shape=(
            pltpu.VMEM((kept, *ztiles.shape[1:]), ztiles.dtype),
            pltpu.VMEM(zinv.shape, zinv.dtype),
            pltpu.VMEM(incident.shape[1:], incident.dtype),
        ),
        in_specs=[hbm()] * 3,
        out_specs=[vmem()] * 3,
        scratch_shapes=[pltpu.SemaphoreType.DMA((kept + 2,))],
    )(off_core(ztiles), off_core(zinv), off_core(incident))


def first_kernel(spots, got, top, ztiles_hbm, zinv, incident, out, spread_out, last, sems):
    kept, tile = top.shape[0], top.shape[2]
    copy = pltpu.make_async_copy(ztiles_hbm.at[kept], last, sems.at[0])
    copy.start()
    for row in range(kept + 1):
        if row == kept:
            copy.wait()
        total = row_sum(spots, lambda spot: got[spot], top.at[row] if row < kept else last, row)
        density = density_of(incident[:, row * tile : (row + 1) * tile], total, zinv[row])
        out[row] = density
        for to in range(spread_out.shape[0]):
            spread_out[to, row] = density


def first_step(spots, got, top, ztiles, zinv, incident):
    rows, tile, dirs = ztiles.shape[0], ztiles.shape[2], got.shape[1]
    return kernel_call(
        first_kernel,
        SMALL,
        out_shape=(
            pltpu.HBM((rows, dirs, tile), jnp.bfloat16),
            pltpu.HBM((Y * Z, rows, dirs, tile), jnp.bfloat16),
        ),
        in_specs=[smem(), vmem(), vmem(), hbm(), vmem(), vmem()],
        out_specs=(vmem(), vmem()),
        scratch_shapes=[pltpu.VMEM(ztiles.shape[1:], ztiles.dtype), pltpu.SemaphoreType.DMA((1,))],
    )(off_core(spots), near_core(got), near_core(top), off_core(ztiles), near_core(zinv), near_core(incident))


def aged_kernel(spots, table, before, incident, *refs):
    near, cross = refs[:Y], refs[Y : 2 * Y]
    ztiles_hbm, basis_hbm, packed, fresh, basis, pool, ztiles, sems, fresh_sems = refs[2 * Y :]
    rows, slots, tile = ztiles.shape[0], ztiles.shape[1], ztiles.shape[2]
    cap = near[0].shape[0] // C
    panels = rows * tile
    pairs = []
    for shift in range(Y):
        for source, at in ((near[shift], 0), (cross[shift], cap)):
            pairs.append((source.at[pl.ds(at, cap)], pool.at[pl.ds(len(pairs) * cap, cap)]))
    pairs += [(ztiles_hbm.at[row], ztiles.at[row]) for row in range(rows)]
    pairs.append((basis_hbm, basis))
    copies = start_all(pairs, sems)
    lag_one = []
    for row in range(rows):
        for k in range(CHUNK):
            source = ztiles_hbm.at[row, table[0, row * slots + k]]
            lag_one.append(pltpu.make_async_copy(source, fresh.at[row, k], fresh_sems.at[row, k]))
    for copy in lag_one:
        copy.start()
    for copy in copies[: 2 * Y]:
        copy.wait()
    for row in range(rows):
        copies[2 * Y + row].wait()
        at = slice(row * tile, (row + 1) * tile)
        packed[0, :, at] = incident[1, :, at].astype(jnp.float32)
        packed[1, :, at] = row_sum(spots, lambda spot: pool[spot], ztiles.at[row], row)
    value = jnp.concatenate([before[row] for row in range(rows)], axis=1)
    packed[2, :, :] = value.astype(jnp.float32)
    copies[-1].wait()
    packed[3, :, : basis.shape[1]] = jnp.dot(value, basis[...], preferred_element_type=jnp.float32)
    packed[3, :, basis.shape[1] :] = jnp.zeros((value.shape[0], panels - basis.shape[1]), jnp.float32)
    for copy in lag_one:
        copy.wait()


def aged_step(spots, table, before, incident, near, cross, ztiles, basis):
    rows, dirs, tile = before.shape
    cap = near[0].shape[0] // C
    return kernel_call(
        aged_kernel,
        SMALL,
        out_shape=(
            pltpu.VMEM((4, dirs, rows * tile), jnp.float32),
            pltpu.VMEM((rows, CHUNK, tile, tile), ztiles.dtype),
            pltpu.VMEM(basis.shape, basis.dtype),
        ),
        in_specs=[smem(), smem(), vmem(), vmem()] + [anywhere()] * (2 * Y) + [hbm()] * 2,
        out_specs=[vmem()] * 3,
        scratch_shapes=[
            pltpu.VMEM((2 * Y * cap, dirs, tile), jnp.bfloat16),
            pltpu.VMEM(ztiles.shape, ztiles.dtype),
            pltpu.SemaphoreType.DMA((2 * Y + rows + 1,)),
            pltpu.SemaphoreType.DMA((rows, CHUNK)),
        ],
    )(
        off_core(spots),
        off_core(table),
        off_core(before),
        off_core(incident),
        *near,
        *cross,
        off_core(ztiles),
        off_core(basis),
    )


def second_kernel(table, packed, fresh, zinv, basis, here, there, ztiles_hbm, dens, far, ztiles, flipped, tile_sems):
    rows, slots, tile = ztiles_hbm.shape[0], ztiles_hbm.shape[1], ztiles_hbm.shape[2]
    near = here.shape[0]

    def load(spot):
        ours = here[jnp.minimum(spot, near - 1)]
        theirs = there[jnp.maximum(spot - near, 0)]
        return jnp.where(spot < near, ours, theirs)

    later = []
    for row in range(rows):
        chunks = lax.div(table[2, row * slots] + (CHUNK - 1), CHUNK)
        at = pl.ds(row * tile, tile)
        first = pieces_of(lambda k: table[1, row * slots + k], CHUNK, load)
        total = packed[1, :, at] + jnp.dot(
            first, fresh[row].reshape(CHUNK * tile, tile), preferred_element_type=jnp.float32
        )

        def more(chunk, total):
            copies = []
            for k in range(CHUNK):
                source = ztiles_hbm.at[row, table[0, row * slots + chunk * CHUNK + k]]
                copies.append(pltpu.make_async_copy(source, ztiles.at[k], tile_sems.at[k]))
            for copy in copies:
                copy.start()
            for copy in copies:
                copy.wait()
            picked = pieces_of(lambda k: table[1, row * slots + chunk * CHUNK + k], CHUNK, load)
            return total + jnp.dot(
                picked, ztiles[...].reshape(CHUNK * tile, tile), preferred_element_type=jnp.float32
            )

        total = lax.fori_loop(1, chunks, more, total)
        later.append(density_of(packed[0, :, at], total, zinv[row]))
    value = jnp.concatenate(later, axis=1)
    dens[0] = packed[2].astype(dens.dtype)
    dens[1] = value
    far_second = jnp.dot(value, basis[...], preferred_element_type=jnp.float32)
    both = jnp.concatenate([packed[3, :, : basis.shape[1]], far_second], axis=0)
    lanes = both.shape[0]
    flipped[:, :lanes] = both.T
    owners = far.shape[0]
    each = basis.shape[1] // owners
    cols = [flipped[pl.ds(c, owners, stride=each), :][:, :lanes] for c in range(each)]
    far[...] = jnp.concatenate([*cols, jnp.zeros((owners, far.shape[1] - each * lanes), jnp.float32)], axis=1)


def second_step(table, packed, fresh, zinv, basis, here, there, ztiles, owners):
    tile, dirs = here.shape[2], here.shape[1]
    panels, harmonics = basis.shape
    return kernel_call(
        second_kernel,
        SMALL,
        out_shape=(
            jax.ShapeDtypeStruct((STEPS, dirs, panels), jnp.bfloat16),
            pltpu.VMEM((owners, 128), jnp.float32),
        ),
        in_specs=[smem()] + [vmem()] * 6 + [hbm()],
        out_specs=(vmem(), vmem()),
        scratch_shapes=[
            pltpu.VMEM((CHUNK, tile, tile), ztiles.dtype),
            pltpu.VMEM((harmonics, 128), jnp.float32),
            pltpu.SemaphoreType.DMA((CHUNK,)),
        ],
    )(
        off_core(table),
        near_core(packed),
        near_core(fresh),
        near_core(zinv),
        near_core(basis),
        near_core(here),
        near_core(there),
        off_core(ztiles),
    )


def sum_kernel(parts, out):
    total = jnp.sum(parts[...], axis=0, keepdims=True)
    steps, each, dirs = out.shape
    for step in range(steps):
        for c in range(each):
            at = (c * steps + step) * dirs
            out[step, c : c + 1, :] = total[:, at : at + dirs]


def sum_parts(parts, steps, each, dirs):
    return kernel_call(
        sum_kernel,
        SMALL,
        out_shape=jax.ShapeDtypeStruct((steps, each, dirs), jnp.float32),
        in_specs=[vmem()],
        out_specs=vmem(),
    )(near_core(parts))


def shifted(value, axis, length, shift):
    return lax.ppermute(value, axis, [(i, (i + shift) % length) for i in range(length)])


def march(history, incident, ztiles, zinv, columns, lags, counts, basis):
    rows, tile = ztiles.shape[0], ztiles.shape[2]
    dirs = history.shape[1]
    owners = Y * Z * C
    cap = BLOCK_CAP * Z
    place = jnp.stack([lax.axis_index("y"), lax.axis_index("c")]).reshape(1, 2)
    fanned, wanted, spots, aged, table = open_up(place, counts, history, columns, lags, tile)
    held = lax.all_to_all(fanned, "z", 0, 0, tiled=True).reshape(-1, dirs, tile)
    both = jnp.concatenate([wanted, lax.ppermute(wanted, "c", SWAP)], axis=1)
    lists = [both] + [shifted(both, "y", Y, s) for s in range(1, Y)]
    first, later = picks(place, lists, held, cap)
    got = lax.all_to_all(first.reshape(GROUPS, cap, dirs, tile), ("y", "c"), 0, 0, tiled=True)
    near = [later[0]] + [shifted(later[s], "y", Y, -s) for s in range(1, Y)]
    cross = [lax.ppermute(piece, "c", SWAP) for piece in near]
    top, inverse, driven = stage(ztiles, zinv, incident)
    density, fanned = first_step(spots, got.reshape(GROUPS * cap, dirs, tile), top, ztiles, inverse, driven)
    here = lax.all_to_all(fanned, ("y", "z"), 0, 0, tiled=True).reshape(Y * Z * rows, dirs, tile)
    packed, lag_one, weights = aged_step(aged, table, density, incident, near, cross, ztiles, basis)
    there = lax.ppermute(here, "c", SWAP)
    dens, far = second_step(table, packed, lag_one, inverse, weights, here, there, ztiles, owners)
    each = basis.shape[1] // owners
    parts = lax.all_to_all(far.reshape(owners, 1, 128), E, 0, 0, tiled=True).reshape(owners, 128)
    total = sum_parts(parts, STEPS, each, dirs)
    return dens, total.transpose(0, 2, 1)


def solution(mesh):
    fine = Mesh(mesh.devices.reshape(Y, Z, C, mesh.shape["dir"]), ("y", "z", "c", "dir"))
    in_specs = (
        P(None, "dir", E),
        P(None, "dir", E),
        P(E, None, None, None),
        P(E, None, None),
        P(E, None),
        P(E, None),
        P(E),
        P(E, None),
    )
    out_specs = (P(None, "dir", E), P(None, "dir", E))
    return jax.shard_map(march, mesh=fine, in_specs=in_specs, out_specs=out_specs, check_vma=False)
```

```python
import jax
import jax.numpy as jnp
from jax import lax
from jax.experimental import pallas as pl
from jax.experimental.pallas import tpu as pltpu
from jax.sharding import Mesh, PartitionSpec as P


STEPS = 2
LEVELS = 8
Y, Z, C = 4, 8, 2
GROUPS = Y * C
E = ("y", "z", "c")
BLOCK_CAP = 4
CHUNK = 8
SMALL = 8 << 20
SWAP = [(0, 1), (1, 0)]


def vmem():
    return pl.BlockSpec(memory_space=pltpu.VMEM)


def smem():
    return pl.BlockSpec(memory_space=pltpu.SMEM)


def hbm():
    return pl.BlockSpec(memory_space=pltpu.HBM)


def anywhere():
    return pl.BlockSpec(memory_space=pl.ANY)


def kernel_call(body, grant, **options):
    return pl.pallas_call(body, compiler_params=pltpu.CompilerParams(vmem_limit_bytes=grant), **options)


def near_core(value):
    return pltpu.with_memory_space_constraint(value, pltpu.VMEM)


def off_core(value):
    return pltpu.with_memory_space_constraint(value, pltpu.HBM)


def turned(row):
    return jnp.broadcast_to(row, (8, row.shape[1])).T[:, :1]


def open_kernel(history, fanned, held, sems):
    rows, tile = held.shape[1], held.shape[3]
    into = start_all(
        [(history.at[:, :, pl.ds(row * tile, tile)], held.at[:, row]) for row in range(rows)], sems
    )
    for copy in into:
        copy.wait()
    for copy in start_all([(held, fanned.at[z]) for z in range(Z)], sems, rows):
        copy.wait()


def open_up(history, tile):
    levels, dirs, panels = history.shape
    rows = panels // tile
    return kernel_call(
        open_kernel,
        SMALL,
        out_shape=pltpu.HBM((Z, levels, rows, dirs, tile), history.dtype),
        in_specs=[hbm()],
        out_specs=hbm(),
        scratch_shapes=[
            pltpu.VMEM((levels, rows, dirs, tile), history.dtype),
            pltpu.SemaphoreType.DMA((rows + Z,)),
        ],
    )(off_core(history))


class Slots:
    def __init__(self, columns, lags):
        self.rows, self.count = columns.shape
        col, self.lag = columns[...], lags[...] - 1
        owner = (col * ((1 << 17) // self.rows + 1)) >> 17
        self.local = col - owner * self.rows
        self.c = lax.rem(owner, C)
        self.z = lax.rem(owner // C, Z)
        self.y = owner // (C * Z)
        group = self.y * C + self.c
        self.here = lax.broadcasted_iota(jnp.int32, (self.count, self.count), 1)
        self.there = lax.broadcasted_iota(jnp.int32, (self.count, self.count), 0)
        groups = [group[row : row + 1] for row in range(self.rows)]
        down = [turned(value) for value in groups]
        self.position = []
        for row in range(self.rows):
            same = (down[row] == groups[row]) & (self.there < self.here)
            position = jnp.sum(same.astype(jnp.int32), axis=0, keepdims=True)
            for before in range(row):
                position += jnp.sum((down[before] == groups[row]).astype(jnp.int32), axis=0, keepdims=True)
            self.position.append(position)
        self.at = [groups[row] * (BLOCK_CAP * Z) + self.position[row] for row in range(self.rows)]


def plan_kernel(columns, lags, wanted):
    slots = Slots(columns, lags)
    spot = (slots.z * LEVELS + slots.lag) * slots.rows + slots.local
    asks = lax.broadcasted_iota(jnp.int32, (slots.count, wanted.shape[1]), 1)
    total = jnp.zeros(wanted.shape, jnp.int32)
    for row in range(slots.rows):
        mine = jnp.where(turned(slots.at[row]) == asks, turned(spot[row : row + 1]), 0)
        total += jnp.sum(mine, axis=0, keepdims=True)
    wanted[...] = total


def plan(columns, lags):
    return kernel_call(
        plan_kernel,
        SMALL,
        out_shape=pltpu.VMEM((1, GROUPS * BLOCK_CAP * Z), jnp.int32),
        in_specs=[vmem(), vmem()],
        out_specs=vmem(),
    )(off_core(columns), off_core(lags))


def chart_kernel(place, counts, columns, lags, spots, aged, table):
    slots = Slots(columns, lags)
    cap = BLOCK_CAP * Z
    y, c = place[0, 0], place[0, 1]
    other = (slots.c != c).astype(jnp.int32)
    across = (lax.rem(slots.y - y + Y, Y) * C + other) * cap
    fresh = (other * (Y * Z) + slots.y * Z + slots.z) * slots.rows + slots.local
    lane = lax.broadcasted_iota(jnp.int32, (1, slots.count), 1)
    spot_parts, aged_parts, order_parts, where_parts, new_parts = [], [], [], [], []
    for row in range(slots.rows):
        live = lane < counts[row]
        new = live & (slots.lag[row : row + 1] == 0)
        spot_parts.append(jnp.where(live, slots.at[row], -1))
        aged_parts.append(jnp.where(live & ~new, across[row : row + 1] + slots.position[row], -1))
        fresh_row = jnp.where(new, fresh[row : row + 1], -1)
        marked = turned(new.astype(jnp.int32)) == 1
        rank = jnp.sum((marked & (slots.there < slots.here)).astype(jnp.int32), axis=0, keepdims=True)
        put = marked & (turned(rank) == slots.here)
        order_parts.append(jnp.sum(jnp.where(put, slots.there, 0), axis=0, keepdims=True))
        where_parts.append(jnp.sum(jnp.where(put, turned(fresh_row) + 1, 0), axis=0, keepdims=True) - 1)
        new_count = jnp.sum(new.astype(jnp.int32), axis=1, keepdims=True)
        new_parts.append(jnp.broadcast_to(new_count, (1, slots.count)))
    rest = jnp.zeros((1, spots.shape[1] - slots.rows * slots.count), jnp.int32)
    tail = rest
    for row in range(slots.rows):
        tail = jnp.where(lax.broadcasted_iota(jnp.int32, rest.shape, 1) == row, counts[row], tail)
    spots[...] = jnp.concatenate([*spot_parts, tail], axis=1)
    aged[...] = jnp.concatenate([*aged_parts, tail], axis=1)
    table[0:1, :] = jnp.concatenate([*order_parts, rest], axis=1)
    table[1:2, :] = jnp.concatenate([*where_parts, rest], axis=1)
    table[2:3, :] = jnp.concatenate([*new_parts, rest], axis=1)


def chart(place, counts, columns, lags):
    return kernel_call(
        chart_kernel,
        SMALL,
        out_shape=tuple(pltpu.VMEM((length, 128), jnp.int32) for length in (1, 1, 3)),
        in_specs=[smem(), smem(), vmem(), vmem()],
        out_specs=[vmem()] * 3,
    )(place, off_core(counts), off_core(columns), off_core(lags))


def whose(place, shift, other):
    y, c = place[0, 0], place[0, 1]
    return lax.rem(y - shift + Y, Y) * C + (c if other == 0 else 1 - c)


def pick_kernel(place, *refs):
    lists, held, first, kept, sems = refs[:Y], refs[Y], refs[Y + 1], refs[Y + 2], refs[Y + 3]
    cap = first.shape[0] // GROUPS
    mine = (place[0, 0] * C + place[0, 1]) * cap
    copies = []
    for shift in range(Y):
        for other in range(C):
            base = len(copies) * cap

            @pl.loop(0, cap, step=16)
            def _(entry):
                for k in range(16):
                    spot = lists[shift][0, other * GROUPS * cap + mine + entry + k]
                    kept[base + entry + k] = held[spot]

            to = whose(place, shift, other) * cap
            pair = (kept.at[pl.ds(base, cap)], first.at[pl.ds(to, cap)])
            copies += start_all([pair], sems, len(copies))
    for copy in copies:
        copy.wait()


def pick_later_kernel(place, *refs):
    lists, held, later, kept, sems = refs[:Y], refs[Y], refs[Y + 1 : 2 * Y + 1], refs[2 * Y + 1], refs[2 * Y + 2]
    cap = later[0].shape[0] // C
    back = held.shape[0] // (Z * LEVELS)
    mine = (place[0, 0] * C + place[0, 1]) * cap
    copies = []
    for shift in range(Y):
        for other in range(C):

            @pl.loop(0, cap, step=16)
            def _(entry):
                for k in range(16):
                    spot = lists[shift][0, other * GROUPS * cap + mine + entry + k]
                    kept[shift, other * cap + entry + k] = held[jnp.maximum(spot - back, 0)]

        copies += start_all([(kept.at[shift], later[shift])], sems, shift)
    for copy in copies:
        copy.wait()


def picks(place, lists, held, cap):
    def out(entries):
        return pltpu.HBM((entries, *held.shape[1:]), held.dtype)

    held = near_core(held)
    lists = [near_core(value) for value in lists]
    specs = [smem()] * (1 + Y) + [vmem()]
    first = kernel_call(
        pick_kernel,
        SMALL,
        out_shape=out(GROUPS * cap),
        in_specs=specs,
        out_specs=hbm(),
        scratch_shapes=[
            pltpu.VMEM((GROUPS * cap, *held.shape[1:]), held.dtype),
            pltpu.SemaphoreType.DMA((GROUPS,)),
        ],
    )(place, *lists, held)
    later = kernel_call(
        pick_later_kernel,
        SMALL,
        out_shape=[out(C * cap)] * Y,
        in_specs=specs,
        out_specs=[hbm()] * Y,
        scratch_shapes=[
            pltpu.VMEM((Y, C * cap, *held.shape[1:]), held.dtype),
            pltpu.SemaphoreType.DMA((Y,)),
        ],
    )(place, *lists, held)
    return first, later


def pieces_of(spot_at, count, load):
    parts = []
    for k in range(count):
        spot = spot_at(k)
        value = load(jnp.maximum(spot, 0))
        parts.append(jnp.where(spot >= 0, value, jnp.zeros_like(value)))
    return jnp.concatenate(parts, axis=1)


def row_sum(spots, load, weights, row):
    slots, tile = weights.shape[0], weights.shape[1]
    picked = pieces_of(lambda k: spots[0, row * slots + k], slots, load)
    return jnp.dot(picked, weights[...].reshape(slots * tile, tile), preferred_element_type=jnp.float32)


def density_of(own, total, zinv):
    source = (own.astype(jnp.float32) - total).astype(jnp.bfloat16)
    return jnp.dot(source, zinv, preferred_element_type=jnp.float32).astype(jnp.bfloat16)


def start_all(pairs, sems, base=0):
    copies = [pltpu.make_async_copy(src, dst, sems.at[base + i]) for i, (src, dst) in enumerate(pairs)]
    for copy in copies:
        copy.start()
    return copies


def live_tiles(count, source, target, sems, row, act):
    slots = target.shape[0]
    for chunk in range(slots // CHUNK):
        part = pl.ds(chunk * CHUNK, CHUNK)

        @pl.when(chunk * CHUNK < count)
        def _():
            copy = pltpu.make_async_copy(source.at[part], target.at[part], sems.at[row, chunk])
            if act == "start":
                copy.start()
            else:
                copy.wait()

        if act == "start":

            @pl.when(chunk * CHUNK >= count)
            def _():
                target[part] = jnp.zeros((CHUNK, *target.shape[1:]), target.dtype)


def stage_kernel(counts, ztiles_hbm, zinv_hbm, incident_hbm, top, zinv, incident, sems, tile_sems):
    kept = top.shape[0]
    for row in range(kept):
        live_tiles(counts[row], ztiles_hbm.at[row], top.at[row], tile_sems, row, "start")
    for copy in start_all([(zinv_hbm, zinv), (incident_hbm.at[0], incident)], sems):
        copy.wait()
    for row in range(kept):
        live_tiles(counts[row], ztiles_hbm.at[row], top.at[row], tile_sems, row, "wait")


def stage(counts, ztiles, zinv, incident):
    kept = ztiles.shape[0] - 1
    return kernel_call(
        stage_kernel,
        SMALL,
        out_shape=(
            pltpu.VMEM((kept, *ztiles.shape[1:]), ztiles.dtype),
            pltpu.VMEM(zinv.shape, zinv.dtype),
            pltpu.VMEM(incident.shape[1:], incident.dtype),
        ),
        in_specs=[smem()] + [hbm()] * 3,
        out_specs=[vmem()] * 3,
        scratch_shapes=[
            pltpu.SemaphoreType.DMA((2,)),
            pltpu.SemaphoreType.DMA((kept, ztiles.shape[1] // CHUNK)),
        ],
    )(off_core(counts), off_core(ztiles), off_core(zinv), off_core(incident))


def first_kernel(spots, got, top, ztiles_hbm, zinv, incident, out, spread_out, last, kept_out, sems, tile_sems):
    kept, slots, tile = top.shape[0], top.shape[1], top.shape[2]
    count = spots[0, (kept + 1) * slots + kept]
    live_tiles(count, ztiles_hbm.at[kept], last, tile_sems, 0, "start")
    copies = []
    for row in range(kept + 1):
        if row == kept:
            live_tiles(count, ztiles_hbm.at[kept], last, tile_sems, 0, "wait")
        total = row_sum(spots, lambda spot: got[spot], top.at[row] if row < kept else last, row)
        density = density_of(incident[:, row * tile : (row + 1) * tile], total, zinv[row])
        out[row] = density
        for to in range(spread_out.shape[0]):
            kept_out[row, to] = density
        copies += start_all([(kept_out.at[row], spread_out.at[:, row])], sems, row)
    for copy in copies:
        copy.wait()


def first_step(spots, got, top, ztiles, zinv, incident):
    rows, slots, tile, dirs = ztiles.shape[0], ztiles.shape[1], ztiles.shape[2], got.shape[1]
    return kernel_call(
        first_kernel,
        SMALL,
        out_shape=(
            pltpu.HBM((rows, dirs, tile), jnp.bfloat16),
            pltpu.HBM((Y * Z, rows, dirs, tile), jnp.bfloat16),
        ),
        in_specs=[smem(), vmem(), vmem(), hbm(), vmem(), vmem()],
        out_specs=(vmem(), hbm()),
        scratch_shapes=[
            pltpu.VMEM(ztiles.shape[1:], ztiles.dtype),
            pltpu.VMEM((rows, Y * Z, dirs, tile), jnp.bfloat16),
            pltpu.SemaphoreType.DMA((rows,)),
            pltpu.SemaphoreType.DMA((1, slots // CHUNK)),
        ],
    )(near_core(spots), near_core(got), near_core(top), off_core(ztiles), near_core(zinv), near_core(incident))


def aged_kernel(spots, table, before, incident, *refs):
    near, cross = refs[:Y], refs[Y : 2 * Y]
    ztiles_hbm, basis_hbm, packed, fresh, basis, pool, ztiles, sems, tile_sems, fresh_sems = refs[2 * Y :]
    rows, slots, tile = ztiles.shape[0], ztiles.shape[1], ztiles.shape[2]
    cap = near[0].shape[0] // C
    panels = rows * tile
    counts = [spots[0, rows * slots + row] for row in range(rows)]
    pairs = []
    for shift in range(Y):
        for source, at in ((near[shift], 0), (cross[shift], cap)):
            pairs.append((source.at[pl.ds(at, cap)], pool.at[pl.ds(len(pairs) * cap, cap)]))
    copies = start_all(pairs, sems)
    for row in range(rows):
        live_tiles(counts[row], ztiles_hbm.at[row], ztiles.at[row], tile_sems, row, "start")
    weights = start_all([(basis_hbm, basis)], sems, len(pairs))[0]
    for copy in copies:
        copy.wait()
    lag_one = []
    for row in range(rows):
        live_tiles(counts[row], ztiles_hbm.at[row], ztiles.at[row], tile_sems, row, "wait")
        for k in range(CHUNK):
            source = ztiles.at[row, table[0, row * slots + k]]
            lag_one.append(pltpu.make_async_copy(source, fresh.at[row, k], fresh_sems.at[row, k]))
            lag_one[-1].start()
        at = slice(row * tile, (row + 1) * tile)
        packed[0, :, at] = incident[1, :, at].astype(jnp.float32)
        packed[1, :, at] = row_sum(spots, lambda spot: pool[spot], ztiles.at[row], row)
    value = jnp.concatenate([before[row] for row in range(rows)], axis=1)
    packed[2, :, :] = value.astype(jnp.float32)
    weights.wait()
    packed[3, :, : basis.shape[1]] = jnp.dot(value, basis[...], preferred_element_type=jnp.float32)
    packed[3, :, basis.shape[1] :] = jnp.zeros((value.shape[0], panels - basis.shape[1]), jnp.float32)
    for copy in lag_one:
        copy.wait()


def aged_step(spots, table, before, incident, near, cross, ztiles, basis):
    rows, dirs, tile = before.shape
    cap = near[0].shape[0] // C
    return kernel_call(
        aged_kernel,
        SMALL,
        out_shape=(
            pltpu.VMEM((4, dirs, rows * tile), jnp.float32),
            pltpu.VMEM((rows, CHUNK, tile, tile), ztiles.dtype),
            pltpu.VMEM(basis.shape, basis.dtype),
        ),
        in_specs=[smem(), smem(), vmem(), vmem()] + [anywhere()] * (2 * Y) + [hbm()] * 2,
        out_specs=[vmem()] * 3,
        scratch_shapes=[
            pltpu.VMEM((2 * Y * cap, dirs, tile), jnp.bfloat16),
            pltpu.VMEM(ztiles.shape, ztiles.dtype),
            pltpu.SemaphoreType.DMA((2 * Y + 1,)),
            pltpu.SemaphoreType.DMA((rows, ztiles.shape[1] // CHUNK)),
            pltpu.SemaphoreType.DMA((rows, CHUNK)),
        ],
    )(
        near_core(spots),
        near_core(table),
        off_core(before),
        off_core(incident),
        *near,
        *cross,
        off_core(ztiles),
        off_core(basis),
    )


def second_kernel(table, packed, fresh, zinv, basis, here, there, ztiles_hbm, dens, far, ztiles, flipped, tile_sems):
    rows, slots, tile = ztiles_hbm.shape[0], ztiles_hbm.shape[1], ztiles_hbm.shape[2]
    near = here.shape[0]

    def load(spot):
        ours = here[jnp.minimum(spot, near - 1)]
        theirs = there[jnp.maximum(spot - near, 0)]
        return jnp.where(spot < near, ours, theirs)

    later = []
    for row in range(rows):
        chunks = lax.div(table[2, row * slots] + (CHUNK - 1), CHUNK)
        at = pl.ds(row * tile, tile)
        first = pieces_of(lambda k: table[1, row * slots + k], CHUNK, load)
        total = packed[1, :, at] + jnp.dot(
            first, fresh[row].reshape(CHUNK * tile, tile), preferred_element_type=jnp.float32
        )

        def more(chunk, total):
            copies = []
            for k in range(CHUNK):
                source = ztiles_hbm.at[row, table[0, row * slots + chunk * CHUNK + k]]
                copies.append(pltpu.make_async_copy(source, ztiles.at[k], tile_sems.at[k]))
            for copy in copies:
                copy.start()
            for copy in copies:
                copy.wait()
            picked = pieces_of(lambda k: table[1, row * slots + chunk * CHUNK + k], CHUNK, load)
            return total + jnp.dot(
                picked, ztiles[...].reshape(CHUNK * tile, tile), preferred_element_type=jnp.float32
            )

        total = lax.fori_loop(1, chunks, more, total)
        later.append(density_of(packed[0, :, at], total, zinv[row]))
    value = jnp.concatenate(later, axis=1)
    dens[0] = packed[2].astype(dens.dtype)
    dens[1] = value
    far_second = jnp.dot(value, basis[...], preferred_element_type=jnp.float32)
    both = jnp.concatenate([packed[3, :, : basis.shape[1]], far_second], axis=0)
    lanes = both.shape[0]
    flipped[:, :lanes] = both.T
    owners = far.shape[0]
    each = basis.shape[1] // owners
    cols = [flipped[pl.ds(c, owners, stride=each), :][:, :lanes] for c in range(each)]
    far[...] = jnp.concatenate([*cols, jnp.zeros((owners, far.shape[1] - each * lanes), jnp.float32)], axis=1)


def second_step(table, packed, fresh, zinv, basis, here, there, ztiles, owners):
    tile, dirs = here.shape[2], here.shape[1]
    panels, harmonics = basis.shape
    return kernel_call(
        second_kernel,
        SMALL,
        out_shape=(
            jax.ShapeDtypeStruct((STEPS, dirs, panels), jnp.bfloat16),
            pltpu.VMEM((owners, 128), jnp.float32),
        ),
        in_specs=[smem()] + [vmem()] * 6 + [hbm()],
        out_specs=(vmem(), vmem()),
        scratch_shapes=[
            pltpu.VMEM((CHUNK, tile, tile), ztiles.dtype),
            pltpu.VMEM((harmonics, 128), jnp.float32),
            pltpu.SemaphoreType.DMA((CHUNK,)),
        ],
    )(
        near_core(table),
        near_core(packed),
        near_core(fresh),
        near_core(zinv),
        near_core(basis),
        near_core(here),
        near_core(there),
        off_core(ztiles),
    )


def sum_kernel(parts, out):
    total = jnp.sum(parts[...], axis=0, keepdims=True)
    steps, each, dirs = out.shape
    for step in range(steps):
        for c in range(each):
            at = (c * steps + step) * dirs
            out[step, c : c + 1, :] = total[:, at : at + dirs]


def sum_parts(parts, steps, each, dirs):
    return kernel_call(
        sum_kernel,
        SMALL,
        out_shape=jax.ShapeDtypeStruct((steps, each, dirs), jnp.float32),
        in_specs=[vmem()],
        out_specs=vmem(),
    )(near_core(parts))


def shifted(value, axis, length, shift):
    return lax.ppermute(value, axis, [(i, (i + shift) % length) for i in range(length)])


def march(history, incident, ztiles, zinv, columns, lags, counts, basis):
    rows, tile = ztiles.shape[0], ztiles.shape[2]
    dirs = history.shape[1]
    owners = Y * Z * C
    cap = BLOCK_CAP * Z
    place = jnp.stack([lax.axis_index("y"), lax.axis_index("c")]).reshape(1, 2)
    held = lax.all_to_all(open_up(history, tile), "z", 0, 0, tiled=True).reshape(-1, dirs, tile)
    wanted = plan(columns, lags)
    spots, aged, table = chart(place, counts, columns, lags)
    both = jnp.concatenate([wanted, lax.ppermute(wanted, "c", SWAP)], axis=1)
    lists = [both] + [shifted(both, "y", Y, s) for s in range(1, Y)]
    first, later = picks(place, lists, held, cap)
    got = lax.all_to_all(first.reshape(GROUPS, cap, dirs, tile), ("y", "c"), 0, 0, tiled=True)
    near = [later[0]] + [shifted(later[s], "y", Y, -s) for s in range(1, Y)]
    cross = [lax.ppermute(piece, "c", SWAP) for piece in near]
    top, inverse, driven = stage(counts, ztiles, zinv, incident)
    density, fanned = first_step(spots, got.reshape(GROUPS * cap, dirs, tile), top, ztiles, inverse, driven)
    here = lax.all_to_all(fanned, ("y", "z"), 0, 0, tiled=True).reshape(Y * Z * rows, dirs, tile)
    packed, lag_one, weights = aged_step(aged, table, density, incident, near, cross, ztiles, basis)
    there = lax.ppermute(here, "c", SWAP)
    dens, far = second_step(table, packed, lag_one, inverse, weights, here, there, ztiles, owners)
    each = basis.shape[1] // owners
    parts = lax.all_to_all(far.reshape(owners, 1, 128), E, 0, 0, tiled=True).reshape(owners, 128)
    total = sum_parts(parts, STEPS, each, dirs)
    return dens, total.transpose(0, 2, 1)


def solution(mesh):
    fine = Mesh(mesh.devices.reshape(Y, Z, C, mesh.shape["dir"]), ("y", "z", "c", "dir"))
    in_specs = (
        P(None, "dir", E),
        P(None, "dir", E),
        P(E, None, None, None),
        P(E, None, None),
        P(E, None),
        P(E, None),
        P(E),
        P(E, None),
    )
    out_specs = (P(None, "dir", E), P(None, "dir", E))
    return jax.shard_map(march, mesh=fine, in_specs=in_specs, out_specs=out_specs, check_vma=False)
```

```python
import jax
import jax.numpy as jnp
from jax import lax
from jax.experimental import pallas as pl
from jax.experimental.pallas import tpu as pltpu
from jax.sharding import Mesh, PartitionSpec as P


STEPS = 2
LEVELS = 8
Y, Z, C = 4, 8, 2
GROUPS = Y * C
E = ("y", "z", "c")
BLOCK_CAP = 4
CHUNK = 8
SMALL = 8 << 20
SWAP = [(0, 1), (1, 0)]


def vmem():
    return pl.BlockSpec(memory_space=pltpu.VMEM)


def smem():
    return pl.BlockSpec(memory_space=pltpu.SMEM)


def hbm():
    return pl.BlockSpec(memory_space=pltpu.HBM)


def anywhere():
    return pl.BlockSpec(memory_space=pl.ANY)


def kernel_call(body, grant, **options):
    return pl.pallas_call(body, compiler_params=pltpu.CompilerParams(vmem_limit_bytes=grant), **options)


def near_core(value):
    return pltpu.with_memory_space_constraint(value, pltpu.VMEM)


def scalar_core(value):
    return pltpu.with_memory_space_constraint(value, pltpu.SMEM)


def off_core(value):
    return pltpu.with_memory_space_constraint(value, pltpu.HBM)


def turned(row):
    return jnp.broadcast_to(row, (8, row.shape[1])).T[:, :1]


def open_kernel(history, fanned, held, sems):
    rows, tile = held.shape[1], held.shape[3]
    into = start_all(
        [(history.at[:, :, pl.ds(row * tile, tile)], held.at[:, row]) for row in range(rows)], sems
    )
    for copy in into:
        copy.wait()
    for copy in start_all([(held, fanned.at[z]) for z in range(Z)], sems, rows):
        copy.wait()


def open_up(history, tile):
    levels, dirs, panels = history.shape
    rows = panels // tile
    return kernel_call(
        open_kernel,
        SMALL,
        out_shape=pltpu.HBM((Z, levels, rows, dirs, tile), history.dtype),
        in_specs=[hbm()],
        out_specs=hbm(),
        scratch_shapes=[
            pltpu.VMEM((levels, rows, dirs, tile), history.dtype),
            pltpu.SemaphoreType.DMA((rows + Z,)),
        ],
    )(off_core(history))


class Slots:
    def __init__(self, columns, lags):
        self.rows, self.count = columns.shape
        col, self.lag = columns[...], lags[...] - 1
        owner = (col * ((1 << 17) // self.rows + 1)) >> 17
        self.local = col - owner * self.rows
        self.c = lax.rem(owner, C)
        self.z = lax.rem(owner // C, Z)
        self.y = owner // (C * Z)
        group = self.y * C + self.c
        self.here = lax.broadcasted_iota(jnp.int32, (self.count, self.count), 1)
        self.there = lax.broadcasted_iota(jnp.int32, (self.count, self.count), 0)
        groups = [group[row : row + 1] for row in range(self.rows)]
        down = [turned(value) for value in groups]
        self.position = []
        for row in range(self.rows):
            same = (down[row] == groups[row]) & (self.there < self.here)
            position = jnp.sum(same.astype(jnp.int32), axis=0, keepdims=True)
            for before in range(row):
                position += jnp.sum((down[before] == groups[row]).astype(jnp.int32), axis=0, keepdims=True)
            self.position.append(position)
        self.at = [groups[row] * (BLOCK_CAP * Z) + self.position[row] for row in range(self.rows)]


def plan_kernel(columns, lags, wanted):
    slots = Slots(columns, lags)
    spot = (slots.z * LEVELS + slots.lag) * slots.rows + slots.local
    asks = lax.broadcasted_iota(jnp.int32, (slots.count, wanted.shape[1]), 1)
    total = jnp.zeros(wanted.shape, jnp.int32)
    for row in range(slots.rows):
        mine = jnp.where(turned(slots.at[row]) == asks, turned(spot[row : row + 1]), 0)
        total += jnp.sum(mine, axis=0, keepdims=True)
    wanted[...] = total


def plan(columns, lags):
    return kernel_call(
        plan_kernel,
        SMALL,
        out_shape=pltpu.VMEM((1, GROUPS * BLOCK_CAP * Z), jnp.int32),
        in_specs=[vmem(), vmem()],
        out_specs=vmem(),
    )(off_core(columns), off_core(lags))


def chart_kernel(counts, columns, lags, spots_out, aged_out, table_out, spots, aged, table, sems):
    slots = Slots(columns, lags)
    cap = BLOCK_CAP * Z
    y, c = lax.axis_index("y"), lax.axis_index("c")
    other = (slots.c != c).astype(jnp.int32)
    across = (lax.rem(slots.y - y + Y, Y) * C + other) * cap
    fresh = (other * (Y * Z) + slots.y * Z + slots.z) * slots.rows + slots.local
    lane = lax.broadcasted_iota(jnp.int32, (1, slots.count), 1)
    spot_parts, aged_parts, order_parts, where_parts, new_parts = [], [], [], [], []
    for row in range(slots.rows):
        live = lane < counts[row]
        new = live & (slots.lag[row : row + 1] == 0)
        spot_parts.append(jnp.where(live, slots.at[row], -1))
        aged_parts.append(jnp.where(live & ~new, across[row : row + 1] + slots.position[row], -1))
        fresh_row = jnp.where(new, fresh[row : row + 1], -1)
        marked = turned(new.astype(jnp.int32)) == 1
        rank = jnp.sum((marked & (slots.there < slots.here)).astype(jnp.int32), axis=0, keepdims=True)
        put = marked & (turned(rank) == slots.here)
        order_parts.append(jnp.sum(jnp.where(put, slots.there, 0), axis=0, keepdims=True))
        where_parts.append(jnp.sum(jnp.where(put, turned(fresh_row) + 1, 0), axis=0, keepdims=True) - 1)
        new_count = jnp.sum(new.astype(jnp.int32), axis=1, keepdims=True)
        new_parts.append(jnp.broadcast_to(new_count, (1, slots.count)))
    rest = jnp.zeros((1, spots.shape[1] - slots.rows * slots.count), jnp.int32)
    tail = rest
    for row in range(slots.rows):
        tail = jnp.where(lax.broadcasted_iota(jnp.int32, rest.shape, 1) == row, counts[row], tail)
    spots[...] = jnp.concatenate([*spot_parts, tail], axis=1)
    aged[...] = jnp.concatenate([*aged_parts, tail], axis=1)
    table[0:1, :] = jnp.concatenate([*order_parts, rest], axis=1)
    table[1:2, :] = jnp.concatenate([*where_parts, rest], axis=1)
    table[2:3, :] = jnp.concatenate([*new_parts, rest], axis=1)
    for copy in start_all([(spots, spots_out), (aged, aged_out), (table, table_out)], sems):
        copy.wait()


def chart(counts, columns, lags):
    lengths = (1, 1, 3)
    return kernel_call(
        chart_kernel,
        SMALL,
        out_shape=tuple(pltpu.SMEM((length, 128), jnp.int32) for length in lengths),
        in_specs=[smem(), vmem(), vmem()],
        out_specs=[smem()] * 3,
        scratch_shapes=[pltpu.VMEM((length, 128), jnp.int32) for length in lengths]
        + [pltpu.SemaphoreType.DMA((3,))],
    )(off_core(counts), off_core(columns), off_core(lags))


def gather_lists_kernel(*refs):
    for copy in start_all(list(zip(refs[:Y], refs[Y : 2 * Y])), refs[2 * Y]):
        copy.wait()


def gather_lists(lists):
    return kernel_call(
        gather_lists_kernel,
        SMALL,
        out_shape=tuple(pltpu.SMEM(value.shape, value.dtype) for value in lists),
        in_specs=[vmem()] * Y,
        out_specs=[smem()] * Y,
        scratch_shapes=[pltpu.SemaphoreType.DMA((Y,))],
    )(*[near_core(value) for value in lists])


def whose(shift, other):
    y, c = lax.axis_index("y"), lax.axis_index("c")
    return lax.rem(y - shift + Y, Y) * C + (c if other == 0 else 1 - c)


def pick_kernel(*refs):
    lists, held, first, kept, sems = refs[:Y], refs[Y], refs[Y + 1], refs[Y + 2], refs[Y + 3]
    cap = first.shape[0] // GROUPS
    mine = (lax.axis_index("y") * C + lax.axis_index("c")) * cap
    copies = []
    for shift in range(Y):
        for other in range(C):
            base = len(copies) * cap

            @pl.loop(0, cap, step=16)
            def _(entry):
                for k in range(16):
                    spot = lists[shift][0, other * GROUPS * cap + mine + entry + k]
                    kept[base + entry + k] = held[spot]

            to = whose(shift, other) * cap
            pair = (kept.at[pl.ds(base, cap)], first.at[pl.ds(to, cap)])
            copies += start_all([pair], sems, len(copies))
    for copy in copies:
        copy.wait()


def pick_later_kernel(*refs):
    lists, held, later, kept, sems = refs[:Y], refs[Y], refs[Y + 1 : 2 * Y + 1], refs[2 * Y + 1], refs[2 * Y + 2]
    cap = later[0].shape[0] // C
    back = held.shape[0] // (Z * LEVELS)
    mine = (lax.axis_index("y") * C + lax.axis_index("c")) * cap
    copies = []
    for shift in range(Y):
        for other in range(C):

            @pl.loop(0, cap, step=16)
            def _(entry):
                for k in range(16):
                    spot = lists[shift][0, other * GROUPS * cap + mine + entry + k]
                    kept[shift, other * cap + entry + k] = held[jnp.maximum(spot - back, 0)]

        copies += start_all([(kept.at[shift], later[shift])], sems, shift)
    for copy in copies:
        copy.wait()


def picks(lists, held, cap):
    def out(entries):
        return pltpu.HBM((entries, *held.shape[1:]), held.dtype)

    held = near_core(held)
    lists = [scalar_core(value) for value in lists]
    specs = [smem()] * Y + [vmem()]
    first = kernel_call(
        pick_kernel,
        SMALL,
        out_shape=out(GROUPS * cap),
        in_specs=specs,
        out_specs=hbm(),
        scratch_shapes=[
            pltpu.VMEM((GROUPS * cap, *held.shape[1:]), held.dtype),
            pltpu.SemaphoreType.DMA((GROUPS,)),
        ],
    )(*lists, held)
    later = kernel_call(
        pick_later_kernel,
        SMALL,
        out_shape=[out(C * cap)] * Y,
        in_specs=specs,
        out_specs=[hbm()] * Y,
        scratch_shapes=[
            pltpu.VMEM((Y, C * cap, *held.shape[1:]), held.dtype),
            pltpu.SemaphoreType.DMA((Y,)),
        ],
    )(*lists, held)
    return first, later


def pieces_of(spot_at, count, load):
    parts = []
    for k in range(count):
        spot = spot_at(k)
        value = load(jnp.maximum(spot, 0))
        parts.append(jnp.where(spot >= 0, value, jnp.zeros_like(value)))
    return jnp.concatenate(parts, axis=1)


def row_sum(spots, load, weights, row):
    slots, tile = weights.shape[0], weights.shape[1]
    picked = pieces_of(lambda k: spots[0, row * slots + k], slots, load)
    return jnp.dot(picked, weights[...].reshape(slots * tile, tile), preferred_element_type=jnp.float32)


def density_of(own, total, zinv):
    source = (own.astype(jnp.float32) - total).astype(jnp.bfloat16)
    return jnp.dot(source, zinv, preferred_element_type=jnp.float32).astype(jnp.bfloat16)


def start_all(pairs, sems, base=0):
    copies = [pltpu.make_async_copy(src, dst, sems.at[base + i]) for i, (src, dst) in enumerate(pairs)]
    for copy in copies:
        copy.start()
    return copies


def live_tiles(count, source, target, sems, row, act):
    slots = target.shape[0]
    for chunk in range(slots // CHUNK):
        part = pl.ds(chunk * CHUNK, CHUNK)

        @pl.when(chunk * CHUNK < count)
        def _():
            copy = pltpu.make_async_copy(source.at[part], target.at[part], sems.at[row, chunk])
            if act == "start":
                copy.start()
            else:
                copy.wait()

        if act == "start":

            @pl.when(chunk * CHUNK >= count)
            def _():
                target[part] = jnp.zeros((CHUNK, *target.shape[1:]), target.dtype)


def stage_kernel(counts, ztiles_hbm, zinv_hbm, incident_hbm, top, zinv, incident, sems, tile_sems):
    kept = top.shape[0]
    for row in range(kept):
        live_tiles(counts[row], ztiles_hbm.at[row], top.at[row], tile_sems, row, "start")
    for copy in start_all([(zinv_hbm, zinv), (incident_hbm.at[0], incident)], sems):
        copy.wait()
    for row in range(kept):
        live_tiles(counts[row], ztiles_hbm.at[row], top.at[row], tile_sems, row, "wait")


def stage(counts, ztiles, zinv, incident):
    kept = ztiles.shape[0] - 1
    return kernel_call(
        stage_kernel,
        SMALL,
        out_shape=(
            pltpu.VMEM((kept, *ztiles.shape[1:]), ztiles.dtype),
            pltpu.VMEM(zinv.shape, zinv.dtype),
            pltpu.VMEM(incident.shape[1:], incident.dtype),
        ),
        in_specs=[smem()] + [hbm()] * 3,
        out_specs=[vmem()] * 3,
        scratch_shapes=[
            pltpu.SemaphoreType.DMA((2,)),
            pltpu.SemaphoreType.DMA((kept, ztiles.shape[1] // CHUNK)),
        ],
    )(off_core(counts), off_core(ztiles), off_core(zinv), off_core(incident))


def first_kernel(spots, got, top, ztiles_hbm, zinv, incident, spread_out, last, kept_out, sems, tile_sems):
    kept, slots, tile = top.shape[0], top.shape[1], top.shape[2]
    count = spots[0, (kept + 1) * slots + kept]
    live_tiles(count, ztiles_hbm.at[kept], last, tile_sems, 0, "start")
    copies = []
    for row in range(kept + 1):
        if row == kept:
            live_tiles(count, ztiles_hbm.at[kept], last, tile_sems, 0, "wait")
        total = row_sum(spots, lambda spot: got[spot], top.at[row] if row < kept else last, row)
        density = density_of(incident[:, row * tile : (row + 1) * tile], total, zinv[row])
        for to in range(spread_out.shape[0]):
            kept_out[row, to] = density
        copies += start_all([(kept_out.at[row], spread_out.at[:, row])], sems, row)
    for copy in copies:
        copy.wait()


def first_step(spots, got, top, ztiles, zinv, incident):
    rows, slots, tile, dirs = ztiles.shape[0], ztiles.shape[1], ztiles.shape[2], got.shape[1]
    return kernel_call(
        first_kernel,
        SMALL,
        out_shape=pltpu.HBM((Y * Z, rows, dirs, tile), jnp.bfloat16),
        in_specs=[smem(), vmem(), vmem(), hbm(), vmem(), vmem()],
        out_specs=hbm(),
        scratch_shapes=[
            pltpu.VMEM(ztiles.shape[1:], ztiles.dtype),
            pltpu.VMEM((rows, Y * Z, dirs, tile), jnp.bfloat16),
            pltpu.SemaphoreType.DMA((rows,)),
            pltpu.SemaphoreType.DMA((1, slots // CHUNK)),
        ],
    )(scalar_core(spots), near_core(got), near_core(top), off_core(ztiles), near_core(zinv), near_core(incident))


def aged_kernel(spots, table, *refs):
    near, cross = refs[:Y], refs[Y : 2 * Y]
    fanned, incident_hbm, ztiles_hbm, basis_hbm, packed, fresh, basis = refs[2 * Y : 2 * Y + 7]
    pool, ztiles, before, incident, sems, tile_sems, fresh_sems = refs[2 * Y + 7 :]
    rows, slots, tile = ztiles.shape[0], ztiles.shape[1], ztiles.shape[2]
    cap = near[0].shape[0] // C
    panels = rows * tile
    counts = [spots[0, rows * slots + row] for row in range(rows)]
    pairs = []
    for shift in range(Y):
        for source, at in ((near[shift], 0), (cross[shift], cap)):
            pairs.append((source.at[pl.ds(at, cap)], pool.at[pl.ds(len(pairs) * cap, cap)]))
    copies = start_all(pairs, sems)
    for row in range(rows):
        live_tiles(counts[row], ztiles_hbm.at[row], ztiles.at[row], tile_sems, row, "start")
    pairs += [(incident_hbm.at[1], incident), (fanned.at[0], before), (basis_hbm, basis)]
    copies += start_all(pairs[2 * Y :], sems, 2 * Y)
    for copy in copies[:-1]:
        copy.wait()
    lag_one = []
    for row in range(rows):
        live_tiles(counts[row], ztiles_hbm.at[row], ztiles.at[row], tile_sems, row, "wait")
        for k in range(CHUNK):
            source = ztiles.at[row, table[0, row * slots + k]]
            lag_one.append(pltpu.make_async_copy(source, fresh.at[row, k], fresh_sems.at[row, k]))
            lag_one[-1].start()
        at = slice(row * tile, (row + 1) * tile)
        packed[0, :, at] = incident[:, at].astype(jnp.float32)
        packed[1, :, at] = row_sum(spots, lambda spot: pool[spot], ztiles.at[row], row)
    value = jnp.concatenate([before[row] for row in range(rows)], axis=1)
    packed[2, :, :] = value.astype(jnp.float32)
    copies[-1].wait()
    packed[3, :, : basis.shape[1]] = jnp.dot(value, basis[...], preferred_element_type=jnp.float32)
    packed[3, :, basis.shape[1] :] = jnp.zeros((value.shape[0], panels - basis.shape[1]), jnp.float32)
    for copy in lag_one:
        copy.wait()


def aged_step(spots, table, fanned, incident, near, cross, ztiles, basis):
    rows, dirs, tile = fanned.shape[1:]
    cap = near[0].shape[0] // C
    return kernel_call(
        aged_kernel,
        SMALL,
        out_shape=(
            pltpu.VMEM((4, dirs, rows * tile), jnp.float32),
            pltpu.VMEM((rows, CHUNK, tile, tile), ztiles.dtype),
            pltpu.VMEM(basis.shape, basis.dtype),
        ),
        in_specs=[smem(), smem()] + [anywhere()] * (2 * Y) + [hbm()] * 4,
        out_specs=[vmem()] * 3,
        scratch_shapes=[
            pltpu.VMEM((2 * Y * cap, dirs, tile), jnp.bfloat16),
            pltpu.VMEM(ztiles.shape, ztiles.dtype),
            pltpu.VMEM(fanned.shape[1:], fanned.dtype),
            pltpu.VMEM(incident.shape[1:], incident.dtype),
            pltpu.SemaphoreType.DMA((2 * Y + 3,)),
            pltpu.SemaphoreType.DMA((rows, ztiles.shape[1] // CHUNK)),
            pltpu.SemaphoreType.DMA((rows, CHUNK)),
        ],
    )(
        scalar_core(spots),
        scalar_core(table),
        *near,
        *cross,
        off_core(fanned),
        off_core(incident),
        off_core(ztiles),
        off_core(basis),
    )


def second_kernel(table, packed, fresh, zinv, basis, here, there, ztiles_hbm, dens_out, far, ztiles, flipped, dens, sems, tile_sems):
    rows, slots, tile = ztiles_hbm.shape[0], ztiles_hbm.shape[1], ztiles_hbm.shape[2]
    near = here.shape[0]

    def load(spot):
        ours = here[jnp.minimum(spot, near - 1)]
        theirs = there[jnp.maximum(spot - near, 0)]
        return jnp.where(spot < near, ours, theirs)

    later = []
    for row in range(rows):
        chunks = lax.div(table[2, row * slots] + (CHUNK - 1), CHUNK)
        at = pl.ds(row * tile, tile)
        first = pieces_of(lambda k: table[1, row * slots + k], CHUNK, load)
        total = packed[1, :, at] + jnp.dot(
            first, fresh[row].reshape(CHUNK * tile, tile), preferred_element_type=jnp.float32
        )

        def more(chunk, total):
            copies = []
            for k in range(CHUNK):
                source = ztiles_hbm.at[row, table[0, row * slots + chunk * CHUNK + k]]
                copies.append(pltpu.make_async_copy(source, ztiles.at[k], tile_sems.at[k]))
            for copy in copies:
                copy.start()
            for copy in copies:
                copy.wait()
            picked = pieces_of(lambda k: table[1, row * slots + chunk * CHUNK + k], CHUNK, load)
            return total + jnp.dot(
                picked, ztiles[...].reshape(CHUNK * tile, tile), preferred_element_type=jnp.float32
            )

        total = lax.fori_loop(1, chunks, more, total)
        later.append(density_of(packed[0, :, at], total, zinv[row]))
    value = jnp.concatenate(later, axis=1)
    dens[0] = packed[2].astype(dens.dtype)
    dens[1] = value
    copy = start_all([(dens, dens_out)], sems)[0]
    far_second = jnp.dot(value, basis[...], preferred_element_type=jnp.float32)
    both = jnp.concatenate([packed[3, :, : basis.shape[1]], far_second], axis=0)
    lanes = both.shape[0]
    flipped[:, :lanes] = both.T
    owners = far.shape[0]
    each = basis.shape[1] // owners
    cols = [flipped[pl.ds(c, owners, stride=each), :][:, :lanes] for c in range(each)]
    far[...] = jnp.concatenate([*cols, jnp.zeros((owners, far.shape[1] - each * lanes), jnp.float32)], axis=1)
    copy.wait()


def second_step(table, packed, fresh, zinv, basis, here, there, ztiles, owners):
    tile, dirs = here.shape[2], here.shape[1]
    panels, harmonics = basis.shape
    return kernel_call(
        second_kernel,
        SMALL,
        out_shape=(
            pltpu.HBM((STEPS, dirs, panels), jnp.bfloat16),
            pltpu.VMEM((owners, 128), jnp.float32),
        ),
        in_specs=[smem()] + [vmem()] * 6 + [hbm()],
        out_specs=(hbm(), vmem()),
        scratch_shapes=[
            pltpu.VMEM((CHUNK, tile, tile), ztiles.dtype),
            pltpu.VMEM((harmonics, 128), jnp.float32),
            pltpu.VMEM((STEPS, dirs, panels), jnp.bfloat16),
            pltpu.SemaphoreType.DMA((1,)),
            pltpu.SemaphoreType.DMA((CHUNK,)),
        ],
    )(
        scalar_core(table),
        near_core(packed),
        near_core(fresh),
        near_core(zinv),
        near_core(basis),
        near_core(here),
        near_core(there),
        off_core(ztiles),
    )


def sum_kernel(parts, out):
    total = jnp.sum(parts[...], axis=0, keepdims=True)
    steps, each, dirs = out.shape
    for step in range(steps):
        for c in range(each):
            at = (c * steps + step) * dirs
            out[step, c : c + 1, :] = total[:, at : at + dirs]


def sum_parts(parts, steps, each, dirs):
    return kernel_call(
        sum_kernel,
        SMALL,
        out_shape=jax.ShapeDtypeStruct((steps, each, dirs), jnp.float32),
        in_specs=[vmem()],
        out_specs=vmem(),
    )(near_core(parts))


def shifted(value, axis, length, shift):
    return lax.ppermute(value, axis, [(i, (i + shift) % length) for i in range(length)])


def march(history, incident, ztiles, zinv, columns, lags, counts, basis):
    rows, tile = ztiles.shape[0], ztiles.shape[2]
    dirs = history.shape[1]
    owners = Y * Z * C
    cap = BLOCK_CAP * Z
    held = lax.all_to_all(open_up(history, tile), "z", 0, 0, tiled=True).reshape(-1, dirs, tile)
    wanted = plan(columns, lags)
    spots, aged, table = chart(counts, columns, lags)
    both = jnp.concatenate([wanted, lax.ppermute(wanted, "c", SWAP)], axis=1)
    lists = [both] + [shifted(both, "y", Y, s) for s in range(1, Y)]
    lists = gather_lists(lists)
    first, later = picks(lists, held, cap)
    got = lax.all_to_all(first.reshape(GROUPS, cap, dirs, tile), ("y", "c"), 0, 0, tiled=True)
    near = [later[0]] + [shifted(later[s], "y", Y, -s) for s in range(1, Y)]
    cross = [lax.ppermute(piece, "c", SWAP) for piece in near]
    top, inverse, driven = stage(counts, ztiles, zinv, incident)
    fanned = first_step(spots, got.reshape(GROUPS * cap, dirs, tile), top, ztiles, inverse, driven)
    here = lax.all_to_all(fanned, ("y", "z"), 0, 0, tiled=True).reshape(Y * Z * rows, dirs, tile)
    packed, lag_one, weights = aged_step(aged, table, fanned, incident, near, cross, ztiles, basis)
    there = lax.ppermute(here, "c", SWAP)
    dens, far = second_step(table, packed, lag_one, inverse, weights, here, there, ztiles, owners)
    each = basis.shape[1] // owners
    parts = lax.all_to_all(far.reshape(owners, 1, 128), E, 0, 0, tiled=True).reshape(owners, 128)
    total = sum_parts(parts, STEPS, each, dirs)
    return dens, total.transpose(0, 2, 1)


def solution(mesh):
    fine = Mesh(mesh.devices.reshape(Y, Z, C, mesh.shape["dir"]), ("y", "z", "c", "dir"))
    in_specs = (
        P(None, "dir", E),
        P(None, "dir", E),
        P(E, None, None, None),
        P(E, None, None),
        P(E, None),
        P(E, None),
        P(E),
        P(E, None),
    )
    out_specs = (P(None, "dir", E), P(None, "dir", E))
    return jax.shard_map(march, mesh=fine, in_specs=in_specs, out_specs=out_specs, check_vma=False)
```

```python
import jax
import jax.numpy as jnp
from jax import lax
from jax.experimental import pallas as pl
from jax.experimental.pallas import tpu as pltpu
from jax.sharding import Mesh, PartitionSpec as P


STEPS = 2
LEVELS = 8
Y, Z, C = 4, 8, 2
GROUPS = Y * C
E = ("y", "z", "c")
BLOCK_CAP = 4
CHUNK = 8
SMALL = 8 << 20
SWAP = [(0, 1), (1, 0)]


def vmem():
    return pl.BlockSpec(memory_space=pltpu.VMEM)


def smem():
    return pl.BlockSpec(memory_space=pltpu.SMEM)


def hbm():
    return pl.BlockSpec(memory_space=pltpu.HBM)


def kernel_call(body, grant, **options):
    return pl.pallas_call(body, compiler_params=pltpu.CompilerParams(vmem_limit_bytes=grant), **options)


def near_core(value):
    return pltpu.with_memory_space_constraint(value, pltpu.VMEM)


def scalar_core(value):
    return pltpu.with_memory_space_constraint(value, pltpu.SMEM)


def off_core(value):
    return pltpu.with_memory_space_constraint(value, pltpu.HBM)


def turned(row):
    return jnp.broadcast_to(row, (8, row.shape[1])).T[:, :1]


def open_kernel(history, fanned, held, sems):
    rows, tile = held.shape[1], held.shape[3]
    into = start_all(
        [(history.at[:, :, pl.ds(row * tile, tile)], held.at[:, row]) for row in range(rows)], sems
    )
    for copy in into:
        copy.wait()
    for copy in start_all([(held, fanned.at[z]) for z in range(Z)], sems, rows):
        copy.wait()


def open_up(history, tile):
    levels, dirs, panels = history.shape
    rows = panels // tile
    return kernel_call(
        open_kernel,
        SMALL,
        out_shape=pltpu.HBM((Z, levels, rows, dirs, tile), history.dtype),
        in_specs=[hbm()],
        out_specs=hbm(),
        scratch_shapes=[
            pltpu.VMEM((levels, rows, dirs, tile), history.dtype),
            pltpu.SemaphoreType.DMA((rows + Z,)),
        ],
    )(off_core(history))


class Slots:
    def __init__(self, columns, lags):
        self.rows, self.count = columns.shape
        col, self.lag = columns[...], lags[...] - 1
        owner = (col * ((1 << 17) // self.rows + 1)) >> 17
        self.local = col - owner * self.rows
        self.c = lax.rem(owner, C)
        self.z = lax.rem(owner // C, Z)
        self.y = owner // (C * Z)
        group = self.y * C + self.c
        self.here = lax.broadcasted_iota(jnp.int32, (self.count, self.count), 1)
        self.there = lax.broadcasted_iota(jnp.int32, (self.count, self.count), 0)
        groups = [group[row : row + 1] for row in range(self.rows)]
        down = [turned(value) for value in groups]
        self.position = []
        for row in range(self.rows):
            same = (down[row] == groups[row]) & (self.there < self.here)
            position = jnp.sum(same.astype(jnp.int32), axis=0, keepdims=True)
            for before in range(row):
                position += jnp.sum((down[before] == groups[row]).astype(jnp.int32), axis=0, keepdims=True)
            self.position.append(position)
        self.at = [groups[row] * (BLOCK_CAP * Z) + self.position[row] for row in range(self.rows)]


def plan_kernel(columns, lags, wanted):
    slots = Slots(columns, lags)
    spot = (slots.z * LEVELS + slots.lag) * slots.rows + slots.local
    asks = lax.broadcasted_iota(jnp.int32, (slots.count, wanted.shape[1]), 1)
    total = jnp.zeros(wanted.shape, jnp.int32)
    for row in range(slots.rows):
        mine = jnp.where(turned(slots.at[row]) == asks, turned(spot[row : row + 1]), 0)
        total += jnp.sum(mine, axis=0, keepdims=True)
    wanted[...] = total


def plan(columns, lags):
    return kernel_call(
        plan_kernel,
        SMALL,
        out_shape=pltpu.VMEM((1, GROUPS * BLOCK_CAP * Z), jnp.int32),
        in_specs=[vmem(), vmem()],
        out_specs=vmem(),
    )(off_core(columns), off_core(lags))


def chart_kernel(counts, columns, lags, spots_out, aged_out, table_out, spots, aged, table, sems):
    slots = Slots(columns, lags)
    cap = BLOCK_CAP * Z
    y, c = lax.axis_index("y"), lax.axis_index("c")
    other = (slots.c != c).astype(jnp.int32)
    across = (lax.rem(slots.y - y + Y, Y) * C + other) * cap
    fresh = (other * (Y * Z) + slots.y * Z + slots.z) * slots.rows + slots.local
    lane = lax.broadcasted_iota(jnp.int32, (1, slots.count), 1)
    spot_parts, aged_parts, order_parts, where_parts, new_parts = [], [], [], [], []
    for row in range(slots.rows):
        live = lane < counts[row]
        new = live & (slots.lag[row : row + 1] == 0)
        spot_parts.append(jnp.where(live, slots.at[row], -1))
        aged_parts.append(jnp.where(live & ~new, across[row : row + 1] + slots.position[row], -1))
        fresh_row = jnp.where(new, fresh[row : row + 1], -1)
        marked = turned(new.astype(jnp.int32)) == 1
        rank = jnp.sum((marked & (slots.there < slots.here)).astype(jnp.int32), axis=0, keepdims=True)
        put = marked & (turned(rank) == slots.here)
        order_parts.append(jnp.sum(jnp.where(put, slots.there, 0), axis=0, keepdims=True))
        where_parts.append(jnp.sum(jnp.where(put, turned(fresh_row) + 1, 0), axis=0, keepdims=True) - 1)
        new_count = jnp.sum(new.astype(jnp.int32), axis=1, keepdims=True)
        new_parts.append(jnp.broadcast_to(new_count, (1, slots.count)))
    rest = jnp.zeros((1, spots.shape[1] - slots.rows * slots.count), jnp.int32)
    tail = rest
    for row in range(slots.rows):
        tail = jnp.where(lax.broadcasted_iota(jnp.int32, rest.shape, 1) == row, counts[row], tail)
    spots[...] = jnp.concatenate([*spot_parts, tail], axis=1)
    aged[...] = jnp.concatenate([*aged_parts, tail], axis=1)
    table[0:1, :] = jnp.concatenate([*order_parts, rest], axis=1)
    table[1:2, :] = jnp.concatenate([*where_parts, rest], axis=1)
    table[2:3, :] = jnp.concatenate([*new_parts, rest], axis=1)
    for copy in start_all([(spots, spots_out), (aged, aged_out), (table, table_out)], sems):
        copy.wait()


def chart(counts, columns, lags):
    lengths = (1, 1, 3)
    return kernel_call(
        chart_kernel,
        SMALL,
        out_shape=tuple(pltpu.SMEM((length, 128), jnp.int32) for length in lengths),
        in_specs=[smem(), vmem(), vmem()],
        out_specs=[smem()] * 3,
        scratch_shapes=[pltpu.VMEM((length, 128), jnp.int32) for length in lengths]
        + [pltpu.SemaphoreType.DMA((3,))],
    )(off_core(counts), off_core(columns), off_core(lags))


def gather_lists_kernel(*refs):
    for copy in start_all(list(zip(refs[:Y], refs[Y : 2 * Y])), refs[2 * Y]):
        copy.wait()


def gather_lists(lists):
    return kernel_call(
        gather_lists_kernel,
        SMALL,
        out_shape=tuple(pltpu.SMEM(value.shape, value.dtype) for value in lists),
        in_specs=[vmem()] * Y,
        out_specs=[smem()] * Y,
        scratch_shapes=[pltpu.SemaphoreType.DMA((Y,))],
    )(*[near_core(value) for value in lists])


def whose(shift, other):
    y, c = lax.axis_index("y"), lax.axis_index("c")
    return lax.rem(y - shift + Y, Y) * C + (c if other == 0 else 1 - c)


def pick_kernel(*refs):
    lists, held, first, kept, sems = refs[:Y], refs[Y], refs[Y + 1], refs[Y + 2], refs[Y + 3]
    cap = first.shape[0] // GROUPS
    mine = (lax.axis_index("y") * C + lax.axis_index("c")) * cap
    copies = []
    for shift in range(Y):
        for other in range(C):
            base = len(copies) * cap

            @pl.loop(0, cap, step=16)
            def _(entry):
                for k in range(16):
                    spot = lists[shift][0, other * GROUPS * cap + mine + entry + k]
                    kept[base + entry + k] = held[spot]

            to = whose(shift, other) * cap
            pair = (kept.at[pl.ds(base, cap)], first.at[pl.ds(to, cap)])
            copies += start_all([pair], sems, len(copies))
    for copy in copies:
        copy.wait()


def pick_later_kernel(*refs):
    lists, held, later, kept, sems = refs[:Y], refs[Y], refs[Y + 1 : 2 * Y + 1], refs[2 * Y + 1], refs[2 * Y + 2]
    cap = later[0].shape[0] // C
    back = held.shape[0] // (Z * LEVELS)
    mine = (lax.axis_index("y") * C + lax.axis_index("c")) * cap
    copies = []
    for shift in range(Y):
        for other in range(C):

            @pl.loop(0, cap, step=16)
            def _(entry):
                for k in range(16):
                    spot = lists[shift][0, other * GROUPS * cap + mine + entry + k]
                    kept[shift, other * cap + entry + k] = held[jnp.maximum(spot - back, 0)]

        copies += start_all([(kept.at[shift], later[shift])], sems, shift)
    for copy in copies:
        copy.wait()


def picks(lists, held, cap):
    def out(entries):
        return pltpu.HBM((entries, *held.shape[1:]), held.dtype)

    held = near_core(held)
    lists = [scalar_core(value) for value in lists]
    specs = [smem()] * Y + [vmem()]
    first = kernel_call(
        pick_kernel,
        SMALL,
        out_shape=out(GROUPS * cap),
        in_specs=specs,
        out_specs=hbm(),
        scratch_shapes=[
            pltpu.VMEM((GROUPS * cap, *held.shape[1:]), held.dtype),
            pltpu.SemaphoreType.DMA((GROUPS,)),
        ],
    )(*lists, held)
    later = kernel_call(
        pick_later_kernel,
        SMALL,
        out_shape=[out(C * cap)] * Y,
        in_specs=specs,
        out_specs=[hbm()] * Y,
        scratch_shapes=[
            pltpu.VMEM((Y, C * cap, *held.shape[1:]), held.dtype),
            pltpu.SemaphoreType.DMA((Y,)),
        ],
    )(*lists, held)
    return first, later


def pieces_of(spot_at, count, load):
    parts = []
    for k in range(count):
        spot = spot_at(k)
        value = load(jnp.maximum(spot, 0))
        parts.append(jnp.where(spot >= 0, value, jnp.zeros_like(value)))
    return jnp.concatenate(parts, axis=1)


def row_sum(spots, load, weights, row):
    slots, tile = weights.shape[0], weights.shape[1]
    picked = pieces_of(lambda k: spots[0, row * slots + k], slots, load)
    return jnp.dot(picked, weights[...].reshape(slots * tile, tile), preferred_element_type=jnp.float32)


def density_of(own, total, zinv):
    source = (own.astype(jnp.float32) - total).astype(jnp.bfloat16)
    return jnp.dot(source, zinv, preferred_element_type=jnp.float32).astype(jnp.bfloat16)


def start_all(pairs, sems, base=0):
    copies = [pltpu.make_async_copy(src, dst, sems.at[base + i]) for i, (src, dst) in enumerate(pairs)]
    for copy in copies:
        copy.start()
    return copies


def live_tiles(count, source, target, sems, row, act):
    slots = target.shape[0]
    for chunk in range(slots // CHUNK):
        part = pl.ds(chunk * CHUNK, CHUNK)

        @pl.when(chunk * CHUNK < count)
        def _():
            copy = pltpu.make_async_copy(source.at[part], target.at[part], sems.at[row, chunk])
            if act == "start":
                copy.start()
            else:
                copy.wait()

        if act == "start":

            @pl.when(chunk * CHUNK >= count)
            def _():
                target[part] = jnp.zeros((CHUNK, *target.shape[1:]), target.dtype)


def stage_kernel(counts, ztiles_hbm, zinv_hbm, incident_hbm, top, zinv, incident, sems, tile_sems):
    kept = top.shape[0]
    for row in range(kept):
        live_tiles(counts[row], ztiles_hbm.at[row], top.at[row], tile_sems, row, "start")
    for copy in start_all([(zinv_hbm, zinv), (incident_hbm.at[0], incident)], sems):
        copy.wait()
    for row in range(kept):
        live_tiles(counts[row], ztiles_hbm.at[row], top.at[row], tile_sems, row, "wait")


def stage(counts, ztiles, zinv, incident):
    kept = ztiles.shape[0] - 1
    return kernel_call(
        stage_kernel,
        SMALL,
        out_shape=(
            pltpu.VMEM((kept, *ztiles.shape[1:]), ztiles.dtype),
            pltpu.VMEM(zinv.shape, zinv.dtype),
            pltpu.VMEM(incident.shape[1:], incident.dtype),
        ),
        in_specs=[smem()] + [hbm()] * 3,
        out_specs=[vmem()] * 3,
        scratch_shapes=[
            pltpu.SemaphoreType.DMA((2,)),
            pltpu.SemaphoreType.DMA((kept, ztiles.shape[1] // CHUNK)),
        ],
    )(off_core(counts), off_core(ztiles), off_core(zinv), off_core(incident))


def first_kernel(spots, got, top, ztiles_hbm, zinv, incident, spread_out, last, kept_out, sems, tile_sems):
    kept, slots, tile = top.shape[0], top.shape[1], top.shape[2]
    count = spots[0, (kept + 1) * slots + kept]
    live_tiles(count, ztiles_hbm.at[kept], last, tile_sems, 0, "start")
    copies = []
    for row in range(kept + 1):
        if row == kept:
            live_tiles(count, ztiles_hbm.at[kept], last, tile_sems, 0, "wait")
        total = row_sum(spots, lambda spot: got[spot], top.at[row] if row < kept else last, row)
        density = density_of(incident[:, row * tile : (row + 1) * tile], total, zinv[row])
        for to in range(spread_out.shape[0]):
            kept_out[row, to] = density
        copies += start_all([(kept_out.at[row], spread_out.at[:, row])], sems, row)
    for copy in copies:
        copy.wait()


def first_step(spots, got, top, ztiles, zinv, incident):
    rows, slots, tile, dirs = ztiles.shape[0], ztiles.shape[1], ztiles.shape[2], got.shape[1]
    return kernel_call(
        first_kernel,
        SMALL,
        out_shape=pltpu.HBM((Y * Z, rows, dirs, tile), jnp.bfloat16),
        in_specs=[smem(), vmem(), vmem(), hbm(), vmem(), vmem()],
        out_specs=hbm(),
        scratch_shapes=[
            pltpu.VMEM(ztiles.shape[1:], ztiles.dtype),
            pltpu.VMEM((rows, Y * Z, dirs, tile), jnp.bfloat16),
            pltpu.SemaphoreType.DMA((rows,)),
            pltpu.SemaphoreType.DMA((1, slots // CHUNK)),
        ],
    )(scalar_core(spots), near_core(got), near_core(top), off_core(ztiles), near_core(zinv), near_core(incident))


def aged_kernel(spots, table, *refs):
    near, cross = refs[:Y], refs[Y : 2 * Y]
    fanned, incident_hbm, ztiles_hbm, basis_hbm, packed, fresh, basis = refs[2 * Y : 2 * Y + 7]
    pool, ztiles, before, incident, sems, tile_sems = refs[2 * Y + 7 :]
    rows, slots, tile = ztiles.shape[0], ztiles.shape[1], ztiles.shape[2]
    cap = near[0].shape[0] // C
    panels = rows * tile
    counts = [spots[0, rows * slots + row] for row in range(rows)]
    for row in range(rows):
        live_tiles(counts[row], ztiles_hbm.at[row], ztiles.at[row], tile_sems, row, "start")
    copies = start_all([(incident_hbm.at[1], incident), (fanned.at[0], before), (basis_hbm, basis)], sems)
    for shift in range(Y):
        for other, source in enumerate((near[shift], cross[shift])):
            pool[pl.ds((shift * C + other) * cap, cap)] = source[pl.ds(other * cap, cap)]
    for row in range(rows):
        live_tiles(counts[row], ztiles_hbm.at[row], ztiles.at[row], tile_sems, row, "wait")
        for k in range(CHUNK):
            fresh[row, k] = ztiles[row, table[0, row * slots + k]]
        at = slice(row * tile, (row + 1) * tile)
        packed[1, :, at] = row_sum(spots, lambda spot: pool[spot], ztiles.at[row], row)
    for copy in copies:
        copy.wait()
    packed[0, :, :] = incident[...].astype(jnp.float32)
    value = jnp.concatenate([before[row] for row in range(rows)], axis=1)
    packed[2, :, :] = value.astype(jnp.float32)
    packed[3, :, : basis.shape[1]] = jnp.dot(value, basis[...], preferred_element_type=jnp.float32)
    packed[3, :, basis.shape[1] :] = jnp.zeros((value.shape[0], panels - basis.shape[1]), jnp.float32)


def aged_step(spots, table, fanned, incident, near, cross, ztiles, basis):
    rows, dirs, tile = fanned.shape[1:]
    cap = near[0].shape[0] // C
    return kernel_call(
        aged_kernel,
        SMALL,
        out_shape=(
            pltpu.VMEM((4, dirs, rows * tile), jnp.float32),
            pltpu.VMEM((rows, CHUNK, tile, tile), ztiles.dtype),
            pltpu.VMEM(basis.shape, basis.dtype),
        ),
        in_specs=[smem(), smem()] + [vmem()] * (2 * Y) + [hbm()] * 4,
        out_specs=[vmem()] * 3,
        scratch_shapes=[
            pltpu.VMEM((2 * Y * cap, dirs, tile), jnp.bfloat16),
            pltpu.VMEM(ztiles.shape, ztiles.dtype),
            pltpu.VMEM(fanned.shape[1:], fanned.dtype),
            pltpu.VMEM(incident.shape[1:], incident.dtype),
            pltpu.SemaphoreType.DMA((3,)),
            pltpu.SemaphoreType.DMA((rows, ztiles.shape[1] // CHUNK)),
        ],
    )(
        scalar_core(spots),
        scalar_core(table),
        *[near_core(piece) for piece in (*near, *cross)],
        off_core(fanned),
        off_core(incident),
        off_core(ztiles),
        off_core(basis),
    )


def second_kernel(table, packed, fresh, zinv, basis, here, there, ztiles_hbm, dens_out, far, ztiles, flipped, dens, sems, tile_sems):
    rows, slots, tile = ztiles_hbm.shape[0], ztiles_hbm.shape[1], ztiles_hbm.shape[2]
    near = here.shape[0]

    def load(spot):
        ours = here[jnp.minimum(spot, near - 1)]
        theirs = there[jnp.maximum(spot - near, 0)]
        return jnp.where(spot < near, ours, theirs)

    later = []
    for row in range(rows):
        chunks = lax.div(table[2, row * slots] + (CHUNK - 1), CHUNK)
        at = pl.ds(row * tile, tile)
        first = pieces_of(lambda k: table[1, row * slots + k], CHUNK, load)
        total = packed[1, :, at] + jnp.dot(
            first, fresh[row].reshape(CHUNK * tile, tile), preferred_element_type=jnp.float32
        )

        def more(chunk, total):
            copies = []
            for k in range(CHUNK):
                source = ztiles_hbm.at[row, table[0, row * slots + chunk * CHUNK + k]]
                copies.append(pltpu.make_async_copy(source, ztiles.at[k], tile_sems.at[k]))
            for copy in copies:
                copy.start()
            for copy in copies:
                copy.wait()
            picked = pieces_of(lambda k: table[1, row * slots + chunk * CHUNK + k], CHUNK, load)
            return total + jnp.dot(
                picked, ztiles[...].reshape(CHUNK * tile, tile), preferred_element_type=jnp.float32
            )

        total = lax.fori_loop(1, chunks, more, total)
        later.append(density_of(packed[0, :, at], total, zinv[row]))
    value = jnp.concatenate(later, axis=1)
    dens[0] = packed[2].astype(dens.dtype)
    dens[1] = value
    copy = start_all([(dens, dens_out)], sems)[0]
    far_second = jnp.dot(value, basis[...], preferred_element_type=jnp.float32)
    both = jnp.concatenate([packed[3, :, : basis.shape[1]], far_second], axis=0)
    lanes = both.shape[0]
    flipped[:, :lanes] = both.T
    owners = far.shape[0]
    each = basis.shape[1] // owners
    cols = [flipped[pl.ds(c, owners, stride=each), :][:, :lanes] for c in range(each)]
    far[...] = jnp.concatenate([*cols, jnp.zeros((owners, far.shape[1] - each * lanes), jnp.float32)], axis=1)
    copy.wait()


def second_step(table, packed, fresh, zinv, basis, here, there, ztiles, owners):
    tile, dirs = here.shape[2], here.shape[1]
    panels, harmonics = basis.shape
    return kernel_call(
        second_kernel,
        SMALL,
        out_shape=(
            pltpu.HBM((STEPS, dirs, panels), jnp.bfloat16),
            pltpu.VMEM((owners, 128), jnp.float32),
        ),
        in_specs=[smem()] + [vmem()] * 6 + [hbm()],
        out_specs=(hbm(), vmem()),
        scratch_shapes=[
            pltpu.VMEM((CHUNK, tile, tile), ztiles.dtype),
            pltpu.VMEM((harmonics, 128), jnp.float32),
            pltpu.VMEM((STEPS, dirs, panels), jnp.bfloat16),
            pltpu.SemaphoreType.DMA((1,)),
            pltpu.SemaphoreType.DMA((CHUNK,)),
        ],
    )(
        scalar_core(table),
        near_core(packed),
        near_core(fresh),
        near_core(zinv),
        near_core(basis),
        near_core(here),
        near_core(there),
        off_core(ztiles),
    )


def sum_kernel(parts, out):
    total = jnp.sum(parts[...], axis=0, keepdims=True)
    steps, each, dirs = out.shape
    for step in range(steps):
        for c in range(each):
            at = (c * steps + step) * dirs
            out[step, c : c + 1, :] = total[:, at : at + dirs]


def sum_parts(parts, steps, each, dirs):
    return kernel_call(
        sum_kernel,
        SMALL,
        out_shape=jax.ShapeDtypeStruct((steps, each, dirs), jnp.float32),
        in_specs=[vmem()],
        out_specs=vmem(),
    )(near_core(parts))


def shifted(value, axis, length, shift):
    return lax.ppermute(value, axis, [(i, (i + shift) % length) for i in range(length)])


def march(history, incident, ztiles, zinv, columns, lags, counts, basis):
    rows, tile = ztiles.shape[0], ztiles.shape[2]
    dirs = history.shape[1]
    owners = Y * Z * C
    cap = BLOCK_CAP * Z
    held = lax.all_to_all(open_up(history, tile), "z", 0, 0, tiled=True).reshape(-1, dirs, tile)
    wanted = plan(columns, lags)
    spots, aged, table = chart(counts, columns, lags)
    both = jnp.concatenate([wanted, lax.ppermute(wanted, "c", SWAP)], axis=1)
    lists = [both] + [shifted(both, "y", Y, s) for s in range(1, Y)]
    lists = gather_lists(lists)
    first, later = picks(lists, held, cap)
    got = lax.all_to_all(first.reshape(GROUPS, cap, dirs, tile), ("y", "c"), 0, 0, tiled=True)
    near = [later[0]] + [shifted(later[s], "y", Y, -s) for s in range(1, Y)]
    cross = [lax.ppermute(piece, "c", SWAP) for piece in near]
    top, inverse, driven = stage(counts, ztiles, zinv, incident)
    fanned = first_step(spots, got.reshape(GROUPS * cap, dirs, tile), top, ztiles, inverse, driven)
    here = lax.all_to_all(fanned, ("y", "z"), 0, 0, tiled=True).reshape(Y * Z * rows, dirs, tile)
    packed, lag_one, weights = aged_step(aged, table, fanned, incident, near, cross, ztiles, basis)
    there = lax.ppermute(here, "c", SWAP)
    dens, far = second_step(table, packed, lag_one, inverse, weights, here, there, ztiles, owners)
    each = basis.shape[1] // owners
    parts = lax.all_to_all(far.reshape(owners, 1, 128), E, 0, 0, tiled=True).reshape(owners, 128)
    total = sum_parts(parts, STEPS, each, dirs)
    return dens, total.transpose(0, 2, 1)


def solution(mesh):
    fine = Mesh(mesh.devices.reshape(Y, Z, C, mesh.shape["dir"]), ("y", "z", "c", "dir"))
    in_specs = (
        P(None, "dir", E),
        P(None, "dir", E),
        P(E, None, None, None),
        P(E, None, None),
        P(E, None),
        P(E, None),
        P(E),
        P(E, None),
    )
    out_specs = (P(None, "dir", E), P(None, "dir", E))
    return jax.shard_map(march, mesh=fine, in_specs=in_specs, out_specs=out_specs, check_vma=False)
```

```python
import jax
import jax.numpy as jnp
from jax import lax
from jax.experimental import pallas as pl
from jax.experimental.pallas import tpu as pltpu
from jax.sharding import Mesh, PartitionSpec as P


STEPS = 2
LEVELS = 8
Y, Z, C = 4, 8, 2
GROUPS = Y * C
E = ("y", "z", "c")
BLOCK_CAP = 4
CHUNK = 8
FETCHED = 8
SMALL = 8 << 20
SWAP = [(0, 1), (1, 0)]


def vmem():
    return pl.BlockSpec(memory_space=pltpu.VMEM)


def smem():
    return pl.BlockSpec(memory_space=pltpu.SMEM)


def hbm():
    return pl.BlockSpec(memory_space=pltpu.HBM)


def kernel_call(body, grant, **options):
    return pl.pallas_call(body, compiler_params=pltpu.CompilerParams(vmem_limit_bytes=grant), **options)


def near_core(value):
    return pltpu.with_memory_space_constraint(value, pltpu.VMEM)


def scalar_core(value):
    return pltpu.with_memory_space_constraint(value, pltpu.SMEM)


def off_core(value):
    return pltpu.with_memory_space_constraint(value, pltpu.HBM)


def turned(row):
    return jnp.broadcast_to(row, (8, row.shape[1])).T[:, :1]


def open_kernel(history, columns_hbm, lags_hbm, fanned, wanted, held, columns, lags, sems):
    rows, tile = held.shape[1], held.shape[3]
    pairs = [(history.at[:, :, pl.ds(row * tile, tile)], held.at[:, row]) for row in range(rows)]
    into = start_all([*pairs, (columns_hbm, columns), (lags_hbm, lags)], sems)
    for copy in into:
        copy.wait()
    out = start_all([(held, fanned.at[z]) for z in range(Z)], sems, len(into))
    slots = Slots(columns, lags)
    spot = (slots.z * LEVELS + slots.lag) * slots.rows + slots.local
    asks = lax.broadcasted_iota(jnp.int32, (slots.count, wanted.shape[1]), 1)
    total = jnp.zeros(wanted.shape, jnp.int32)
    for row in range(slots.rows):
        mine = jnp.where(turned(slots.at[row]) == asks, turned(spot[row : row + 1]), 0)
        total += jnp.sum(mine, axis=0, keepdims=True)
    wanted[...] = total
    for copy in out:
        copy.wait()


def open_up(history, columns, lags, tile):
    levels, dirs, panels = history.shape
    rows = panels // tile
    return kernel_call(
        open_kernel,
        SMALL,
        out_shape=(
            pltpu.HBM((Z, levels, rows, dirs, tile), history.dtype),
            pltpu.VMEM((1, GROUPS * BLOCK_CAP * Z), jnp.int32),
        ),
        in_specs=[hbm()] * 3,
        out_specs=(hbm(), vmem()),
        scratch_shapes=[
            pltpu.VMEM((levels, rows, dirs, tile), history.dtype),
            pltpu.VMEM(columns.shape, columns.dtype),
            pltpu.VMEM(lags.shape, lags.dtype),
            pltpu.SemaphoreType.DMA((rows + 2 + Z,)),
        ],
    )(off_core(history), off_core(columns), off_core(lags))


class Slots:
    def __init__(self, columns, lags):
        self.rows, self.count = columns.shape
        col, self.lag = columns[...], lags[...] - 1
        owner = (col * ((1 << 17) // self.rows + 1)) >> 17
        self.local = col - owner * self.rows
        self.c = lax.rem(owner, C)
        self.z = lax.rem(owner // C, Z)
        self.y = owner // (C * Z)
        group = self.y * C + self.c
        self.here = lax.broadcasted_iota(jnp.int32, (self.count, self.count), 1)
        self.there = lax.broadcasted_iota(jnp.int32, (self.count, self.count), 0)
        groups = [group[row : row + 1] for row in range(self.rows)]
        down = [turned(value) for value in groups]
        self.position = []
        for row in range(self.rows):
            same = (down[row] == groups[row]) & (self.there < self.here)
            position = jnp.sum(same.astype(jnp.int32), axis=0, keepdims=True)
            for before in range(row):
                position += jnp.sum((down[before] == groups[row]).astype(jnp.int32), axis=0, keepdims=True)
            self.position.append(position)
        self.at = [groups[row] * (BLOCK_CAP * Z) + self.position[row] for row in range(self.rows)]


def chart_kernel(counts, columns, lags, spots_out, aged_out, table_out, spots, aged, table, sems):
    slots = Slots(columns, lags)
    cap = BLOCK_CAP * Z
    y, c = lax.axis_index("y"), lax.axis_index("c")
    other = (slots.c != c).astype(jnp.int32)
    across = (lax.rem(slots.y - y + Y, Y) * C + other) * cap
    fresh = (other * (Y * Z) + slots.y * Z + slots.z) * slots.rows + slots.local
    lane = lax.broadcasted_iota(jnp.int32, (1, slots.count), 1)
    spot_parts, aged_parts, order_parts, where_parts, new_parts = [], [], [], [], []
    for row in range(slots.rows):
        live = lane < counts[row]
        new = live & (slots.lag[row : row + 1] == 0)
        spot_parts.append(jnp.where(live, slots.at[row], -1))
        aged_parts.append(jnp.where(live & ~new, across[row : row + 1] + slots.position[row], -1))
        fresh_row = jnp.where(new, fresh[row : row + 1], -1)
        marked = turned(new.astype(jnp.int32)) == 1
        rank = jnp.sum((marked & (slots.there < slots.here)).astype(jnp.int32), axis=0, keepdims=True)
        put = marked & (turned(rank) == slots.here)
        order_parts.append(jnp.sum(jnp.where(put, slots.there, 0), axis=0, keepdims=True))
        where_parts.append(jnp.sum(jnp.where(put, turned(fresh_row) + 1, 0), axis=0, keepdims=True) - 1)
        new_count = jnp.sum(new.astype(jnp.int32), axis=1, keepdims=True)
        new_parts.append(jnp.broadcast_to(new_count, (1, slots.count)))
    rest = jnp.zeros((1, spots.shape[1] - slots.rows * slots.count), jnp.int32)
    tail = rest
    for row in range(slots.rows):
        tail = jnp.where(lax.broadcasted_iota(jnp.int32, rest.shape, 1) == row, counts[row], tail)
    spots[...] = jnp.concatenate([*spot_parts, tail], axis=1)
    aged[...] = jnp.concatenate([*aged_parts, tail], axis=1)
    table[0:1, :] = jnp.concatenate([*order_parts, rest], axis=1)
    table[1:2, :] = jnp.concatenate([*where_parts, rest], axis=1)
    table[2:3, :] = jnp.concatenate([*new_parts, rest], axis=1)
    for copy in start_all([(spots, spots_out), (aged, aged_out), (table, table_out)], sems):
        copy.wait()


def chart(counts, columns, lags):
    lengths = (1, 1, 3)
    return kernel_call(
        chart_kernel,
        SMALL,
        out_shape=tuple(pltpu.SMEM((length, 128), jnp.int32) for length in lengths),
        in_specs=[smem(), vmem(), vmem()],
        out_specs=[smem()] * 3,
        scratch_shapes=[pltpu.VMEM((length, 128), jnp.int32) for length in lengths]
        + [pltpu.SemaphoreType.DMA((3,))],
    )(off_core(counts), off_core(columns), off_core(lags))


def gather_lists_kernel(*refs):
    for copy in start_all(list(zip(refs[:Y], refs[Y : 2 * Y])), refs[2 * Y]):
        copy.wait()


def gather_lists(lists):
    return kernel_call(
        gather_lists_kernel,
        SMALL,
        out_shape=tuple(pltpu.SMEM(value.shape, value.dtype) for value in lists),
        in_specs=[vmem()] * Y,
        out_specs=[smem()] * Y,
        scratch_shapes=[pltpu.SemaphoreType.DMA((Y,))],
    )(*[near_core(value) for value in lists])


def whose(shift, other):
    y, c = lax.axis_index("y"), lax.axis_index("c")
    return lax.rem(y - shift + Y, Y) * C + (c if other == 0 else 1 - c)


def pick_kernel(*refs):
    lists, held, first, kept, sems = refs[:Y], refs[Y], refs[Y + 1], refs[Y + 2], refs[Y + 3]
    cap = first.shape[0] // GROUPS
    mine = (lax.axis_index("y") * C + lax.axis_index("c")) * cap
    copies = []
    for shift in range(Y):
        for other in range(C):
            base = len(copies) * cap

            @pl.loop(0, cap, step=16)
            def _(entry):
                for k in range(16):
                    spot = lists[shift][0, other * GROUPS * cap + mine + entry + k]
                    kept[base + entry + k] = held[spot]

            to = whose(shift, other) * cap
            pair = (kept.at[pl.ds(base, cap)], first.at[pl.ds(to, cap)])
            copies += start_all([pair], sems, len(copies))
    for copy in copies:
        copy.wait()


def pick_later_kernel(*refs):
    lists, held, later, kept, sems = refs[:Y], refs[Y], refs[Y + 1 : 2 * Y + 1], refs[2 * Y + 1], refs[2 * Y + 2]
    cap = later[0].shape[0] // C
    back = held.shape[0] // (Z * LEVELS)
    mine = (lax.axis_index("y") * C + lax.axis_index("c")) * cap
    copies = []
    for shift in range(Y):
        for other in range(C):

            @pl.loop(0, cap, step=16)
            def _(entry):
                for k in range(16):
                    spot = lists[shift][0, other * GROUPS * cap + mine + entry + k]
                    kept[shift, other * cap + entry + k] = held[jnp.maximum(spot - back, 0)]

        copies += start_all([(kept.at[shift], later[shift])], sems, shift)
    for copy in copies:
        copy.wait()


def picks(lists, held, cap):
    def out(entries):
        return pltpu.HBM((entries, *held.shape[1:]), held.dtype)

    held = near_core(held)
    lists = [scalar_core(value) for value in lists]
    specs = [smem()] * Y + [vmem()]
    first = kernel_call(
        pick_kernel,
        SMALL,
        out_shape=out(GROUPS * cap),
        in_specs=specs,
        out_specs=hbm(),
        scratch_shapes=[
            pltpu.VMEM((GROUPS * cap, *held.shape[1:]), held.dtype),
            pltpu.SemaphoreType.DMA((GROUPS,)),
        ],
    )(*lists, held)
    later = kernel_call(
        pick_later_kernel,
        SMALL,
        out_shape=[out(C * cap)] * Y,
        in_specs=specs,
        out_specs=[hbm()] * Y,
        scratch_shapes=[
            pltpu.VMEM((Y, C * cap, *held.shape[1:]), held.dtype),
            pltpu.SemaphoreType.DMA((Y,)),
        ],
    )(*lists, held)
    return first, later


def pieces_of(spot_at, count, load):
    parts = []
    for k in range(count):
        spot = spot_at(k)
        value = load(jnp.maximum(spot, 0))
        parts.append(jnp.where(spot >= 0, value, jnp.zeros_like(value)))
    return jnp.concatenate(parts, axis=1)


def row_sum(spots, load, weights, base):
    slots, tile = weights.shape[0], weights.shape[1]
    picked = pieces_of(lambda k: spots[0, base + k], slots, load)
    return jnp.dot(picked, weights[...].reshape(slots * tile, tile), preferred_element_type=jnp.float32)


def density_of(own, total, zinv):
    source = (own.astype(jnp.float32) - total).astype(jnp.bfloat16)
    return jnp.dot(source, zinv, preferred_element_type=jnp.float32).astype(jnp.bfloat16)


def start_all(pairs, sems, base=0):
    copies = [pltpu.make_async_copy(src, dst, sems.at[base + i]) for i, (src, dst) in enumerate(pairs)]
    for copy in copies:
        copy.start()
    return copies


def live_tiles(count, source, target, sems, row, act):
    slots = target.shape[0]
    for chunk in range(slots // CHUNK):
        part = pl.ds(chunk * CHUNK, CHUNK)

        @pl.when(chunk * CHUNK < count)
        def _():
            copy = pltpu.make_async_copy(source.at[part], target.at[part], sems.at[row, chunk])
            if act == "start":
                copy.start()
            else:
                copy.wait()

        if act == "start":

            @pl.when(chunk * CHUNK >= count)
            def _():
                target[part] = jnp.zeros((CHUNK, *target.shape[1:]), target.dtype)


def staged_rows(counts, ztiles_hbm, top, sems, act):
    slots = ztiles_hbm.shape[1]
    for row in range(ztiles_hbm.shape[0]):
        length = min(slots, top.shape[0] - row * slots)
        if length > 0:
            target = top.at[pl.ds(row * slots, length)]
            live_tiles(counts[row], ztiles_hbm.at[row, pl.ds(0, length)], target, sems, row, act)


def stage_kernel(counts, ztiles_hbm, zinv_hbm, incident_hbm, top, zinv, incident, sems, tile_sems):
    staged_rows(counts, ztiles_hbm, top, tile_sems, "start")
    for copy in start_all([(zinv_hbm, zinv), (incident_hbm.at[0], incident)], sems):
        copy.wait()
    staged_rows(counts, ztiles_hbm, top, tile_sems, "wait")


def stage(counts, ztiles, zinv, incident):
    rows, slots, tile = ztiles.shape[0], ztiles.shape[1], ztiles.shape[2]
    return kernel_call(
        stage_kernel,
        SMALL,
        out_shape=(
            pltpu.VMEM((rows * slots - FETCHED, tile, tile), ztiles.dtype),
            pltpu.VMEM(zinv.shape, zinv.dtype),
            pltpu.VMEM(incident.shape[1:], incident.dtype),
        ),
        in_specs=[smem()] + [hbm()] * 3,
        out_specs=[vmem()] * 3,
        scratch_shapes=[
            pltpu.SemaphoreType.DMA((2,)),
            pltpu.SemaphoreType.DMA((rows, slots // CHUNK)),
        ],
    )(off_core(counts), off_core(ztiles), off_core(zinv), off_core(incident))


def first_kernel(spots, got, top, ztiles_hbm, zinv, incident, spread_out, last, kept_out, sems, tile_sems):
    rows, slots, tile = ztiles_hbm.shape[0], ztiles_hbm.shape[1], ztiles_hbm.shape[2]
    begin = slots - last.shape[0]
    rest = ztiles_hbm.at[rows - 1, pl.ds(begin, last.shape[0])]
    count = spots[0, rows * slots + rows - 1] - begin
    live_tiles(count, rest, last, tile_sems, 0, "start")
    copies = []
    for row in range(rows):
        length = slots if row < rows - 1 else begin
        weights = top.at[pl.ds(row * slots, length)]
        total = row_sum(spots, lambda spot: got[spot], weights, row * slots)
        if row == rows - 1:
            live_tiles(count, rest, last, tile_sems, 0, "wait")
            total += row_sum(spots, lambda spot: got[spot], last, row * slots + begin)
        density = density_of(incident[:, row * tile : (row + 1) * tile], total, zinv[row])
        for to in range(spread_out.shape[0]):
            kept_out[row, to] = density
        copies += start_all([(kept_out.at[row], spread_out.at[:, row])], sems, row)
    for copy in copies:
        copy.wait()


def first_step(spots, got, top, ztiles, zinv, incident):
    rows, tile, dirs = ztiles.shape[0], ztiles.shape[2], got.shape[1]
    return kernel_call(
        first_kernel,
        SMALL,
        out_shape=pltpu.HBM((Y * Z, rows, dirs, tile), jnp.bfloat16),
        in_specs=[smem(), vmem(), vmem(), hbm(), vmem(), vmem()],
        out_specs=hbm(),
        scratch_shapes=[
            pltpu.VMEM((FETCHED, tile, tile), ztiles.dtype),
            pltpu.VMEM((rows, Y * Z, dirs, tile), jnp.bfloat16),
            pltpu.SemaphoreType.DMA((rows,)),
            pltpu.SemaphoreType.DMA((1, FETCHED // CHUNK)),
        ],
    )(scalar_core(spots), near_core(got), near_core(top), off_core(ztiles), near_core(zinv), near_core(incident))


def aged_kernel(spots, table, *refs):
    near, cross = refs[:Y], refs[Y : 2 * Y]
    fanned, incident_hbm, ztiles_hbm, basis_hbm, packed, fresh, basis = refs[2 * Y : 2 * Y + 7]
    pool, ztiles, before, incident, sems, tile_sems = refs[2 * Y + 7 :]
    rows, slots, tile = ztiles.shape[0], ztiles.shape[1], ztiles.shape[2]
    cap = near[0].shape[0] // C
    panels = rows * tile
    counts = [spots[0, rows * slots + row] for row in range(rows)]
    for row in range(rows):
        live_tiles(counts[row], ztiles_hbm.at[row], ztiles.at[row], tile_sems, row, "start")
    copies = start_all([(incident_hbm.at[1], incident), (fanned.at[0], before), (basis_hbm, basis)], sems)
    for shift in range(Y):
        for other, source in enumerate((near[shift], cross[shift])):
            pool[pl.ds((shift * C + other) * cap, cap)] = source[pl.ds(other * cap, cap)]
    for row in range(rows):
        live_tiles(counts[row], ztiles_hbm.at[row], ztiles.at[row], tile_sems, row, "wait")
        for k in range(CHUNK):
            fresh[row, k] = ztiles[row, table[0, row * slots + k]]
        at = slice(row * tile, (row + 1) * tile)
        packed[1, :, at] = row_sum(spots, lambda spot: pool[spot], ztiles.at[row], row * slots)
    for copy in copies:
        copy.wait()
    packed[0, :, :] = incident[...].astype(jnp.float32)
    value = jnp.concatenate([before[row] for row in range(rows)], axis=1)
    packed[2, :, :] = value.astype(jnp.float32)
    packed[3, :, : basis.shape[1]] = jnp.dot(value, basis[...], preferred_element_type=jnp.float32)
    packed[3, :, basis.shape[1] :] = jnp.zeros((value.shape[0], panels - basis.shape[1]), jnp.float32)


def aged_step(spots, table, fanned, incident, near, cross, ztiles, basis):
    rows, dirs, tile = fanned.shape[1:]
    cap = near[0].shape[0] // C
    return kernel_call(
        aged_kernel,
        SMALL,
        out_shape=(
            pltpu.VMEM((4, dirs, rows * tile), jnp.float32),
            pltpu.VMEM((rows, CHUNK, tile, tile), ztiles.dtype),
            pltpu.VMEM(basis.shape, basis.dtype),
        ),
        in_specs=[smem(), smem()] + [vmem()] * (2 * Y) + [hbm()] * 4,
        out_specs=[vmem()] * 3,
        scratch_shapes=[
            pltpu.VMEM((2 * Y * cap, dirs, tile), jnp.bfloat16),
            pltpu.VMEM(ztiles.shape, ztiles.dtype),
            pltpu.VMEM(fanned.shape[1:], fanned.dtype),
            pltpu.VMEM(incident.shape[1:], incident.dtype),
            pltpu.SemaphoreType.DMA((3,)),
            pltpu.SemaphoreType.DMA((rows, ztiles.shape[1] // CHUNK)),
        ],
    )(
        scalar_core(spots),
        scalar_core(table),
        *[near_core(piece) for piece in (*near, *cross)],
        off_core(fanned),
        off_core(incident),
        off_core(ztiles),
        off_core(basis),
    )


def second_kernel(table, packed, fresh, zinv, basis, here, there, ztiles_hbm, dens_out, far, ztiles, flipped, dens, sems, tile_sems):
    rows, slots, tile = ztiles_hbm.shape[0], ztiles_hbm.shape[1], ztiles_hbm.shape[2]
    near = here.shape[0]

    def load(spot):
        ours = here[jnp.minimum(spot, near - 1)]
        theirs = there[jnp.maximum(spot - near, 0)]
        return jnp.where(spot < near, ours, theirs)

    later = []
    for row in range(rows):
        chunks = lax.div(table[2, row * slots] + (CHUNK - 1), CHUNK)
        at = pl.ds(row * tile, tile)
        first = pieces_of(lambda k: table[1, row * slots + k], CHUNK, load)
        total = packed[1, :, at] + jnp.dot(
            first, fresh[row].reshape(CHUNK * tile, tile), preferred_element_type=jnp.float32
        )

        def more(chunk, total):
            copies = []
            for k in range(CHUNK):
                source = ztiles_hbm.at[row, table[0, row * slots + chunk * CHUNK + k]]
                copies.append(pltpu.make_async_copy(source, ztiles.at[k], tile_sems.at[k]))
            for copy in copies:
                copy.start()
            for copy in copies:
                copy.wait()
            picked = pieces_of(lambda k: table[1, row * slots + chunk * CHUNK + k], CHUNK, load)
            return total + jnp.dot(
                picked, ztiles[...].reshape(CHUNK * tile, tile), preferred_element_type=jnp.float32
            )

        total = lax.fori_loop(1, chunks, more, total)
        later.append(density_of(packed[0, :, at], total, zinv[row]))
    value = jnp.concatenate(later, axis=1)
    dens[0] = packed[2].astype(dens.dtype)
    dens[1] = value
    copy = start_all([(dens, dens_out)], sems)[0]
    far_second = jnp.dot(value, basis[...], preferred_element_type=jnp.float32)
    both = jnp.concatenate([packed[3, :, : basis.shape[1]], far_second], axis=0)
    lanes = both.shape[0]
    flipped[:, :lanes] = both.T
    owners = far.shape[0]
    each = basis.shape[1] // owners
    cols = [flipped[pl.ds(c, owners, stride=each), :][:, :lanes] for c in range(each)]
    far[...] = jnp.concatenate([*cols, jnp.zeros((owners, far.shape[1] - each * lanes), jnp.float32)], axis=1)
    copy.wait()


def second_step(table, packed, fresh, zinv, basis, here, there, ztiles, owners):
    tile, dirs = here.shape[2], here.shape[1]
    panels, harmonics = basis.shape
    return kernel_call(
        second_kernel,
        SMALL,
        out_shape=(
            pltpu.HBM((STEPS, dirs, panels), jnp.bfloat16),
            pltpu.VMEM((owners, 128), jnp.float32),
        ),
        in_specs=[smem()] + [vmem()] * 6 + [hbm()],
        out_specs=(hbm(), vmem()),
        scratch_shapes=[
            pltpu.VMEM((CHUNK, tile, tile), ztiles.dtype),
            pltpu.VMEM((harmonics, 128), jnp.float32),
            pltpu.VMEM((STEPS, dirs, panels), jnp.bfloat16),
            pltpu.SemaphoreType.DMA((1,)),
            pltpu.SemaphoreType.DMA((CHUNK,)),
        ],
    )(
        scalar_core(table),
        near_core(packed),
        near_core(fresh),
        near_core(zinv),
        near_core(basis),
        near_core(here),
        near_core(there),
        off_core(ztiles),
    )


def sum_kernel(parts, out):
    total = jnp.sum(parts[...], axis=0, keepdims=True)
    steps, each, dirs = out.shape
    for step in range(steps):
        for c in range(each):
            at = (c * steps + step) * dirs
            out[step, c : c + 1, :] = total[:, at : at + dirs]


def sum_parts(parts, steps, each, dirs):
    return kernel_call(
        sum_kernel,
        SMALL,
        out_shape=jax.ShapeDtypeStruct((steps, each, dirs), jnp.float32),
        in_specs=[vmem()],
        out_specs=vmem(),
    )(near_core(parts))


def shifted(value, axis, length, shift):
    return lax.ppermute(value, axis, [(i, (i + shift) % length) for i in range(length)])


def march(history, incident, ztiles, zinv, columns, lags, counts, basis):
    rows, tile = ztiles.shape[0], ztiles.shape[2]
    dirs = history.shape[1]
    owners = Y * Z * C
    cap = BLOCK_CAP * Z
    outgoing, wanted = open_up(history, columns, lags, tile)
    held = lax.all_to_all(outgoing, "z", 0, 0, tiled=True).reshape(-1, dirs, tile)
    spots, aged, table = chart(counts, columns, lags)
    both = jnp.concatenate([wanted, lax.ppermute(wanted, "c", SWAP)], axis=1)
    lists = [both] + [shifted(both, "y", Y, s) for s in range(1, Y)]
    lists = gather_lists(lists)
    first, later = picks(lists, held, cap)
    got = lax.all_to_all(first.reshape(GROUPS, cap, dirs, tile), ("y", "c"), 0, 0, tiled=True)
    near = [later[0]] + [shifted(later[s], "y", Y, -s) for s in range(1, Y)]
    cross = [lax.ppermute(piece, "c", SWAP) for piece in near]
    top, inverse, driven = stage(counts, ztiles, zinv, incident)
    fanned = first_step(spots, got.reshape(GROUPS * cap, dirs, tile), top, ztiles, inverse, driven)
    here = lax.all_to_all(fanned, ("y", "z"), 0, 0, tiled=True).reshape(Y * Z * rows, dirs, tile)
    packed, lag_one, weights = aged_step(aged, table, fanned, incident, near, cross, ztiles, basis)
    there = lax.ppermute(here, "c", SWAP)
    dens, far = second_step(table, packed, lag_one, inverse, weights, here, there, ztiles, owners)
    each = basis.shape[1] // owners
    parts = lax.all_to_all(far.reshape(owners, 1, 128), E, 0, 0, tiled=True).reshape(owners, 128)
    total = sum_parts(parts, STEPS, each, dirs)
    return dens, total.transpose(0, 2, 1)


def solution(mesh):
    fine = Mesh(mesh.devices.reshape(Y, Z, C, mesh.shape["dir"]), ("y", "z", "c", "dir"))
    in_specs = (
        P(None, "dir", E),
        P(None, "dir", E),
        P(E, None, None, None),
        P(E, None, None),
        P(E, None),
        P(E, None),
        P(E),
        P(E, None),
    )
    out_specs = (P(None, "dir", E), P(None, "dir", E))
    return jax.shard_map(march, mesh=fine, in_specs=in_specs, out_specs=out_specs, check_vma=False)
```

```python
import jax
import jax.numpy as jnp
from jax import lax
from jax.experimental import pallas as pl
from jax.experimental.pallas import tpu as pltpu
from jax.sharding import Mesh, PartitionSpec as P


STEPS = 2
LEVELS = 8
Y, Z, C = 4, 8, 2
GROUPS = Y * C
E = ("y", "z", "c")
BLOCK_CAP = 4
CHUNK = 8
FETCHED = 24
SMALL = 8 << 20
SWAP = [(0, 1), (1, 0)]


def vmem():
    return pl.BlockSpec(memory_space=pltpu.VMEM)


def smem():
    return pl.BlockSpec(memory_space=pltpu.SMEM)


def hbm():
    return pl.BlockSpec(memory_space=pltpu.HBM)


def kernel_call(body, grant, **options):
    return pl.pallas_call(body, compiler_params=pltpu.CompilerParams(vmem_limit_bytes=grant), **options)


def near_core(value):
    return pltpu.with_memory_space_constraint(value, pltpu.VMEM)


def scalar_core(value):
    return pltpu.with_memory_space_constraint(value, pltpu.SMEM)


def off_core(value):
    return pltpu.with_memory_space_constraint(value, pltpu.HBM)


def turned(row):
    return jnp.broadcast_to(row, (8, row.shape[1])).T[:, :1]


def open_kernel(history, columns_hbm, lags_hbm, fanned, wanted, held, columns, lags, sems):
    rows, tile = held.shape[1], held.shape[3]
    pairs = [(history.at[:, :, pl.ds(row * tile, tile)], held.at[:, row]) for row in range(rows)]
    into = start_all([*pairs, (columns_hbm, columns), (lags_hbm, lags)], sems)
    for copy in into:
        copy.wait()
    out = start_all([(held, fanned.at[z]) for z in range(Z)], sems, len(into))
    slots = Slots(columns, lags)
    spot = (slots.z * LEVELS + slots.lag) * slots.rows + slots.local
    asks = lax.broadcasted_iota(jnp.int32, (slots.count, wanted.shape[1]), 1)
    total = jnp.zeros(wanted.shape, jnp.int32)
    for row in range(slots.rows):
        mine = jnp.where(turned(slots.at[row]) == asks, turned(spot[row : row + 1]), 0)
        total += jnp.sum(mine, axis=0, keepdims=True)
    wanted[...] = total
    for copy in out:
        copy.wait()


def open_up(history, columns, lags, tile):
    levels, dirs, panels = history.shape
    rows = panels // tile
    return kernel_call(
        open_kernel,
        SMALL,
        out_shape=(
            pltpu.HBM((Z, levels, rows, dirs, tile), history.dtype),
            pltpu.VMEM((1, GROUPS * BLOCK_CAP * Z), jnp.int32),
        ),
        in_specs=[hbm()] * 3,
        out_specs=(hbm(), vmem()),
        scratch_shapes=[
            pltpu.VMEM((levels, rows, dirs, tile), history.dtype),
            pltpu.VMEM(columns.shape, columns.dtype),
            pltpu.VMEM(lags.shape, lags.dtype),
            pltpu.SemaphoreType.DMA((rows + 2 + Z,)),
        ],
    )(off_core(history), off_core(columns), off_core(lags))


class Slots:
    def __init__(self, columns, lags):
        self.rows, self.count = columns.shape
        col, self.lag = columns[...], lags[...] - 1
        owner = (col * ((1 << 17) // self.rows + 1)) >> 17
        self.local = col - owner * self.rows
        self.c = lax.rem(owner, C)
        self.z = lax.rem(owner // C, Z)
        self.y = owner // (C * Z)
        group = self.y * C + self.c
        self.here = lax.broadcasted_iota(jnp.int32, (self.count, self.count), 1)
        self.there = lax.broadcasted_iota(jnp.int32, (self.count, self.count), 0)
        groups = [group[row : row + 1] for row in range(self.rows)]
        down = [turned(value) for value in groups]
        self.position = []
        for row in range(self.rows):
            same = (down[row] == groups[row]) & (self.there < self.here)
            position = jnp.sum(same.astype(jnp.int32), axis=0, keepdims=True)
            for before in range(row):
                position += jnp.sum((down[before] == groups[row]).astype(jnp.int32), axis=0, keepdims=True)
            self.position.append(position)
        self.at = [groups[row] * (BLOCK_CAP * Z) + self.position[row] for row in range(self.rows)]


def chart_kernel(counts, columns, lags, spots_out, aged_out, table_out, spots, aged, table, sems):
    slots = Slots(columns, lags)
    cap = BLOCK_CAP * Z
    y, c = lax.axis_index("y"), lax.axis_index("c")
    other = (slots.c != c).astype(jnp.int32)
    across = (lax.rem(slots.y - y + Y, Y) * C + other) * cap
    fresh = (other * (Y * Z) + slots.y * Z + slots.z) * slots.rows + slots.local
    lane = lax.broadcasted_iota(jnp.int32, (1, slots.count), 1)
    spot_parts, aged_parts, order_parts, where_parts, new_parts = [], [], [], [], []
    for row in range(slots.rows):
        live = lane < counts[row]
        new = live & (slots.lag[row : row + 1] == 0)
        spot_parts.append(jnp.where(live, slots.at[row], -1))
        aged_parts.append(jnp.where(live & ~new, across[row : row + 1] + slots.position[row], -1))
        fresh_row = jnp.where(new, fresh[row : row + 1], -1)
        marked = turned(new.astype(jnp.int32)) == 1
        rank = jnp.sum((marked & (slots.there < slots.here)).astype(jnp.int32), axis=0, keepdims=True)
        put = marked & (turned(rank) == slots.here)
        order_parts.append(jnp.sum(jnp.where(put, slots.there, 0), axis=0, keepdims=True))
        where_parts.append(jnp.sum(jnp.where(put, turned(fresh_row) + 1, 0), axis=0, keepdims=True) - 1)
        new_count = jnp.sum(new.astype(jnp.int32), axis=1, keepdims=True)
        new_parts.append(jnp.broadcast_to(new_count, (1, slots.count)))
    rest = jnp.zeros((1, spots.shape[1] - slots.rows * slots.count), jnp.int32)
    tail = rest
    for row in range(slots.rows):
        tail = jnp.where(lax.broadcasted_iota(jnp.int32, rest.shape, 1) == row, counts[row], tail)
    spots[...] = jnp.concatenate([*spot_parts, tail], axis=1)
    aged[...] = jnp.concatenate([*aged_parts, tail], axis=1)
    table[0:1, :] = jnp.concatenate([*order_parts, rest], axis=1)
    table[1:2, :] = jnp.concatenate([*where_parts, rest], axis=1)
    table[2:3, :] = jnp.concatenate([*new_parts, rest], axis=1)
    for copy in start_all([(spots, spots_out), (aged, aged_out), (table, table_out)], sems):
        copy.wait()


def chart(counts, columns, lags):
    lengths = (1, 1, 3)
    return kernel_call(
        chart_kernel,
        SMALL,
        out_shape=tuple(pltpu.SMEM((length, 128), jnp.int32) for length in lengths),
        in_specs=[smem(), vmem(), vmem()],
        out_specs=[smem()] * 3,
        scratch_shapes=[pltpu.VMEM((length, 128), jnp.int32) for length in lengths]
        + [pltpu.SemaphoreType.DMA((3,))],
    )(off_core(counts), off_core(columns), off_core(lags))


def gather_lists_kernel(*refs):
    for copy in start_all(list(zip(refs[:Y], refs[Y : 2 * Y])), refs[2 * Y]):
        copy.wait()


def gather_lists(lists):
    return kernel_call(
        gather_lists_kernel,
        SMALL,
        out_shape=tuple(pltpu.SMEM(value.shape, value.dtype) for value in lists),
        in_specs=[vmem()] * Y,
        out_specs=[smem()] * Y,
        scratch_shapes=[pltpu.SemaphoreType.DMA((Y,))],
    )(*[near_core(value) for value in lists])


def whose(shift, other):
    y, c = lax.axis_index("y"), lax.axis_index("c")
    return lax.rem(y - shift + Y, Y) * C + (c if other == 0 else 1 - c)


def pick_kernel(*refs):
    lists, held, first, kept, sems = refs[:Y], refs[Y], refs[Y + 1], refs[Y + 2], refs[Y + 3]
    cap = first.shape[0] // GROUPS
    mine = (lax.axis_index("y") * C + lax.axis_index("c")) * cap
    copies = []
    for shift in range(Y):
        for other in range(C):
            base = len(copies) * cap

            @pl.loop(0, cap, step=16)
            def _(entry):
                for k in range(16):
                    spot = lists[shift][0, other * GROUPS * cap + mine + entry + k]
                    kept[base + entry + k] = held[spot]

            to = whose(shift, other) * cap
            pair = (kept.at[pl.ds(base, cap)], first.at[pl.ds(to, cap)])
            copies += start_all([pair], sems, len(copies))
    for copy in copies:
        copy.wait()


def pick_later_kernel(*refs):
    lists, held, later, kept, sems = refs[:Y], refs[Y], refs[Y + 1 : 2 * Y + 1], refs[2 * Y + 1], refs[2 * Y + 2]
    cap = later[0].shape[0] // C
    back = held.shape[0] // (Z * LEVELS)
    mine = (lax.axis_index("y") * C + lax.axis_index("c")) * cap
    copies = []
    for shift in range(Y):
        for other in range(C):

            @pl.loop(0, cap, step=16)
            def _(entry):
                for k in range(16):
                    spot = lists[shift][0, other * GROUPS * cap + mine + entry + k]
                    kept[shift, other * cap + entry + k] = held[jnp.maximum(spot - back, 0)]

        copies += start_all([(kept.at[shift], later[shift])], sems, shift)
    for copy in copies:
        copy.wait()


def picks(lists, held, cap):
    def out(entries):
        return pltpu.HBM((entries, *held.shape[1:]), held.dtype)

    held = near_core(held)
    lists = [scalar_core(value) for value in lists]
    specs = [smem()] * Y + [vmem()]
    first = kernel_call(
        pick_kernel,
        SMALL,
        out_shape=out(GROUPS * cap),
        in_specs=specs,
        out_specs=hbm(),
        scratch_shapes=[
            pltpu.VMEM((GROUPS * cap, *held.shape[1:]), held.dtype),
            pltpu.SemaphoreType.DMA((GROUPS,)),
        ],
    )(*lists, held)
    later = kernel_call(
        pick_later_kernel,
        SMALL,
        out_shape=[out(C * cap)] * Y,
        in_specs=specs,
        out_specs=[hbm()] * Y,
        scratch_shapes=[
            pltpu.VMEM((Y, C * cap, *held.shape[1:]), held.dtype),
            pltpu.SemaphoreType.DMA((Y,)),
        ],
    )(*lists, held)
    return first, later


def pieces_of(spot_at, count, load):
    parts = []
    for k in range(count):
        spot = spot_at(k)
        value = load(jnp.maximum(spot, 0))
        parts.append(jnp.where(spot >= 0, value, jnp.zeros_like(value)))
    return jnp.concatenate(parts, axis=1)


def row_sum(spots, load, weights, base):
    slots, tile = weights.shape[0], weights.shape[1]
    picked = pieces_of(lambda k: spots[0, base + k], slots, load)
    return jnp.dot(picked, weights[...].reshape(slots * tile, tile), preferred_element_type=jnp.float32)


def density_of(own, total, zinv):
    source = (own.astype(jnp.float32) - total).astype(jnp.bfloat16)
    return jnp.dot(source, zinv, preferred_element_type=jnp.float32).astype(jnp.bfloat16)


def start_all(pairs, sems, base=0):
    copies = [pltpu.make_async_copy(src, dst, sems.at[base + i]) for i, (src, dst) in enumerate(pairs)]
    for copy in copies:
        copy.start()
    return copies


def live_tiles(count, source, target, sems, row, act):
    slots = target.shape[0]
    for chunk in range(slots // CHUNK):
        part = pl.ds(chunk * CHUNK, CHUNK)

        @pl.when(chunk * CHUNK < count)
        def _():
            copy = pltpu.make_async_copy(source.at[part], target.at[part], sems.at[row, chunk])
            if act == "start":
                copy.start()
            else:
                copy.wait()

        if act == "start":

            @pl.when(chunk * CHUNK >= count)
            def _():
                target[part] = jnp.zeros((CHUNK, *target.shape[1:]), target.dtype)


def staged_rows(counts, ztiles_hbm, top, sems, act):
    slots = ztiles_hbm.shape[1]
    for row in range(ztiles_hbm.shape[0]):
        length = min(slots, top.shape[0] - row * slots)
        if length > 0:
            target = top.at[pl.ds(row * slots, length)]
            live_tiles(counts[row], ztiles_hbm.at[row, pl.ds(0, length)], target, sems, row, act)


def stage_kernel(counts, ztiles_hbm, zinv_hbm, incident_hbm, top, zinv, incident, sems, tile_sems):
    staged_rows(counts, ztiles_hbm, top, tile_sems, "start")
    for copy in start_all([(zinv_hbm, zinv), (incident_hbm.at[0], incident)], sems):
        copy.wait()
    staged_rows(counts, ztiles_hbm, top, tile_sems, "wait")


def stage(counts, ztiles, zinv, incident):
    rows, slots, tile = ztiles.shape[0], ztiles.shape[1], ztiles.shape[2]
    return kernel_call(
        stage_kernel,
        SMALL,
        out_shape=(
            pltpu.VMEM((rows * slots - FETCHED, tile, tile), ztiles.dtype),
            pltpu.VMEM(zinv.shape, zinv.dtype),
            pltpu.VMEM(incident.shape[1:], incident.dtype),
        ),
        in_specs=[smem()] + [hbm()] * 3,
        out_specs=[vmem()] * 3,
        scratch_shapes=[
            pltpu.SemaphoreType.DMA((2,)),
            pltpu.SemaphoreType.DMA((rows, slots // CHUNK)),
        ],
    )(off_core(counts), off_core(ztiles), off_core(zinv), off_core(incident))


def first_kernel(spots, got, top, ztiles_hbm, zinv, incident, spread_out, last, kept_out, sems, tile_sems):
    rows, slots, tile = ztiles_hbm.shape[0], ztiles_hbm.shape[1], ztiles_hbm.shape[2]
    begin = slots - last.shape[0]
    rest = ztiles_hbm.at[rows - 1, pl.ds(begin, last.shape[0])]
    count = spots[0, rows * slots + rows - 1] - begin
    live_tiles(count, rest, last, tile_sems, 0, "start")
    copies = []
    for row in range(rows):
        length = slots if row < rows - 1 else begin
        weights = top.at[pl.ds(row * slots, length)]
        total = row_sum(spots, lambda spot: got[spot], weights, row * slots)
        if row == rows - 1:
            live_tiles(count, rest, last, tile_sems, 0, "wait")
            total += row_sum(spots, lambda spot: got[spot], last, row * slots + begin)
        density = density_of(incident[:, row * tile : (row + 1) * tile], total, zinv[row])
        for to in range(spread_out.shape[0]):
            kept_out[row, to] = density
        copies += start_all([(kept_out.at[row], spread_out.at[:, row])], sems, row)
    for copy in copies:
        copy.wait()


def first_step(spots, got, top, ztiles, zinv, incident):
    rows, tile, dirs = ztiles.shape[0], ztiles.shape[2], got.shape[1]
    return kernel_call(
        first_kernel,
        SMALL,
        out_shape=pltpu.HBM((Y * Z, rows, dirs, tile), jnp.bfloat16),
        in_specs=[smem(), vmem(), vmem(), hbm(), vmem(), vmem()],
        out_specs=hbm(),
        scratch_shapes=[
            pltpu.VMEM((FETCHED, tile, tile), ztiles.dtype),
            pltpu.VMEM((rows, Y * Z, dirs, tile), jnp.bfloat16),
            pltpu.SemaphoreType.DMA((rows,)),
            pltpu.SemaphoreType.DMA((1, FETCHED // CHUNK)),
        ],
    )(scalar_core(spots), near_core(got), near_core(top), off_core(ztiles), near_core(zinv), near_core(incident))


def aged_kernel(spots, table, *refs):
    near, cross = refs[:Y], refs[Y : 2 * Y]
    fanned, incident_hbm, ztiles_hbm, basis_hbm, packed, fresh, basis = refs[2 * Y : 2 * Y + 7]
    pool, ztiles, before, incident, sems, tile_sems = refs[2 * Y + 7 :]
    rows, slots, tile = ztiles.shape[0], ztiles.shape[1], ztiles.shape[2]
    cap = near[0].shape[0] // C
    panels = rows * tile
    counts = [spots[0, rows * slots + row] for row in range(rows)]
    for row in range(rows):
        live_tiles(counts[row], ztiles_hbm.at[row], ztiles.at[row], tile_sems, row, "start")
    copies = start_all([(incident_hbm.at[1], incident), (fanned.at[0], before), (basis_hbm, basis)], sems)
    for shift in range(Y):
        for other, source in enumerate((near[shift], cross[shift])):
            pool[pl.ds((shift * C + other) * cap, cap)] = source[pl.ds(other * cap, cap)]
    for row in range(rows):
        live_tiles(counts[row], ztiles_hbm.at[row], ztiles.at[row], tile_sems, row, "wait")
        for k in range(CHUNK):
            fresh[row, k] = ztiles[row, table[0, row * slots + k]]
        at = slice(row * tile, (row + 1) * tile)
        packed[1, :, at] = row_sum(spots, lambda spot: pool[spot], ztiles.at[row], row * slots)
    for copy in copies:
        copy.wait()
    packed[0, :, :] = incident[...].astype(jnp.float32)
    value = jnp.concatenate([before[row] for row in range(rows)], axis=1)
    packed[2, :, :] = value.astype(jnp.float32)
    packed[3, :, : basis.shape[1]] = jnp.dot(value, basis[...], preferred_element_type=jnp.float32)
    packed[3, :, basis.shape[1] :] = jnp.zeros((value.shape[0], panels - basis.shape[1]), jnp.float32)


def aged_step(spots, table, fanned, incident, near, cross, ztiles, basis):
    rows, dirs, tile = fanned.shape[1:]
    cap = near[0].shape[0] // C
    return kernel_call(
        aged_kernel,
        SMALL,
        out_shape=(
            pltpu.VMEM((4, dirs, rows * tile), jnp.float32),
            pltpu.VMEM((rows, CHUNK, tile, tile), ztiles.dtype),
            pltpu.VMEM(basis.shape, basis.dtype),
        ),
        in_specs=[smem(), smem()] + [vmem()] * (2 * Y) + [hbm()] * 4,
        out_specs=[vmem()] * 3,
        scratch_shapes=[
            pltpu.VMEM((2 * Y * cap, dirs, tile), jnp.bfloat16),
            pltpu.VMEM(ztiles.shape, ztiles.dtype),
            pltpu.VMEM(fanned.shape[1:], fanned.dtype),
            pltpu.VMEM(incident.shape[1:], incident.dtype),
            pltpu.SemaphoreType.DMA((3,)),
            pltpu.SemaphoreType.DMA((rows, ztiles.shape[1] // CHUNK)),
        ],
    )(
        scalar_core(spots),
        scalar_core(table),
        *[near_core(piece) for piece in (*near, *cross)],
        off_core(fanned),
        off_core(incident),
        off_core(ztiles),
        off_core(basis),
    )


def second_kernel(table, packed, fresh, zinv, basis, here, there, ztiles_hbm, dens_out, far, ztiles, flipped, dens, sems, tile_sems):
    rows, slots, tile = ztiles_hbm.shape[0], ztiles_hbm.shape[1], ztiles_hbm.shape[2]
    near = here.shape[0]

    def load(spot):
        ours = here[jnp.minimum(spot, near - 1)]
        theirs = there[jnp.maximum(spot - near, 0)]
        return jnp.where(spot < near, ours, theirs)

    later = []
    for row in range(rows):
        chunks = lax.div(table[2, row * slots] + (CHUNK - 1), CHUNK)
        at = pl.ds(row * tile, tile)
        first = pieces_of(lambda k: table[1, row * slots + k], CHUNK, load)
        total = packed[1, :, at] + jnp.dot(
            first, fresh[row].reshape(CHUNK * tile, tile), preferred_element_type=jnp.float32
        )

        def more(chunk, total):
            copies = []
            for k in range(CHUNK):
                source = ztiles_hbm.at[row, table[0, row * slots + chunk * CHUNK + k]]
                copies.append(pltpu.make_async_copy(source, ztiles.at[k], tile_sems.at[k]))
            for copy in copies:
                copy.start()
            for copy in copies:
                copy.wait()
            picked = pieces_of(lambda k: table[1, row * slots + chunk * CHUNK + k], CHUNK, load)
            return total + jnp.dot(
                picked, ztiles[...].reshape(CHUNK * tile, tile), preferred_element_type=jnp.float32
            )

        total = lax.fori_loop(1, chunks, more, total)
        later.append(density_of(packed[0, :, at], total, zinv[row]))
    value = jnp.concatenate(later, axis=1)
    dens[0] = packed[2].astype(dens.dtype)
    dens[1] = value
    copy = start_all([(dens, dens_out)], sems)[0]
    far_second = jnp.dot(value, basis[...], preferred_element_type=jnp.float32)
    both = jnp.concatenate([packed[3, :, : basis.shape[1]], far_second], axis=0)
    lanes = both.shape[0]
    flipped[:, :lanes] = both.T
    owners = far.shape[0]
    each = basis.shape[1] // owners
    cols = [flipped[pl.ds(c, owners, stride=each), :][:, :lanes] for c in range(each)]
    far[...] = jnp.concatenate([*cols, jnp.zeros((owners, far.shape[1] - each * lanes), jnp.float32)], axis=1)
    copy.wait()


def second_step(table, packed, fresh, zinv, basis, here, there, ztiles, owners):
    tile, dirs = here.shape[2], here.shape[1]
    panels, harmonics = basis.shape
    return kernel_call(
        second_kernel,
        SMALL,
        out_shape=(
            pltpu.HBM((STEPS, dirs, panels), jnp.bfloat16),
            pltpu.VMEM((owners, 128), jnp.float32),
        ),
        in_specs=[smem()] + [vmem()] * 6 + [hbm()],
        out_specs=(hbm(), vmem()),
        scratch_shapes=[
            pltpu.VMEM((CHUNK, tile, tile), ztiles.dtype),
            pltpu.VMEM((harmonics, 128), jnp.float32),
            pltpu.VMEM((STEPS, dirs, panels), jnp.bfloat16),
            pltpu.SemaphoreType.DMA((1,)),
            pltpu.SemaphoreType.DMA((CHUNK,)),
        ],
    )(
        scalar_core(table),
        near_core(packed),
        near_core(fresh),
        near_core(zinv),
        near_core(basis),
        near_core(here),
        near_core(there),
        off_core(ztiles),
    )


def sum_kernel(parts, out):
    total = jnp.sum(parts[...], axis=0, keepdims=True)
    steps, each, dirs = out.shape
    for step in range(steps):
        for c in range(each):
            at = (c * steps + step) * dirs
            out[step, c : c + 1, :] = total[:, at : at + dirs]


def sum_parts(parts, steps, each, dirs):
    return kernel_call(
        sum_kernel,
        SMALL,
        out_shape=jax.ShapeDtypeStruct((steps, each, dirs), jnp.float32),
        in_specs=[vmem()],
        out_specs=vmem(),
    )(near_core(parts))


def shifted(value, axis, length, shift):
    return lax.ppermute(value, axis, [(i, (i + shift) % length) for i in range(length)])


def march(history, incident, ztiles, zinv, columns, lags, counts, basis):
    rows, tile = ztiles.shape[0], ztiles.shape[2]
    dirs = history.shape[1]
    owners = Y * Z * C
    cap = BLOCK_CAP * Z
    outgoing, wanted = open_up(history, columns, lags, tile)
    held = lax.all_to_all(outgoing, "z", 0, 0, tiled=True).reshape(-1, dirs, tile)
    spots, aged, table = chart(counts, columns, lags)
    both = jnp.concatenate([wanted, lax.ppermute(wanted, "c", SWAP)], axis=1)
    lists = [both] + [shifted(both, "y", Y, s) for s in range(1, Y)]
    lists = gather_lists(lists)
    first, later = picks(lists, held, cap)
    got = lax.all_to_all(first.reshape(GROUPS, cap, dirs, tile), ("y", "c"), 0, 0, tiled=True)
    near = [later[0]] + [shifted(later[s], "y", Y, -s) for s in range(1, Y)]
    cross = [lax.ppermute(near[0], "c", SWAP)]
    cross += [lax.ppermute(piece, "c", SWAP) for piece in near[1:]]
    top, inverse, driven = stage(counts, ztiles, zinv, incident)
    fanned = first_step(spots, got.reshape(GROUPS * cap, dirs, tile), top, ztiles, inverse, driven)
    here = lax.all_to_all(fanned, ("y", "z"), 0, 0, tiled=True).reshape(Y * Z * rows, dirs, tile)
    packed, lag_one, weights = aged_step(aged, table, fanned, incident, near, cross, ztiles, basis)
    there = lax.ppermute(here, "c", SWAP)
    dens, far = second_step(table, packed, lag_one, inverse, weights, here, there, ztiles, owners)
    each = basis.shape[1] // owners
    parts = lax.all_to_all(far.reshape(owners, 1, 128), E, 0, 0, tiled=True).reshape(owners, 128)
    total = sum_parts(parts, STEPS, each, dirs)
    return dens, total.transpose(0, 2, 1)


def solution(mesh):
    fine = Mesh(mesh.devices.reshape(Y, Z, C, mesh.shape["dir"]), ("y", "z", "c", "dir"))
    in_specs = (
        P(None, "dir", E),
        P(None, "dir", E),
        P(E, None, None, None),
        P(E, None, None),
        P(E, None),
        P(E, None),
        P(E),
        P(E, None),
    )
    out_specs = (P(None, "dir", E), P(None, "dir", E))
    return jax.shard_map(march, mesh=fine, in_specs=in_specs, out_specs=out_specs, check_vma=False)
```

```python
import jax
import jax.numpy as jnp
from jax import lax
from jax.experimental import pallas as pl
from jax.experimental.pallas import tpu as pltpu
from jax.sharding import Mesh, PartitionSpec as P


STEPS = 2
LEVELS = 8
Y, Z, C = 4, 8, 2
GROUPS = Y * C
E = ("y", "z", "c")
BLOCK_CAP = 4
CHUNK = 8
FETCHED = 24
SMALL = 8 << 20
SWAP = [(0, 1), (1, 0)]


def vmem():
    return pl.BlockSpec(memory_space=pltpu.VMEM)


def smem():
    return pl.BlockSpec(memory_space=pltpu.SMEM)


def hbm():
    return pl.BlockSpec(memory_space=pltpu.HBM)


def kernel_call(body, grant, **options):
    return pl.pallas_call(body, compiler_params=pltpu.CompilerParams(vmem_limit_bytes=grant), **options)


def near_core(value):
    return pltpu.with_memory_space_constraint(value, pltpu.VMEM)


def scalar_core(value):
    return pltpu.with_memory_space_constraint(value, pltpu.SMEM)


def off_core(value):
    return pltpu.with_memory_space_constraint(value, pltpu.HBM)


def turned(row):
    return jnp.broadcast_to(row, (8, row.shape[1])).T[:, :1]


def open_kernel(history, columns_hbm, lags_hbm, fanned, wanted, held, columns, lags, sems):
    rows, tile = held.shape[1], held.shape[3]
    pairs = [(history.at[:, :, pl.ds(row * tile, tile)], held.at[:, row]) for row in range(rows)]
    into = start_all([*pairs, (columns_hbm, columns), (lags_hbm, lags)], sems)
    for copy in into:
        copy.wait()
    out = start_all([(held, fanned.at[z]) for z in range(Z)], sems, len(into))
    slots = Slots(columns, lags)
    spot = (slots.z * LEVELS + slots.lag) * slots.rows + slots.local
    asks = lax.broadcasted_iota(jnp.int32, (slots.count, wanted.shape[1]), 1)
    total = jnp.zeros(wanted.shape, jnp.int32)
    for row in range(slots.rows):
        mine = jnp.where(turned(slots.at[row]) == asks, turned(spot[row : row + 1]), 0)
        total += jnp.sum(mine, axis=0, keepdims=True)
    wanted[...] = total
    for copy in out:
        copy.wait()


def open_up(history, columns, lags, tile):
    levels, dirs, panels = history.shape
    rows = panels // tile
    return kernel_call(
        open_kernel,
        SMALL,
        out_shape=(
            pltpu.HBM((Z, levels, rows, dirs, tile), history.dtype),
            pltpu.VMEM((1, GROUPS * BLOCK_CAP * Z), jnp.int32),
        ),
        in_specs=[hbm()] * 3,
        out_specs=(hbm(), vmem()),
        scratch_shapes=[
            pltpu.VMEM((levels, rows, dirs, tile), history.dtype),
            pltpu.VMEM(columns.shape, columns.dtype),
            pltpu.VMEM(lags.shape, lags.dtype),
            pltpu.SemaphoreType.DMA((rows + 2 + Z,)),
        ],
    )(off_core(history), off_core(columns), off_core(lags))


class Slots:
    def __init__(self, columns, lags):
        self.rows, self.count = columns.shape
        col, self.lag = columns[...], lags[...] - 1
        owner = (col * ((1 << 17) // self.rows + 1)) >> 17
        self.local = col - owner * self.rows
        self.c = lax.rem(owner, C)
        self.z = lax.rem(owner // C, Z)
        self.y = owner // (C * Z)
        group = self.y * C + self.c
        self.here = lax.broadcasted_iota(jnp.int32, (self.count, self.count), 1)
        self.there = lax.broadcasted_iota(jnp.int32, (self.count, self.count), 0)
        groups = [group[row : row + 1] for row in range(self.rows)]
        down = [turned(value) for value in groups]
        self.position = []
        for row in range(self.rows):
            same = (down[row] == groups[row]) & (self.there < self.here)
            position = jnp.sum(same.astype(jnp.int32), axis=0, keepdims=True)
            for before in range(row):
                position += jnp.sum((down[before] == groups[row]).astype(jnp.int32), axis=0, keepdims=True)
            self.position.append(position)
        self.at = [groups[row] * (BLOCK_CAP * Z) + self.position[row] for row in range(self.rows)]


def chart_kernel(counts, columns, lags, spots_out, aged_out, table_out, spots, aged, table, sems):
    slots = Slots(columns, lags)
    cap = BLOCK_CAP * Z
    y, c = lax.axis_index("y"), lax.axis_index("c")
    other = (slots.c != c).astype(jnp.int32)
    across = (lax.rem(slots.y - y + Y, Y) * C + other) * cap
    fresh = (other * (Y * Z) + slots.y * Z + slots.z) * slots.rows + slots.local
    lane = lax.broadcasted_iota(jnp.int32, (1, slots.count), 1)
    spot_parts, aged_parts, order_parts, where_parts, new_parts = [], [], [], [], []
    for row in range(slots.rows):
        live = lane < counts[row]
        new = live & (slots.lag[row : row + 1] == 0)
        spot_parts.append(jnp.where(live, slots.at[row], -1))
        aged_parts.append(jnp.where(live & ~new, across[row : row + 1] + slots.position[row], -1))
        fresh_row = jnp.where(new, fresh[row : row + 1], -1)
        marked = turned(new.astype(jnp.int32)) == 1
        rank = jnp.sum((marked & (slots.there < slots.here)).astype(jnp.int32), axis=0, keepdims=True)
        put = marked & (turned(rank) == slots.here)
        order_parts.append(jnp.sum(jnp.where(put, slots.there, 0), axis=0, keepdims=True))
        where_parts.append(jnp.sum(jnp.where(put, turned(fresh_row) + 1, 0), axis=0, keepdims=True) - 1)
        new_count = jnp.sum(new.astype(jnp.int32), axis=1, keepdims=True)
        new_parts.append(jnp.broadcast_to(new_count, (1, slots.count)))
    rest = jnp.zeros((1, spots.shape[1] - slots.rows * slots.count), jnp.int32)
    tail = rest
    for row in range(slots.rows):
        tail = jnp.where(lax.broadcasted_iota(jnp.int32, rest.shape, 1) == row, counts[row], tail)
    spots[...] = jnp.concatenate([*spot_parts, tail], axis=1)
    aged[...] = jnp.concatenate([*aged_parts, tail], axis=1)
    table[0:1, :] = jnp.concatenate([*order_parts, rest], axis=1)
    table[1:2, :] = jnp.concatenate([*where_parts, rest], axis=1)
    table[2:3, :] = jnp.concatenate([*new_parts, rest], axis=1)
    for copy in start_all([(spots, spots_out), (aged, aged_out), (table, table_out)], sems):
        copy.wait()


def chart(counts, columns, lags):
    lengths = (1, 1, 3)
    return kernel_call(
        chart_kernel,
        SMALL,
        out_shape=tuple(pltpu.SMEM((length, 128), jnp.int32) for length in lengths),
        in_specs=[smem(), vmem(), vmem()],
        out_specs=[smem()] * 3,
        scratch_shapes=[pltpu.VMEM((length, 128), jnp.int32) for length in lengths]
        + [pltpu.SemaphoreType.DMA((3,))],
    )(off_core(counts), off_core(columns), off_core(lags))


def gather_lists_kernel(*refs):
    for copy in start_all(list(zip(refs[:Y], refs[Y : 2 * Y])), refs[2 * Y]):
        copy.wait()


def gather_lists(lists):
    return kernel_call(
        gather_lists_kernel,
        SMALL,
        out_shape=tuple(pltpu.SMEM(value.shape, value.dtype) for value in lists),
        in_specs=[vmem()] * Y,
        out_specs=[smem()] * Y,
        scratch_shapes=[pltpu.SemaphoreType.DMA((Y,))],
    )(*[near_core(value) for value in lists])


def whose(shift, other):
    y, c = lax.axis_index("y"), lax.axis_index("c")
    return lax.rem(y - shift + Y, Y) * C + (c if other == 0 else 1 - c)


def pick_kernel(*refs):
    lists, held, first, kept, sems = refs[:Y], refs[Y], refs[Y + 1], refs[Y + 2], refs[Y + 3]
    cap = first.shape[0] // GROUPS
    mine = (lax.axis_index("y") * C + lax.axis_index("c")) * cap
    copies = []
    for shift in range(Y):
        for other in range(C):
            base = len(copies) * cap

            @pl.loop(0, cap, step=16)
            def _(entry):
                for k in range(16):
                    spot = lists[shift][0, other * GROUPS * cap + mine + entry + k]
                    kept[base + entry + k] = held[spot]

            to = whose(shift, other) * cap
            pair = (kept.at[pl.ds(base, cap)], first.at[pl.ds(to, cap)])
            copies += start_all([pair], sems, len(copies))
    for copy in copies:
        copy.wait()


def pick_later_kernel(*refs):
    lists, held, later, kept, sems = refs[:Y], refs[Y], refs[Y + 1 : 2 * Y + 1], refs[2 * Y + 1], refs[2 * Y + 2]
    cap = later[0].shape[0] // C
    back = held.shape[0] // (Z * LEVELS)
    mine = (lax.axis_index("y") * C + lax.axis_index("c")) * cap
    copies = []
    for shift in range(Y):
        for other in range(C):

            @pl.loop(0, cap, step=16)
            def _(entry):
                for k in range(16):
                    spot = lists[shift][0, other * GROUPS * cap + mine + entry + k]
                    kept[shift, other * cap + entry + k] = held[jnp.maximum(spot - back, 0)]

        copies += start_all([(kept.at[shift], later[shift])], sems, shift)
    for copy in copies:
        copy.wait()


def picks(lists, held, cap):
    def out(entries):
        return pltpu.HBM((entries, *held.shape[1:]), held.dtype)

    held = near_core(held)
    lists = [scalar_core(value) for value in lists]
    specs = [smem()] * Y + [vmem()]
    first = kernel_call(
        pick_kernel,
        SMALL,
        out_shape=out(GROUPS * cap),
        in_specs=specs,
        out_specs=hbm(),
        scratch_shapes=[
            pltpu.VMEM((GROUPS * cap, *held.shape[1:]), held.dtype),
            pltpu.SemaphoreType.DMA((GROUPS,)),
        ],
    )(*lists, held)
    later = kernel_call(
        pick_later_kernel,
        SMALL,
        out_shape=[out(C * cap)] * Y,
        in_specs=specs,
        out_specs=[hbm()] * Y,
        scratch_shapes=[
            pltpu.VMEM((Y, C * cap, *held.shape[1:]), held.dtype),
            pltpu.SemaphoreType.DMA((Y,)),
        ],
    )(*lists, held)
    return first, later


def pieces_of(spot_at, count, load):
    parts = []
    for k in range(count):
        spot = spot_at(k)
        value = load(jnp.maximum(spot, 0))
        parts.append(jnp.where(spot >= 0, value, jnp.zeros_like(value)))
    return jnp.concatenate(parts, axis=1)


def row_sum(spots, load, weights, base):
    slots, tile = weights.shape[0], weights.shape[1]
    picked = pieces_of(lambda k: spots[0, base + k], slots, load)
    return jnp.dot(picked, weights[...].reshape(slots * tile, tile), preferred_element_type=jnp.float32)


def density_of(own, total, zinv):
    source = (own.astype(jnp.float32) - total).astype(jnp.bfloat16)
    return jnp.dot(source, zinv, preferred_element_type=jnp.float32).astype(jnp.bfloat16)


def start_all(pairs, sems, base=0):
    copies = [pltpu.make_async_copy(src, dst, sems.at[base + i]) for i, (src, dst) in enumerate(pairs)]
    for copy in copies:
        copy.start()
    return copies


def live_tiles(count, source, target, sems, row, act):
    slots = target.shape[0]
    for chunk in range(slots // CHUNK):
        part = pl.ds(chunk * CHUNK, CHUNK)

        @pl.when(chunk * CHUNK < count)
        def _():
            copy = pltpu.make_async_copy(source.at[part], target.at[part], sems.at[row, chunk])
            if act == "start":
                copy.start()
            else:
                copy.wait()

        if act == "start":

            @pl.when(chunk * CHUNK >= count)
            def _():
                target[part] = jnp.zeros((CHUNK, *target.shape[1:]), target.dtype)


def staged_rows(counts, ztiles_hbm, top, sems, act):
    slots = ztiles_hbm.shape[1]
    for row in range(ztiles_hbm.shape[0]):
        length = min(slots, top.shape[0] - row * slots)
        if length > 0:
            target = top.at[pl.ds(row * slots, length)]
            live_tiles(counts[row], ztiles_hbm.at[row, pl.ds(0, length)], target, sems, row, act)


def stage_kernel(counts, ztiles_hbm, zinv_hbm, incident_hbm, top, zinv, incident, sems, tile_sems):
    staged_rows(counts, ztiles_hbm, top, tile_sems, "start")
    for copy in start_all([(zinv_hbm, zinv), (incident_hbm.at[0], incident)], sems):
        copy.wait()
    staged_rows(counts, ztiles_hbm, top, tile_sems, "wait")


def stage(counts, ztiles, zinv, incident):
    rows, slots, tile = ztiles.shape[0], ztiles.shape[1], ztiles.shape[2]
    return kernel_call(
        stage_kernel,
        SMALL,
        out_shape=(
            pltpu.VMEM((rows * slots - FETCHED, tile, tile), ztiles.dtype),
            pltpu.VMEM(zinv.shape, zinv.dtype),
            pltpu.VMEM(incident.shape[1:], incident.dtype),
        ),
        in_specs=[smem()] + [hbm()] * 3,
        out_specs=[vmem()] * 3,
        scratch_shapes=[
            pltpu.SemaphoreType.DMA((2,)),
            pltpu.SemaphoreType.DMA((rows, slots // CHUNK)),
        ],
    )(off_core(counts), off_core(ztiles), off_core(zinv), off_core(incident))


def first_kernel(spots, got, top, ztiles_hbm, zinv, incident, spread_out, last, kept_out, sems, tile_sems):
    rows, slots, tile = ztiles_hbm.shape[0], ztiles_hbm.shape[1], ztiles_hbm.shape[2]
    begin = slots - last.shape[0]
    rest = ztiles_hbm.at[rows - 1, pl.ds(begin, last.shape[0])]
    count = spots[0, rows * slots + rows - 1] - begin
    live_tiles(count, rest, last, tile_sems, 0, "start")
    copies = []
    for row in range(rows):
        length = slots if row < rows - 1 else begin
        weights = top.at[pl.ds(row * slots, length)]
        total = row_sum(spots, lambda spot: got[spot], weights, row * slots)
        if row == rows - 1:
            live_tiles(count, rest, last, tile_sems, 0, "wait")
            total += row_sum(spots, lambda spot: got[spot], last, row * slots + begin)
        density = density_of(incident[:, row * tile : (row + 1) * tile], total, zinv[row])
        for to in range(spread_out.shape[0]):
            kept_out[row, to] = density
        copies += start_all([(kept_out.at[row], spread_out.at[:, row])], sems, row)
    for copy in copies:
        copy.wait()


def first_step(spots, got, top, ztiles, zinv, incident):
    rows, tile, dirs = ztiles.shape[0], ztiles.shape[2], got.shape[1]
    return kernel_call(
        first_kernel,
        SMALL,
        out_shape=pltpu.HBM((Y * Z, rows, dirs, tile), jnp.bfloat16),
        in_specs=[smem(), vmem(), vmem(), hbm(), vmem(), vmem()],
        out_specs=hbm(),
        scratch_shapes=[
            pltpu.VMEM((FETCHED, tile, tile), ztiles.dtype),
            pltpu.VMEM((rows, Y * Z, dirs, tile), jnp.bfloat16),
            pltpu.SemaphoreType.DMA((rows,)),
            pltpu.SemaphoreType.DMA((1, FETCHED // CHUNK)),
        ],
    )(scalar_core(spots), near_core(got), near_core(top), off_core(ztiles), near_core(zinv), near_core(incident))


def aged_kernel(spots, table, *refs):
    near, cross = refs[:Y], refs[Y : 2 * Y]
    fanned, incident_hbm, ztiles_hbm, basis_hbm, packed, fresh, basis = refs[2 * Y : 2 * Y + 7]
    pool, ztiles, before, incident, sems, tile_sems = refs[2 * Y + 7 :]
    rows, slots, tile = ztiles.shape[0], ztiles.shape[1], ztiles.shape[2]
    cap = near[0].shape[0] // C
    panels = rows * tile
    counts = [spots[0, rows * slots + row] for row in range(rows)]
    for row in range(rows):
        live_tiles(counts[row], ztiles_hbm.at[row], ztiles.at[row], tile_sems, row, "start")
    own = [
        (source.at[pl.ds(other * cap, cap)], pool.at[pl.ds(other * cap, cap)])
        for other, source in enumerate((near[0], cross[0]))
    ]
    own = start_all(own, sems)
    copies = start_all([(incident_hbm.at[1], incident), (fanned.at[0], before), (basis_hbm, basis)], sems, C)
    for shift in range(1, Y):
        for other, source in enumerate((near[shift], cross[shift])):
            pool[pl.ds((shift * C + other) * cap, cap)] = source[pl.ds(other * cap, cap)]
    for copy in own:
        copy.wait()
    for row in range(rows):
        live_tiles(counts[row], ztiles_hbm.at[row], ztiles.at[row], tile_sems, row, "wait")
        for k in range(CHUNK):
            fresh[row, k] = ztiles[row, table[0, row * slots + k]]
        at = slice(row * tile, (row + 1) * tile)
        packed[1, :, at] = row_sum(spots, lambda spot: pool[spot], ztiles.at[row], row * slots)
    for copy in copies:
        copy.wait()
    packed[0, :, :] = incident[...].astype(jnp.float32)
    value = jnp.concatenate([before[row] for row in range(rows)], axis=1)
    packed[2, :, :] = value.astype(jnp.float32)
    packed[3, :, : basis.shape[1]] = jnp.dot(value, basis[...], preferred_element_type=jnp.float32)
    packed[3, :, basis.shape[1] :] = jnp.zeros((value.shape[0], panels - basis.shape[1]), jnp.float32)


def aged_step(spots, table, fanned, incident, near, cross, ztiles, basis):
    rows, dirs, tile = fanned.shape[1:]
    cap = near[0].shape[0] // C
    return kernel_call(
        aged_kernel,
        SMALL,
        out_shape=(
            pltpu.VMEM((4, dirs, rows * tile), jnp.float32),
            pltpu.VMEM((rows, CHUNK, tile, tile), ztiles.dtype),
            pltpu.VMEM(basis.shape, basis.dtype),
        ),
        in_specs=[smem(), smem()] + ([hbm()] + [vmem()] * (Y - 1)) * 2 + [hbm()] * 4,
        out_specs=[vmem()] * 3,
        scratch_shapes=[
            pltpu.VMEM((2 * Y * cap, dirs, tile), jnp.bfloat16),
            pltpu.VMEM(ztiles.shape, ztiles.dtype),
            pltpu.VMEM(fanned.shape[1:], fanned.dtype),
            pltpu.VMEM(incident.shape[1:], incident.dtype),
            pltpu.SemaphoreType.DMA((C + 3,)),
            pltpu.SemaphoreType.DMA((rows, ztiles.shape[1] // CHUNK)),
        ],
    )(
        scalar_core(spots),
        scalar_core(table),
        off_core(near[0]),
        *[near_core(piece) for piece in near[1:]],
        off_core(cross[0]),
        *[near_core(piece) for piece in cross[1:]],
        off_core(fanned),
        off_core(incident),
        off_core(ztiles),
        off_core(basis),
    )


def second_kernel(table, packed, fresh, zinv, basis, here, there, ztiles_hbm, dens_out, far, ztiles, flipped, dens, sems, tile_sems):
    rows, slots, tile = ztiles_hbm.shape[0], ztiles_hbm.shape[1], ztiles_hbm.shape[2]
    near = here.shape[0]

    def load(spot):
        ours = here[jnp.minimum(spot, near - 1)]
        theirs = there[jnp.maximum(spot - near, 0)]
        return jnp.where(spot < near, ours, theirs)

    later = []
    for row in range(rows):
        chunks = lax.div(table[2, row * slots] + (CHUNK - 1), CHUNK)
        at = pl.ds(row * tile, tile)
        first = pieces_of(lambda k: table[1, row * slots + k], CHUNK, load)
        total = packed[1, :, at] + jnp.dot(
            first, fresh[row].reshape(CHUNK * tile, tile), preferred_element_type=jnp.float32
        )

        def more(chunk, total):
            copies = []
            for k in range(CHUNK):
                source = ztiles_hbm.at[row, table[0, row * slots + chunk * CHUNK + k]]
                copies.append(pltpu.make_async_copy(source, ztiles.at[k], tile_sems.at[k]))
            for copy in copies:
                copy.start()
            for copy in copies:
                copy.wait()
            picked = pieces_of(lambda k: table[1, row * slots + chunk * CHUNK + k], CHUNK, load)
            return total + jnp.dot(
                picked, ztiles[...].reshape(CHUNK * tile, tile), preferred_element_type=jnp.float32
            )

        total = lax.fori_loop(1, chunks, more, total)
        later.append(density_of(packed[0, :, at], total, zinv[row]))
    value = jnp.concatenate(later, axis=1)
    dens[0] = packed[2].astype(dens.dtype)
    dens[1] = value
    copy = start_all([(dens, dens_out)], sems)[0]
    far_second = jnp.dot(value, basis[...], preferred_element_type=jnp.float32)
    both = jnp.concatenate([packed[3, :, : basis.shape[1]], far_second], axis=0)
    lanes = both.shape[0]
    flipped[:, :lanes] = both.T
    owners = far.shape[0]
    each = basis.shape[1] // owners
    cols = [flipped[pl.ds(c, owners, stride=each), :][:, :lanes] for c in range(each)]
    far[...] = jnp.concatenate([*cols, jnp.zeros((owners, far.shape[1] - each * lanes), jnp.float32)], axis=1)
    copy.wait()


def second_step(table, packed, fresh, zinv, basis, here, there, ztiles, owners):
    tile, dirs = here.shape[2], here.shape[1]
    panels, harmonics = basis.shape
    return kernel_call(
        second_kernel,
        SMALL,
        out_shape=(
            pltpu.HBM((STEPS, dirs, panels), jnp.bfloat16),
            pltpu.VMEM((owners, 128), jnp.float32),
        ),
        in_specs=[smem()] + [vmem()] * 6 + [hbm()],
        out_specs=(hbm(), vmem()),
        scratch_shapes=[
            pltpu.VMEM((CHUNK, tile, tile), ztiles.dtype),
            pltpu.VMEM((harmonics, 128), jnp.float32),
            pltpu.VMEM((STEPS, dirs, panels), jnp.bfloat16),
            pltpu.SemaphoreType.DMA((1,)),
            pltpu.SemaphoreType.DMA((CHUNK,)),
        ],
    )(
        scalar_core(table),
        near_core(packed),
        near_core(fresh),
        near_core(zinv),
        near_core(basis),
        near_core(here),
        near_core(there),
        off_core(ztiles),
    )


def sum_kernel(parts, out):
    total = jnp.sum(parts[...], axis=0, keepdims=True)
    steps, each, dirs = out.shape
    for step in range(steps):
        for c in range(each):
            at = (c * steps + step) * dirs
            out[step, c : c + 1, :] = total[:, at : at + dirs]


def sum_parts(parts, steps, each, dirs):
    return kernel_call(
        sum_kernel,
        SMALL,
        out_shape=jax.ShapeDtypeStruct((steps, each, dirs), jnp.float32),
        in_specs=[vmem()],
        out_specs=vmem(),
    )(near_core(parts))


def shifted(value, axis, length, shift):
    return lax.ppermute(value, axis, [(i, (i + shift) % length) for i in range(length)])


def march(history, incident, ztiles, zinv, columns, lags, counts, basis):
    rows, tile = ztiles.shape[0], ztiles.shape[2]
    dirs = history.shape[1]
    owners = Y * Z * C
    cap = BLOCK_CAP * Z
    outgoing, wanted = open_up(history, columns, lags, tile)
    held = lax.all_to_all(outgoing, "z", 0, 0, tiled=True).reshape(-1, dirs, tile)
    spots, aged, table = chart(counts, columns, lags)
    both = jnp.concatenate([wanted, lax.ppermute(wanted, "c", SWAP)], axis=1)
    lists = [both] + [shifted(both, "y", Y, s) for s in range(1, Y)]
    lists = gather_lists(lists)
    first, later = picks(lists, held, cap)
    got = lax.all_to_all(first.reshape(GROUPS, cap, dirs, tile), ("y", "c"), 0, 0, tiled=True)
    near = [later[0]] + [shifted(later[s], "y", Y, -s) for s in range(1, Y)]
    cross = [lax.ppermute(near[0], "c", SWAP)]
    cross += [lax.ppermute(piece, "c", SWAP) for piece in near[1:]]
    top, inverse, driven = stage(counts, ztiles, zinv, incident)
    fanned = first_step(spots, got.reshape(GROUPS * cap, dirs, tile), top, ztiles, inverse, driven)
    here = lax.all_to_all(fanned, ("y", "z"), 0, 0, tiled=True).reshape(Y * Z * rows, dirs, tile)
    packed, lag_one, weights = aged_step(aged, table, fanned, incident, near, cross, ztiles, basis)
    there = lax.ppermute(here, "c", SWAP)
    dens, far = second_step(table, packed, lag_one, inverse, weights, here, there, ztiles, owners)
    each = basis.shape[1] // owners
    parts = lax.all_to_all(far.reshape(owners, 1, 128), E, 0, 0, tiled=True).reshape(owners, 128)
    total = sum_parts(parts, STEPS, each, dirs)
    return dens, total.transpose(0, 2, 1)


def solution(mesh):
    fine = Mesh(mesh.devices.reshape(Y, Z, C, mesh.shape["dir"]), ("y", "z", "c", "dir"))
    in_specs = (
        P(None, "dir", E),
        P(None, "dir", E),
        P(E, None, None, None),
        P(E, None, None),
        P(E, None),
        P(E, None),
        P(E),
        P(E, None),
    )
    out_specs = (P(None, "dir", E), P(None, "dir", E))
    return jax.shard_map(march, mesh=fine, in_specs=in_specs, out_specs=out_specs, check_vma=False)
```

```python
import jax
import jax.numpy as jnp
from jax import lax
from jax.experimental import pallas as pl
from jax.experimental.pallas import tpu as pltpu
from jax.sharding import Mesh, PartitionSpec as P


STEPS = 2
LEVELS = 8
Y, Z, C = 4, 8, 2
GROUPS = Y * C
E = ("y", "z", "c")
BLOCK_CAP = 4
CHUNK = 8
FETCHED = 24
SMALL = 8 << 20
SWAP = [(0, 1), (1, 0)]


def vmem():
    return pl.BlockSpec(memory_space=pltpu.VMEM)


def smem():
    return pl.BlockSpec(memory_space=pltpu.SMEM)


def hbm():
    return pl.BlockSpec(memory_space=pltpu.HBM)


def kernel_call(body, grant, **options):
    return pl.pallas_call(body, compiler_params=pltpu.CompilerParams(vmem_limit_bytes=grant), **options)


def near_core(value):
    return pltpu.with_memory_space_constraint(value, pltpu.VMEM)


def scalar_core(value):
    return pltpu.with_memory_space_constraint(value, pltpu.SMEM)


def off_core(value):
    return pltpu.with_memory_space_constraint(value, pltpu.HBM)


def turned(row):
    return jnp.broadcast_to(row, (8, row.shape[1])).T[:, :1]


def open_kernel(history, columns_hbm, lags_hbm, fanned, wanted, held, columns, lags, sems):
    rows, tile = held.shape[1], held.shape[3]
    pairs = [(history.at[:, :, pl.ds(row * tile, tile)], held.at[:, row]) for row in range(rows)]
    into = start_all([*pairs, (columns_hbm, columns), (lags_hbm, lags)], sems)
    for copy in into:
        copy.wait()
    out = start_all([(held, fanned.at[z]) for z in range(Z)], sems, len(into))
    slots = Slots(columns, lags)
    spot = (slots.z * LEVELS + slots.lag) * slots.rows + slots.local
    asks = lax.broadcasted_iota(jnp.int32, (slots.count, wanted.shape[1]), 1)
    total = jnp.zeros(wanted.shape, jnp.int32)
    for row in range(slots.rows):
        mine = jnp.where(turned(slots.at[row]) == asks, turned(spot[row : row + 1]), 0)
        total += jnp.sum(mine, axis=0, keepdims=True)
    wanted[...] = total
    for copy in out:
        copy.wait()


def open_up(history, columns, lags, tile):
    levels, dirs, panels = history.shape
    rows = panels // tile
    return kernel_call(
        open_kernel,
        SMALL,
        out_shape=(
            pltpu.HBM((Z, levels, rows, dirs, tile), history.dtype),
            pltpu.VMEM((1, GROUPS * BLOCK_CAP * Z), jnp.int32),
        ),
        in_specs=[hbm()] * 3,
        out_specs=(hbm(), vmem()),
        scratch_shapes=[
            pltpu.VMEM((levels, rows, dirs, tile), history.dtype),
            pltpu.VMEM(columns.shape, columns.dtype),
            pltpu.VMEM(lags.shape, lags.dtype),
            pltpu.SemaphoreType.DMA((rows + 2 + Z,)),
        ],
    )(off_core(history), off_core(columns), off_core(lags))


class Slots:
    def __init__(self, columns, lags):
        self.rows, self.count = columns.shape
        col, self.lag = columns[...], lags[...] - 1
        owner = (col * ((1 << 17) // self.rows + 1)) >> 17
        self.local = col - owner * self.rows
        self.c = lax.rem(owner, C)
        self.z = lax.rem(owner // C, Z)
        self.y = owner // (C * Z)
        group = self.y * C + self.c
        self.here = lax.broadcasted_iota(jnp.int32, (self.count, self.count), 1)
        self.there = lax.broadcasted_iota(jnp.int32, (self.count, self.count), 0)
        groups = [group[row : row + 1] for row in range(self.rows)]
        down = [turned(value) for value in groups]
        self.position = []
        for row in range(self.rows):
            same = (down[row] == groups[row]) & (self.there < self.here)
            position = jnp.sum(same.astype(jnp.int32), axis=0, keepdims=True)
            for before in range(row):
                position += jnp.sum((down[before] == groups[row]).astype(jnp.int32), axis=0, keepdims=True)
            self.position.append(position)
        self.at = [groups[row] * (BLOCK_CAP * Z) + self.position[row] for row in range(self.rows)]


def chart_kernel(counts, columns, lags, spots_out, aged_out, table_out, spots, aged, table, sems):
    slots = Slots(columns, lags)
    cap = BLOCK_CAP * Z
    y, c = lax.axis_index("y"), lax.axis_index("c")
    other = (slots.c != c).astype(jnp.int32)
    across = (lax.rem(slots.y - y + Y, Y) * C + other) * cap
    fresh = (other * (Y * Z) + slots.y * Z + slots.z) * slots.rows + slots.local
    lane = lax.broadcasted_iota(jnp.int32, (1, slots.count), 1)
    spot_parts, aged_parts, order_parts, where_parts, new_parts = [], [], [], [], []
    for row in range(slots.rows):
        live = lane < counts[row]
        new = live & (slots.lag[row : row + 1] == 0)
        spot_parts.append(jnp.where(live, slots.at[row], -1))
        aged_parts.append(jnp.where(live & ~new, across[row : row + 1] + slots.position[row], -1))
        fresh_row = jnp.where(new, fresh[row : row + 1], -1)
        marked = turned(new.astype(jnp.int32)) == 1
        rank = jnp.sum((marked & (slots.there < slots.here)).astype(jnp.int32), axis=0, keepdims=True)
        put = marked & (turned(rank) == slots.here)
        order_parts.append(jnp.sum(jnp.where(put, slots.there, 0), axis=0, keepdims=True))
        where_parts.append(jnp.sum(jnp.where(put, turned(fresh_row) + 1, 0), axis=0, keepdims=True) - 1)
        new_count = jnp.sum(new.astype(jnp.int32), axis=1, keepdims=True)
        new_parts.append(jnp.broadcast_to(new_count, (1, slots.count)))
    rest = jnp.zeros((1, spots.shape[1] - slots.rows * slots.count), jnp.int32)
    tail = rest
    for row in range(slots.rows):
        tail = jnp.where(lax.broadcasted_iota(jnp.int32, rest.shape, 1) == row, counts[row], tail)
    spots[...] = jnp.concatenate([*spot_parts, tail], axis=1)
    aged[...] = jnp.concatenate([*aged_parts, tail], axis=1)
    table[0:1, :] = jnp.concatenate([*order_parts, rest], axis=1)
    table[1:2, :] = jnp.concatenate([*where_parts, rest], axis=1)
    table[2:3, :] = jnp.concatenate([*new_parts, rest], axis=1)
    for copy in start_all([(spots, spots_out), (aged, aged_out), (table, table_out)], sems):
        copy.wait()


def chart(counts, columns, lags):
    lengths = (1, 1, 3)
    return kernel_call(
        chart_kernel,
        SMALL,
        out_shape=tuple(pltpu.SMEM((length, 128), jnp.int32) for length in lengths),
        in_specs=[smem(), vmem(), vmem()],
        out_specs=[smem()] * 3,
        scratch_shapes=[pltpu.VMEM((length, 128), jnp.int32) for length in lengths]
        + [pltpu.SemaphoreType.DMA((3,))],
    )(off_core(counts), off_core(columns), off_core(lags))


def gather_lists_kernel(*refs):
    for copy in start_all(list(zip(refs[:Y], refs[Y : 2 * Y])), refs[2 * Y]):
        copy.wait()


def gather_lists(lists):
    return kernel_call(
        gather_lists_kernel,
        SMALL,
        out_shape=tuple(pltpu.SMEM(value.shape, value.dtype) for value in lists),
        in_specs=[vmem()] * Y,
        out_specs=[smem()] * Y,
        scratch_shapes=[pltpu.SemaphoreType.DMA((Y,))],
    )(*[near_core(value) for value in lists])


def whose(shift, other):
    y, c = lax.axis_index("y"), lax.axis_index("c")
    return lax.rem(y - shift + Y, Y) * C + (c if other == 0 else 1 - c)


def pick_kernel(*refs):
    lists, held, first, kept, sems = refs[:Y], refs[Y], refs[Y + 1], refs[Y + 2], refs[Y + 3]
    cap = first.shape[0] // GROUPS
    mine = (lax.axis_index("y") * C + lax.axis_index("c")) * cap
    copies = []
    for shift in range(Y):
        for other in range(C):
            base = len(copies) * cap

            @pl.loop(0, cap, step=16)
            def _(entry):
                for k in range(16):
                    spot = lists[shift][0, other * GROUPS * cap + mine + entry + k]
                    kept[base + entry + k] = held[spot]

            to = whose(shift, other) * cap
            pair = (kept.at[pl.ds(base, cap)], first.at[pl.ds(to, cap)])
            copies += start_all([pair], sems, len(copies))
    for copy in copies:
        copy.wait()


def pick_later_kernel(*refs):
    lists, held, later, kept, sems = refs[:Y], refs[Y], refs[Y + 1 : 2 * Y + 1], refs[2 * Y + 1], refs[2 * Y + 2]
    cap = later[0].shape[0] // C
    back = held.shape[0] // (Z * LEVELS)
    mine = (lax.axis_index("y") * C + lax.axis_index("c")) * cap
    copies = []
    for shift in range(Y):
        for other in range(C):

            @pl.loop(0, cap, step=16)
            def _(entry):
                for k in range(16):
                    spot = lists[shift][0, other * GROUPS * cap + mine + entry + k]
                    kept[shift, other * cap + entry + k] = held[jnp.maximum(spot - back, 0)]

        copies += start_all([(kept.at[shift], later[shift])], sems, shift)
    for copy in copies:
        copy.wait()


def picks(lists, held, cap):
    def out(entries):
        return pltpu.HBM((entries, *held.shape[1:]), held.dtype)

    held = near_core(held)
    lists = [scalar_core(value) for value in lists]
    specs = [smem()] * Y + [vmem()]
    first = kernel_call(
        pick_kernel,
        SMALL,
        out_shape=out(GROUPS * cap),
        in_specs=specs,
        out_specs=hbm(),
        scratch_shapes=[
            pltpu.VMEM((GROUPS * cap, *held.shape[1:]), held.dtype),
            pltpu.SemaphoreType.DMA((GROUPS,)),
        ],
    )(*lists, held)
    later = kernel_call(
        pick_later_kernel,
        SMALL,
        out_shape=[out(C * cap)] * Y,
        in_specs=specs,
        out_specs=[hbm()] * Y,
        scratch_shapes=[
            pltpu.VMEM((Y, C * cap, *held.shape[1:]), held.dtype),
            pltpu.SemaphoreType.DMA((Y,)),
        ],
    )(*lists, held)
    return first, later


def pieces_of(spot_at, count, load):
    parts = []
    for k in range(count):
        spot = spot_at(k)
        value = load(jnp.maximum(spot, 0))
        parts.append(jnp.where(spot >= 0, value, jnp.zeros_like(value)))
    return jnp.concatenate(parts, axis=1)


def row_sum(spots, load, weights, base):
    slots, tile = weights.shape[0], weights.shape[1]
    picked = pieces_of(lambda k: spots[0, base + k], slots, load)
    return jnp.dot(picked, weights[...].reshape(slots * tile, tile), preferred_element_type=jnp.float32)


def density_of(own, total, zinv):
    source = (own.astype(jnp.float32) - total).astype(jnp.bfloat16)
    return jnp.dot(source, zinv, preferred_element_type=jnp.float32).astype(jnp.bfloat16)


def start_all(pairs, sems, base=0):
    copies = [pltpu.make_async_copy(src, dst, sems.at[base + i]) for i, (src, dst) in enumerate(pairs)]
    for copy in copies:
        copy.start()
    return copies


def live_tiles(count, source, target, sems, row, act):
    slots = target.shape[0]
    for chunk in range(slots // CHUNK):
        part = pl.ds(chunk * CHUNK, CHUNK)

        @pl.when(chunk * CHUNK < count)
        def _():
            copy = pltpu.make_async_copy(source.at[part], target.at[part], sems.at[row, chunk])
            if act == "start":
                copy.start()
            else:
                copy.wait()

        if act == "start":

            @pl.when(chunk * CHUNK >= count)
            def _():
                target[part] = jnp.zeros((CHUNK, *target.shape[1:]), target.dtype)


def stage_kernel(ztiles_hbm, zinv_hbm, incident_hbm, top, zinv, incident, sems):
    slots = ztiles_hbm.shape[1]
    pairs = []
    for row in range(ztiles_hbm.shape[0]):
        length = min(slots, top.shape[0] - row * slots)
        if length > 0:
            pairs.append((ztiles_hbm.at[row, pl.ds(0, length)], top.at[pl.ds(row * slots, length)]))
    for copy in start_all([*pairs, (zinv_hbm, zinv), (incident_hbm.at[0], incident)], sems):
        copy.wait()


def stage(ztiles, zinv, incident):
    rows, slots, tile = ztiles.shape[0], ztiles.shape[1], ztiles.shape[2]
    return kernel_call(
        stage_kernel,
        SMALL,
        out_shape=(
            pltpu.VMEM((rows * slots - FETCHED, tile, tile), ztiles.dtype),
            pltpu.VMEM(zinv.shape, zinv.dtype),
            pltpu.VMEM(incident.shape[1:], incident.dtype),
        ),
        in_specs=[hbm()] * 3,
        out_specs=[vmem()] * 3,
        scratch_shapes=[pltpu.SemaphoreType.DMA((rows + 2,))],
    )(off_core(ztiles), off_core(zinv), off_core(incident))


def first_kernel(spots, got, top, ztiles_hbm, zinv, incident, spread_out, last, kept_out, sems, tile_sems):
    rows, slots, tile = ztiles_hbm.shape[0], ztiles_hbm.shape[1], ztiles_hbm.shape[2]
    begin = slots - last.shape[0]
    rest = ztiles_hbm.at[rows - 1, pl.ds(begin, last.shape[0])]
    count = spots[0, rows * slots + rows - 1] - begin
    live_tiles(count, rest, last, tile_sems, 0, "start")
    copies = []
    for row in range(rows):
        length = slots if row < rows - 1 else begin
        weights = top.at[pl.ds(row * slots, length)]
        total = row_sum(spots, lambda spot: got[spot], weights, row * slots)
        if row == rows - 1:
            live_tiles(count, rest, last, tile_sems, 0, "wait")
            total += row_sum(spots, lambda spot: got[spot], last, row * slots + begin)
        density = density_of(incident[:, row * tile : (row + 1) * tile], total, zinv[row])
        for to in range(spread_out.shape[0]):
            kept_out[row, to] = density
        copies += start_all([(kept_out.at[row], spread_out.at[:, row])], sems, row)
    for copy in copies:
        copy.wait()


def first_step(spots, got, top, ztiles, zinv, incident):
    rows, tile, dirs = ztiles.shape[0], ztiles.shape[2], got.shape[1]
    return kernel_call(
        first_kernel,
        SMALL,
        out_shape=pltpu.HBM((Y * Z, rows, dirs, tile), jnp.bfloat16),
        in_specs=[smem(), vmem(), vmem(), hbm(), vmem(), vmem()],
        out_specs=hbm(),
        scratch_shapes=[
            pltpu.VMEM((FETCHED, tile, tile), ztiles.dtype),
            pltpu.VMEM((rows, Y * Z, dirs, tile), jnp.bfloat16),
            pltpu.SemaphoreType.DMA((rows,)),
            pltpu.SemaphoreType.DMA((1, FETCHED // CHUNK)),
        ],
    )(scalar_core(spots), near_core(got), near_core(top), off_core(ztiles), near_core(zinv), near_core(incident))


def aged_kernel(spots, table, *refs):
    near, cross = refs[:Y], refs[Y : 2 * Y]
    fanned, incident_hbm, ztiles_hbm, basis_hbm, packed, fresh, basis = refs[2 * Y : 2 * Y + 7]
    pool, ztiles, before, incident, sems, tile_sems = refs[2 * Y + 7 :]
    rows, slots, tile = ztiles.shape[0], ztiles.shape[1], ztiles.shape[2]
    cap = near[0].shape[0] // C
    panels = rows * tile
    counts = [spots[0, rows * slots + row] for row in range(rows)]
    for row in range(rows):
        live_tiles(counts[row], ztiles_hbm.at[row], ztiles.at[row], tile_sems, row, "start")
    own = [
        (source.at[pl.ds(other * cap, cap)], pool.at[pl.ds(other * cap, cap)])
        for other, source in enumerate((near[0], cross[0]))
    ]
    own = start_all(own, sems)
    copies = start_all([(incident_hbm.at[1], incident), (fanned.at[0], before), (basis_hbm, basis)], sems, C)
    for shift in range(1, Y):
        for other, source in enumerate((near[shift], cross[shift])):
            pool[pl.ds((shift * C + other) * cap, cap)] = source[pl.ds(other * cap, cap)]
    for copy in own:
        copy.wait()
    for row in range(rows):
        live_tiles(counts[row], ztiles_hbm.at[row], ztiles.at[row], tile_sems, row, "wait")
        for k in range(CHUNK):
            fresh[row, k] = ztiles[row, table[0, row * slots + k]]
        at = slice(row * tile, (row + 1) * tile)
        packed[1, :, at] = row_sum(spots, lambda spot: pool[spot], ztiles.at[row], row * slots)
    for copy in copies:
        copy.wait()
    packed[0, :, :] = incident[...].astype(jnp.float32)
    value = jnp.concatenate([before[row] for row in range(rows)], axis=1)
    packed[2, :, :] = value.astype(jnp.float32)
    packed[3, :, : basis.shape[1]] = jnp.dot(value, basis[...], preferred_element_type=jnp.float32)
    packed[3, :, basis.shape[1] :] = jnp.zeros((value.shape[0], panels - basis.shape[1]), jnp.float32)


def aged_step(spots, table, fanned, incident, near, cross, ztiles, basis):
    rows, dirs, tile = fanned.shape[1:]
    cap = near[0].shape[0] // C
    return kernel_call(
        aged_kernel,
        SMALL,
        out_shape=(
            pltpu.VMEM((4, dirs, rows * tile), jnp.float32),
            pltpu.VMEM((rows, CHUNK, tile, tile), ztiles.dtype),
            pltpu.VMEM(basis.shape, basis.dtype),
        ),
        in_specs=[smem(), smem()] + ([hbm()] + [vmem()] * (Y - 1)) * 2 + [hbm()] * 4,
        out_specs=[vmem()] * 3,
        scratch_shapes=[
            pltpu.VMEM((2 * Y * cap, dirs, tile), jnp.bfloat16),
            pltpu.VMEM(ztiles.shape, ztiles.dtype),
            pltpu.VMEM(fanned.shape[1:], fanned.dtype),
            pltpu.VMEM(incident.shape[1:], incident.dtype),
            pltpu.SemaphoreType.DMA((C + 3,)),
            pltpu.SemaphoreType.DMA((rows, ztiles.shape[1] // CHUNK)),
        ],
    )(
        scalar_core(spots),
        scalar_core(table),
        off_core(near[0]),
        *[near_core(piece) for piece in near[1:]],
        off_core(cross[0]),
        *[near_core(piece) for piece in cross[1:]],
        off_core(fanned),
        off_core(incident),
        off_core(ztiles),
        off_core(basis),
    )


def second_kernel(table, packed, fresh, zinv, basis, here, there, ztiles_hbm, dens_out, far, ztiles, flipped, dens, sems, tile_sems):
    rows, slots, tile = ztiles_hbm.shape[0], ztiles_hbm.shape[1], ztiles_hbm.shape[2]
    near = here.shape[0]

    def load(spot):
        ours = here[jnp.minimum(spot, near - 1)]
        theirs = there[jnp.maximum(spot - near, 0)]
        return jnp.where(spot < near, ours, theirs)

    later = []
    for row in range(rows):
        chunks = lax.div(table[2, row * slots] + (CHUNK - 1), CHUNK)
        at = pl.ds(row * tile, tile)
        first = pieces_of(lambda k: table[1, row * slots + k], CHUNK, load)
        total = packed[1, :, at] + jnp.dot(
            first, fresh[row].reshape(CHUNK * tile, tile), preferred_element_type=jnp.float32
        )

        def more(chunk, total):
            copies = []
            for k in range(CHUNK):
                source = ztiles_hbm.at[row, table[0, row * slots + chunk * CHUNK + k]]
                copies.append(pltpu.make_async_copy(source, ztiles.at[k], tile_sems.at[k]))
            for copy in copies:
                copy.start()
            for copy in copies:
                copy.wait()
            picked = pieces_of(lambda k: table[1, row * slots + chunk * CHUNK + k], CHUNK, load)
            return total + jnp.dot(
                picked, ztiles[...].reshape(CHUNK * tile, tile), preferred_element_type=jnp.float32
            )

        total = lax.fori_loop(1, chunks, more, total)
        later.append(density_of(packed[0, :, at], total, zinv[row]))
    value = jnp.concatenate(later, axis=1)
    dens[0] = packed[2].astype(dens.dtype)
    dens[1] = value
    copy = start_all([(dens, dens_out)], sems)[0]
    far_second = jnp.dot(value, basis[...], preferred_element_type=jnp.float32)
    both = jnp.concatenate([packed[3, :, : basis.shape[1]], far_second], axis=0)
    lanes = both.shape[0]
    flipped[:, :lanes] = both.T
    owners = far.shape[0]
    each = basis.shape[1] // owners
    cols = [flipped[pl.ds(c, owners, stride=each), :][:, :lanes] for c in range(each)]
    far[...] = jnp.concatenate([*cols, jnp.zeros((owners, far.shape[1] - each * lanes), jnp.float32)], axis=1)
    copy.wait()


def second_step(table, packed, fresh, zinv, basis, here, there, ztiles, owners):
    tile, dirs = here.shape[2], here.shape[1]
    panels, harmonics = basis.shape
    return kernel_call(
        second_kernel,
        SMALL,
        out_shape=(
            pltpu.HBM((STEPS, dirs, panels), jnp.bfloat16),
            pltpu.VMEM((owners, 128), jnp.float32),
        ),
        in_specs=[smem()] + [vmem()] * 6 + [hbm()],
        out_specs=(hbm(), vmem()),
        scratch_shapes=[
            pltpu.VMEM((CHUNK, tile, tile), ztiles.dtype),
            pltpu.VMEM((harmonics, 128), jnp.float32),
            pltpu.VMEM((STEPS, dirs, panels), jnp.bfloat16),
            pltpu.SemaphoreType.DMA((1,)),
            pltpu.SemaphoreType.DMA((CHUNK,)),
        ],
    )(
        scalar_core(table),
        near_core(packed),
        near_core(fresh),
        near_core(zinv),
        near_core(basis),
        near_core(here),
        near_core(there),
        off_core(ztiles),
    )


def sum_kernel(parts, out):
    total = jnp.sum(parts[...], axis=0, keepdims=True)
    steps, each, dirs = out.shape
    for step in range(steps):
        for c in range(each):
            at = (c * steps + step) * dirs
            out[step, c : c + 1, :] = total[:, at : at + dirs]


def sum_parts(parts, steps, each, dirs):
    return kernel_call(
        sum_kernel,
        SMALL,
        out_shape=jax.ShapeDtypeStruct((steps, each, dirs), jnp.float32),
        in_specs=[vmem()],
        out_specs=vmem(),
    )(near_core(parts))


def shifted(value, axis, length, shift):
    return lax.ppermute(value, axis, [(i, (i + shift) % length) for i in range(length)])


def march(history, incident, ztiles, zinv, columns, lags, counts, basis):
    rows, tile = ztiles.shape[0], ztiles.shape[2]
    dirs = history.shape[1]
    owners = Y * Z * C
    cap = BLOCK_CAP * Z
    outgoing, wanted = open_up(history, columns, lags, tile)
    held = lax.all_to_all(outgoing, "z", 0, 0, tiled=True).reshape(-1, dirs, tile)
    spots, aged, table = chart(counts, columns, lags)
    both = jnp.concatenate([wanted, lax.ppermute(wanted, "c", SWAP)], axis=1)
    lists = [both] + [shifted(both, "y", Y, s) for s in range(1, Y)]
    lists = gather_lists(lists)
    first, later = picks(lists, held, cap)
    got = lax.all_to_all(first.reshape(GROUPS, cap, dirs, tile), ("y", "c"), 0, 0, tiled=True)
    near = [later[0]] + [shifted(later[s], "y", Y, -s) for s in range(1, Y)]
    cross = [lax.ppermute(near[0], "c", SWAP)]
    cross += [lax.ppermute(piece, "c", SWAP) for piece in near[1:]]
    top, inverse, driven = stage(ztiles, zinv, incident)
    fanned = first_step(spots, got.reshape(GROUPS * cap, dirs, tile), top, ztiles, inverse, driven)
    here = lax.all_to_all(fanned, ("y", "z"), 0, 0, tiled=True).reshape(Y * Z * rows, dirs, tile)
    packed, lag_one, weights = aged_step(aged, table, fanned, incident, near, cross, ztiles, basis)
    there = lax.ppermute(here, "c", SWAP)
    dens, far = second_step(table, packed, lag_one, inverse, weights, here, there, ztiles, owners)
    each = basis.shape[1] // owners
    parts = lax.all_to_all(far.reshape(owners, 1, 128), E, 0, 0, tiled=True).reshape(owners, 128)
    total = sum_parts(parts, STEPS, each, dirs)
    return dens, total.transpose(0, 2, 1)


def solution(mesh):
    fine = Mesh(mesh.devices.reshape(Y, Z, C, mesh.shape["dir"]), ("y", "z", "c", "dir"))
    in_specs = (
        P(None, "dir", E),
        P(None, "dir", E),
        P(E, None, None, None),
        P(E, None, None),
        P(E, None),
        P(E, None),
        P(E),
        P(E, None),
    )
    out_specs = (P(None, "dir", E), P(None, "dir", E))
    return jax.shard_map(march, mesh=fine, in_specs=in_specs, out_specs=out_specs, check_vma=False)
```
